256 devices in a mesh: tile: 32 (over z_hi, x, core), mem: 8 (over y, z_lo).
Axes of the slice: x: 4, y: 4, z: 8 (z_hi: 4, z_lo: 2; z = z_hi * 2 + z_lo), core: 2. Of those that a mesh axis runs over, the one named last changes fastest.
Arguments:
- members: float32 [32, 32, 512, 256], P('mem', None, 'tile'), may hold values from -6 to 6
- control: float32 [32, 512, 256], P(None, 'tile'), may hold values from -6 to 6
- u_courant: float32 [32, 512, 256], P(None, 'tile'), may hold values from -0.4 to 0.4
- v_courant: float32 [32, 512, 256], P(None, 'tile'), may hold values from -0.4 to 0.4
- diffusion: float32 [31, 512, 256], P(None, 'tile'), may hold values from 0.05 to 5
- group_scale: float32 [4], replicated, may hold values from 0.3 to 3
- group_of: int32 [32], P('mem'), may hold values from 0 to 3
- wet: int32 [512, 256], P('tile'), may hold values 0 or 1
Outputs:
- forecast: float32 [32, 32, 512, 256], P('mem', None, 'tile')
The draws below stay inside these ranges and needn't reach their ends.
All inputs are finite; a program needn't handle non-finite values. No bound on the sum of `wet` on one device may be relied on, other than what follows from the above.
Results may differ from the reference program's by a relative error of at most 0.0003.
Values sent between devices are 32-bit elements; how exact they have to be, the bound alone decides.
A program may use at most 64 MiB of HBM per device.

```python
import math
import jax
import jax.numpy as jnp
from jax import lax

Z = 32
GROUPS = 4
NY = 256
MEMBERS = 32
NX = 512


def with_ends(entries, rng, least, high):
    longest = entries.shape.index(max(entries.shape))
    spots = []
    for shift in (0, 1):
        where = [jax.random.randint(jax.random.fold_in(rng, axis), (), 0, length) for axis, length in enumerate(entries.shape)]
        where[longest] = (where[longest] + shift) % entries.shape[longest]
        spots.append(tuple(where))
    return entries.at[spots[0]].set(least).at[spots[1]].set(high)


def block_scale(stream_key, dims, shards, smallest, high):
    loudness, own = 1.0, jax.random.fold_in(stream_key, 6)
    for position, blocks in shards:
        steps = jnp.exp(jax.random.uniform(jax.random.fold_in(own, position), (blocks,), jnp.float32, smallest / len(shards), high / len(shards)))
        loudness = loudness * jnp.repeat(steps, dims[position] // blocks).reshape([-1 if axis == position else 1 for axis in range(len(dims))])
    return loudness


def scatter_about(stream_key, shape, scale, bound, cuts=(), kind=jnp.bfloat16):
    loudness = block_scale(stream_key, shape, cuts, -0.22, 0.18) if cuts else 1.0
    entries = jax.random.normal(stream_key, shape, jnp.float32) * scale * loudness
    return jnp.minimum(jnp.maximum(entries, -bound), bound).astype(kind)


def setup_inputs(seed: int = 0) -> dict:
    arg_keys = jax.random.split(jax.random.key(seed), 9)
    members = scatter_about(arg_keys[0], (MEMBERS, Z, NX, NY), 1.0, 6.0, ((0, 8), (2, 32)), jnp.float32)
    control = scatter_about(arg_keys[1], (Z, NX, NY), 1.0, 6.0, ((1, 32),), jnp.float32)
    u_courant = jnp.clip(jax.random.uniform(arg_keys[2], (Z, NX, NY), jnp.float32, -0.4, 0.4) * block_scale(arg_keys[2], (Z, NX, NY), ((1, 32),), -0.4, 0.0), -0.4, 0.4)
    v_courant = jnp.clip(jax.random.uniform(arg_keys[3], (Z, NX, NY), jnp.float32, -0.4, 0.4) * block_scale(arg_keys[3], (Z, NX, NY), ((1, 32),), -0.4, 0.0), -0.4, 0.4)
    diffusion = jnp.clip(jnp.exp(math.log(5.0) - 4.6051702 * jax.random.uniform(arg_keys[4], (Z - 1, NX, NY), jnp.float32) ** block_scale(arg_keys[4], (Z - 1, NX, NY), ((1, 32),), -0.2, 0.2)), 0.05, 5.0)
    group_scale = jnp.clip(jnp.exp(jax.random.uniform(arg_keys[5], (GROUPS,), jnp.float32, math.log(0.3), math.log(3.0))), 0.3, 3.0)
    group_of = with_ends(jax.random.randint(arg_keys[6], (MEMBERS,), 0, GROUPS), jax.random.fold_in(arg_keys[6], 1), 0, GROUPS - 1).astype(jnp.int32)
    wet = with_ends((jax.random.randint(arg_keys[7], (NX, NY), 0, 5) < 4).astype(jnp.int32), jax.random.fold_in(arg_keys[7], 1), 0, 1)
    return {"members": members, "control": control, "u_courant": u_courant, "v_courant": v_courant, "diffusion": diffusion, "group_scale": group_scale, "group_of": group_of, "wet": wet}


def minmod(first_diff, second_diff):
    return 0.5 * (jnp.sign(first_diff) + jnp.sign(second_diff)) * jnp.minimum(jnp.abs(first_diff), jnp.abs(second_diff))


def face_flux(courant, far_back, near_back, near_ahead, far_ahead, open_face):
    positive = courant > 0.0
    upwind = jnp.where(positive, near_back, near_ahead)
    side_diff = jnp.where(positive, near_back - far_back, far_ahead - near_ahead)
    limited = minmod(near_ahead - near_back, side_diff)
    magnitude = jnp.abs(courant)
    return (courant * upwind + 0.5 * magnitude * (1.0 - magnitude) * limited) * open_face


def advect(salinity, east_courant, eastern_face_open, north_courant, wet_cells):
    columns = salinity.shape[2]
    east_flux = face_flux(east_courant, salinity[:, :, 0:columns - 3], salinity[:, :, 1:columns - 2], salinity[:, :, 2:columns - 1], salinity[:, :, 3:columns], eastern_face_open)
    interior = salinity[:, :, 2:columns - 2]
    zero_col = jnp.zeros_like(interior[..., :1])
    lower_cells = jnp.concatenate([zero_col, interior[..., :-1]], -1)
    upper_cells = jnp.concatenate([interior[..., 1:], zero_col], -1)
    upper_two = jnp.concatenate([interior[..., 2:], zero_col, zero_col], -1)
    wet_next = jnp.concatenate([wet_cells[:, 1:], jnp.zeros_like(wet_cells[:, :1])], -1)
    poleward_transport = face_flux(north_courant, lower_cells, interior, upper_cells, upper_two, wet_cells * wet_next)
    equatorward_transport = jnp.concatenate([zero_col, poleward_transport[..., :-1]], -1)
    return interior - (east_flux[:, :, 1:] - east_flux[:, :, :-1]) - (poleward_transport - equatorward_transport)


def factor(diff_rates):
    levels = diff_rates.shape[1] + 1
    thomas_coefficients = []
    inverse_terms = []
    previous = None
    for level_index in range(levels):
        diagonal = jnp.ones_like(diff_rates[:, 0])
        if level_index > 0:
            diagonal = diagonal + diff_rates[:, level_index - 1]
        if level_index < levels - 1:
            diagonal = diagonal + diff_rates[:, level_index]
        if level_index > 0:
            diagonal = diagonal + diff_rates[:, level_index - 1] * previous
        inverse_den = 1.0 / diagonal
        inverse_terms.append(inverse_den)
        if level_index < levels - 1:
            previous = -diff_rates[:, level_index] * inverse_den
            thomas_coefficients.append(previous)
    return diff_rates, thomas_coefficients, inverse_terms


def solve_columns(values, tridiag_terms):
    diff_rates, thomas_coefficients, inverse_terms = tridiag_terms
    levels = values.shape[1]
    forward = [values[:, 0] * inverse_terms[0]]
    for level_index in range(1, levels):
        forward.append((values[:, level_index] + diff_rates[:, level_index - 1] * forward[-1]) * inverse_terms[level_index])
    solution = [None] * levels
    solution[levels - 1] = forward[levels - 1]
    for level_index in range(levels - 2, -1, -1):
        solution[level_index] = forward[level_index] - thomas_coefficients[level_index] * solution[level_index + 1]
    return jnp.stack(solution, 1)


def reference(members, control, u_courant, v_courant, diffusion, group_scale, group_of, wet):
    member_mean = jnp.sum(members, 0) / MEMBERS
    adjusted_realisations = members + (control - member_mean)
    wet_float = wet.astype(jnp.float32)
    padded_wet_mask = jnp.pad(wet_float, ((1, 1), (0, 0)))
    eastern_face_open = padded_wet_mask[0:NX + 1] * padded_wet_mask[1:NX + 2]
    east_courant = jnp.pad(u_courant, ((0, 0), (1, 0), (0, 0)))
    spread_multiplier = group_scale[group_of]

    def lone_realisation_prediction(given_arrays):
        salinity, scale_one = given_arrays
        tridiag_terms = factor(scale_one * diffusion[None])
        salinity = salinity[None]
        for time_step_index in range(2):
            padded = jnp.pad(salinity, ((0, 0), (0, 0), (2, 2), (0, 0)))
            salinity = solve_columns(advect(padded, east_courant, eastern_face_open, v_courant, wet_float), tridiag_terms)
        return salinity[0]

    return lax.map(lone_realisation_prediction, (adjusted_realisations, spread_multiplier))
```

```python
import functools

import jax
import jax.numpy as jnp
from jax import lax
from jax.experimental import pallas as pl
from jax.experimental.pallas import tpu as pltpu
from jax.sharding import PartitionSpec as P

MESH_ID = pl.DeviceIdType.MESH


def allreduce_kernel(n, x_ref, o_ref, recv, red, gath, s1, r1, s2, r2):
    me = lax.axis_index("mem")
    tile = lax.axis_index("tile")
    rows = x_ref.shape[0] // n
    peers = [lax.rem(me + d, n) for d in range(1, n)]
    barrier = pltpu.get_barrier_semaphore()
    for peer in peers:
        pl.semaphore_signal(barrier, inc=1, device_id=(tile, peer), device_id_type=MESH_ID)
    pl.semaphore_wait(barrier, n - 1)

    def scatter_copy(peer):
        return pltpu.make_async_remote_copy(
            src_ref=x_ref.at[pl.ds(peer * rows, rows)],
            dst_ref=recv.at[me],
            send_sem=s1.at[peer],
            recv_sem=r1.at[me],
            device_id=(tile, peer),
            device_id_type=MESH_ID,
        )

    def gather_copy(peer):
        return pltpu.make_async_remote_copy(
            src_ref=red,
            dst_ref=gath.at[me],
            send_sem=s2.at[peer],
            recv_sem=r2.at[me],
            device_id=(tile, peer),
            device_id_type=MESH_ID,
        )

    firsts = [scatter_copy(peer) for peer in peers]
    for copy in firsts:
        copy.start()
    for peer in peers:
        pltpu.make_async_remote_copy(
            src_ref=x_ref.at[pl.ds(0, rows)],
            dst_ref=recv.at[peer],
            send_sem=s1.at[peer],
            recv_sem=r1.at[peer],
            device_id=(tile, peer),
            device_id_type=MESH_ID,
        ).wait_recv()
    acc = x_ref[pl.ds(me * rows, rows)]
    for peer in peers:
        acc = acc + recv[peer]
    red[...] = acc
    o_ref[pl.ds(me * rows, rows)] = acc
    seconds = [gather_copy(peer) for peer in peers]
    for copy in seconds:
        copy.start()
    for peer in peers:
        pltpu.make_async_remote_copy(
            src_ref=red,
            dst_ref=gath.at[peer],
            send_sem=s2.at[peer],
            recv_sem=r2.at[peer],
            device_id=(tile, peer),
            device_id_type=MESH_ID,
        ).wait_recv()
        o_ref[pl.ds(peer * rows, rows)] = gath[peer]
    for copy in firsts + seconds:
        copy.wait_send()


def member_allreduce(total):
    n = lax.axis_size("mem")
    rows = total.shape[0] // n
    chunk = (rows,) + total.shape[1:]
    return pl.pallas_call(
        functools.partial(allreduce_kernel, n),
        out_shape=jax.ShapeDtypeStruct(total.shape, total.dtype),
        in_specs=[pl.BlockSpec(memory_space=pltpu.VMEM)],
        out_specs=pl.BlockSpec(memory_space=pltpu.VMEM),
        scratch_shapes=[
            pltpu.VMEM((n,) + chunk, total.dtype),
            pltpu.VMEM(chunk, total.dtype),
            pltpu.VMEM((n,) + chunk, total.dtype),
            pltpu.SemaphoreType.DMA((n,)),
            pltpu.SemaphoreType.DMA((n,)),
            pltpu.SemaphoreType.DMA((n,)),
            pltpu.SemaphoreType.DMA((n,)),
        ],
        compiler_params=pltpu.CompilerParams(collective_id=0, has_side_effects=True),
    )(total)


def with_halo(block, sides, width):
    for axis, dim in sides:
        count = lax.axis_size(axis)
        forward = [(i, i + 1) for i in range(count - 1)]
        backward = [(target, source) for source, target in forward]
        low = lax.ppermute(
            lax.slice_in_dim(block, block.shape[dim] - width, None, axis=dim), axis, forward
        )
        high = lax.ppermute(lax.slice_in_dim(block, 0, width, axis=dim), axis, backward)
        block = jnp.concatenate([low, block, high], axis=dim)
    return block


def minmod(first_diff, second_diff):
    return (
        0.5
        * (jnp.sign(first_diff) + jnp.sign(second_diff))
        * jnp.minimum(jnp.abs(first_diff), jnp.abs(second_diff))
    )


def face_flux(courant, far_back, near_back, near_ahead, far_ahead, open_face):
    positive = courant > 0.0
    upwind = jnp.where(positive, near_back, near_ahead)
    side_diff = jnp.where(positive, near_back - far_back, far_ahead - near_ahead)
    limited = minmod(near_ahead - near_back, side_diff)
    magnitude = jnp.abs(courant)
    return (courant * upwind + 0.5 * magnitude * (1.0 - magnitude) * limited) * open_face


def advect(salinity, east_courant, eastern_face_open, north_courant, wet_cells):
    columns = salinity.shape[2]
    east_flux = face_flux(
        east_courant,
        salinity[:, :, 0 : columns - 3],
        salinity[:, :, 1 : columns - 2],
        salinity[:, :, 2 : columns - 1],
        salinity[:, :, 3:columns],
        eastern_face_open,
    )
    interior = salinity[:, :, 2 : columns - 2]
    zero_col = jnp.zeros_like(interior[..., :1])
    lower_cells = jnp.concatenate([zero_col, interior[..., :-1]], -1)
    upper_cells = jnp.concatenate([interior[..., 1:], zero_col], -1)
    upper_two = jnp.concatenate([interior[..., 2:], zero_col, zero_col], -1)
    wet_next = jnp.concatenate([wet_cells[:, 1:], jnp.zeros_like(wet_cells[:, :1])], -1)
    poleward_transport = face_flux(
        north_courant, lower_cells, interior, upper_cells, upper_two, wet_cells * wet_next
    )
    equatorward_transport = jnp.concatenate([zero_col, poleward_transport[..., :-1]], -1)
    return (
        interior
        - (east_flux[:, :, 1:] - east_flux[:, :, :-1])
        - (poleward_transport - equatorward_transport)
    )


def factor(diff_rates):
    levels = diff_rates.shape[1] + 1
    thomas_coefficients = []
    inverse_terms = []
    previous = None
    for level_index in range(levels):
        diagonal = jnp.ones_like(diff_rates[:, 0])
        if level_index > 0:
            diagonal = diagonal + diff_rates[:, level_index - 1]
        if level_index < levels - 1:
            diagonal = diagonal + diff_rates[:, level_index]
        if level_index > 0:
            diagonal = diagonal + diff_rates[:, level_index - 1] * previous
        inverse_den = 1.0 / diagonal
        inverse_terms.append(inverse_den)
        if level_index < levels - 1:
            previous = -diff_rates[:, level_index] * inverse_den
            thomas_coefficients.append(previous)
    return (diff_rates, thomas_coefficients, inverse_terms)


def solve_columns(values, tridiag_terms):
    diff_rates, thomas_coefficients, inverse_terms = tridiag_terms
    levels = values.shape[1]
    forward = [values[:, 0] * inverse_terms[0]]
    for level_index in range(1, levels):
        forward.append(
            (values[:, level_index] + diff_rates[:, level_index - 1] * forward[-1])
            * inverse_terms[level_index]
        )
    solution = [None] * levels
    solution[levels - 1] = forward[levels - 1]
    for level_index in range(levels - 2, -1, -1):
        solution[level_index] = (
            forward[level_index] - thomas_coefficients[level_index] * solution[level_index + 1]
        )
    return jnp.stack(solution, 1)


def per_device(members, control, u_courant, v_courant, diffusion, group_scale, group_of, wet):
    levels = members.shape[1]
    columns = members.shape[2]
    realisation_total = members.shape[0] * lax.axis_size("mem")
    group_ids = jnp.arange(group_scale.shape[0], dtype=jnp.int32)
    spread_multiplier = jnp.sum(
        jnp.where(group_of[:, None] == group_ids[None, :], group_scale[None, :], 0.0), 1
    )
    wet_float = wet.astype(jnp.float32)
    local_total = jnp.sum(members, 0)
    member_total = member_allreduce(local_total)
    recentre_shift = control - member_total / realisation_total
    salinity = members + recentre_shift[None]
    extended = with_halo(jnp.concatenate([u_courant, wet_float[None]], 0), (("tile", 1),), 1)
    east_courant = extended[:levels, 0 : columns + 1]
    wet_ext = extended[levels]
    eastern_face_open = wet_ext[0 : columns + 1] * wet_ext[1 : columns + 2]
    tridiag_terms = factor(spread_multiplier[:, None, None, None] * diffusion[None])
    for time_step_index in range(2):
        padded = with_halo(salinity, (("tile", 2),), 2)
        salinity = solve_columns(
            advect(padded, east_courant, eastern_face_open, v_courant, wet_float), tridiag_terms
        )
    return salinity


def solution(mesh):
    placed = (
        P("mem", None, "tile", None),
        P(None, "tile", None),
        P(None, "tile", None),
        P(None, "tile", None),
        P(None, "tile", None),
        P(),
        P("mem"),
        P("tile", None),
    )
    return jax.shard_map(
        per_device,
        mesh=mesh,
        in_specs=placed,
        out_specs=P("mem", None, "tile", None),
        check_vma=False,
    )
```

```python
import functools

import jax
import jax.numpy as jnp
from jax import lax
from jax.experimental import pallas as pl
from jax.experimental.pallas import tpu as pltpu
from jax.sharding import PartitionSpec as P

MESH_ID = pl.DeviceIdType.MESH


def allreduce_kernel(n, x_ref, o_ref, recv, red, gath, s1, r1, s2, r2):
    me = lax.axis_index("mem")
    tile = lax.axis_index("tile")
    rows = x_ref.shape[0] // n
    peers = [lax.rem(me + d, n) for d in range(1, n)]
    barrier = pltpu.get_barrier_semaphore()
    for peer in peers:
        pl.semaphore_signal(barrier, inc=1, device_id=(tile, peer), device_id_type=MESH_ID)
    pl.semaphore_wait(barrier, n - 1)

    def scatter_copy(peer):
        return pltpu.make_async_remote_copy(
            src_ref=x_ref.at[pl.ds(peer * rows, rows)],
            dst_ref=recv.at[me],
            send_sem=s1.at[peer],
            recv_sem=r1.at[me],
            device_id=(tile, peer),
            device_id_type=MESH_ID,
        )

    def gather_copy(peer):
        return pltpu.make_async_remote_copy(
            src_ref=red,
            dst_ref=gath.at[me],
            send_sem=s2.at[peer],
            recv_sem=r2.at[me],
            device_id=(tile, peer),
            device_id_type=MESH_ID,
        )

    firsts = [scatter_copy(peer) for peer in peers]
    for copy in firsts:
        copy.start()
    for peer in peers:
        pltpu.make_async_remote_copy(
            src_ref=x_ref.at[pl.ds(0, rows)],
            dst_ref=recv.at[peer],
            send_sem=s1.at[peer],
            recv_sem=r1.at[peer],
            device_id=(tile, peer),
            device_id_type=MESH_ID,
        ).wait_recv()
    acc = x_ref[pl.ds(me * rows, rows)]
    for peer in peers:
        acc = acc + recv[peer]
    red[...] = acc
    o_ref[pl.ds(me * rows, rows)] = acc
    seconds = [gather_copy(peer) for peer in peers]
    for copy in seconds:
        copy.start()
    for peer in peers:
        pltpu.make_async_remote_copy(
            src_ref=red,
            dst_ref=gath.at[peer],
            send_sem=s2.at[peer],
            recv_sem=r2.at[peer],
            device_id=(tile, peer),
            device_id_type=MESH_ID,
        ).wait_recv()
        o_ref[pl.ds(peer * rows, rows)] = gath[peer]
    for copy in firsts + seconds:
        copy.wait_send()


def member_allreduce(total):
    n = lax.axis_size("mem")
    rows = total.shape[0] // n
    chunk = (rows,) + total.shape[1:]
    return pl.pallas_call(
        functools.partial(allreduce_kernel, n),
        out_shape=jax.ShapeDtypeStruct(total.shape, total.dtype),
        in_specs=[pl.BlockSpec(memory_space=pltpu.VMEM)],
        out_specs=pl.BlockSpec(memory_space=pltpu.VMEM),
        scratch_shapes=[
            pltpu.VMEM((n,) + chunk, total.dtype),
            pltpu.VMEM(chunk, total.dtype),
            pltpu.VMEM((n,) + chunk, total.dtype),
            pltpu.SemaphoreType.DMA((n,)),
            pltpu.SemaphoreType.DMA((n,)),
            pltpu.SemaphoreType.DMA((n,)),
            pltpu.SemaphoreType.DMA((n,)),
        ],
        compiler_params=pltpu.CompilerParams(collective_id=0, has_side_effects=True),
    )(total)


def with_halo(block, sides, width):
    for axis, dim in sides:
        count = lax.axis_size(axis)
        forward = [(i, i + 1) for i in range(count - 1)]
        backward = [(target, source) for source, target in forward]
        low = lax.ppermute(
            lax.slice_in_dim(block, block.shape[dim] - width, None, axis=dim), axis, forward
        )
        high = lax.ppermute(lax.slice_in_dim(block, 0, width, axis=dim), axis, backward)
        block = jnp.concatenate([low, block, high], axis=dim)
    return block


def minmod(first_diff, second_diff):
    return (
        0.5
        * (jnp.sign(first_diff) + jnp.sign(second_diff))
        * jnp.minimum(jnp.abs(first_diff), jnp.abs(second_diff))
    )


def face_flux(courant, far_back, near_back, near_ahead, far_ahead, open_face):
    positive = courant > 0.0
    upwind = jnp.where(positive, near_back, near_ahead)
    side_diff = jnp.where(positive, near_back - far_back, far_ahead - near_ahead)
    limited = minmod(near_ahead - near_back, side_diff)
    magnitude = jnp.abs(courant)
    return (courant * upwind + 0.5 * magnitude * (1.0 - magnitude) * limited) * open_face


def advect(salinity, east_courant, eastern_face_open, north_courant, wet_cells):
    columns = salinity.shape[2]
    east_flux = face_flux(
        east_courant,
        salinity[:, :, 0 : columns - 3],
        salinity[:, :, 1 : columns - 2],
        salinity[:, :, 2 : columns - 1],
        salinity[:, :, 3:columns],
        eastern_face_open,
    )
    interior = salinity[:, :, 2 : columns - 2]
    zero_col = jnp.zeros_like(interior[..., :1])
    lower_cells = jnp.concatenate([zero_col, interior[..., :-1]], -1)
    upper_cells = jnp.concatenate([interior[..., 1:], zero_col], -1)
    upper_two = jnp.concatenate([interior[..., 2:], zero_col, zero_col], -1)
    wet_next = jnp.concatenate([wet_cells[:, 1:], jnp.zeros_like(wet_cells[:, :1])], -1)
    poleward_transport = face_flux(
        north_courant, lower_cells, interior, upper_cells, upper_two, wet_cells * wet_next
    )
    equatorward_transport = jnp.concatenate([zero_col, poleward_transport[..., :-1]], -1)
    return (
        interior
        - (east_flux[:, :, 1:] - east_flux[:, :, :-1])
        - (poleward_transport - equatorward_transport)
    )


def factor(diff_rates):
    levels = diff_rates.shape[1] + 1
    thomas_coefficients = []
    inverse_terms = []
    previous = None
    for level_index in range(levels):
        diagonal = jnp.ones_like(diff_rates[:, 0])
        if level_index > 0:
            diagonal = diagonal + diff_rates[:, level_index - 1]
        if level_index < levels - 1:
            diagonal = diagonal + diff_rates[:, level_index]
        if level_index > 0:
            diagonal = diagonal + diff_rates[:, level_index - 1] * previous
        inverse_den = 1.0 / diagonal
        inverse_terms.append(inverse_den)
        if level_index < levels - 1:
            previous = -diff_rates[:, level_index] * inverse_den
            thomas_coefficients.append(previous)
    return (diff_rates, thomas_coefficients, inverse_terms)


def solve_columns(values, tridiag_terms):
    diff_rates, thomas_coefficients, inverse_terms = tridiag_terms
    levels = values.shape[1]
    forward = [values[:, 0] * inverse_terms[0]]
    for level_index in range(1, levels):
        forward.append(
            (values[:, level_index] + diff_rates[:, level_index - 1] * forward[-1])
            * inverse_terms[level_index]
        )
    solution = [None] * levels
    solution[levels - 1] = forward[levels - 1]
    for level_index in range(levels - 2, -1, -1):
        solution[level_index] = (
            forward[level_index] - thomas_coefficients[level_index] * solution[level_index + 1]
        )
    return jnp.stack(solution, 1)


def kernel_flux(courant, far_back, near_back, near_ahead, far_ahead, open_face):
    positive = courant > 0.0
    upwind = jnp.where(positive, near_back, near_ahead)
    side_diff = jnp.where(positive, near_back - far_back, far_ahead - near_ahead)
    first_diff = near_ahead - near_back
    limited = jnp.maximum(jnp.minimum(first_diff, side_diff), 0.0) + jnp.minimum(
        jnp.maximum(first_diff, side_diff), 0.0
    )
    magnitude = jnp.abs(courant)
    return (courant * upwind + 0.5 * magnitude * (1.0 - magnitude) * limited) * open_face


def step_kernel(
    scale_ref, s_ref, ec_ref, fo_ref, v_ref, wn_ref, d_ref, o_ref, east_sc, fwd_sc, coef_sc
):
    member = pl.program_id(0)
    scale = scale_ref[member]
    levels = s_ref.shape[1]
    rows = o_ref.shape[2]
    lanes = o_ref.shape[3]
    lane = lax.broadcasted_iota(jnp.int32, (rows, lanes), 1)
    first_lane = lane == 0
    last_lane = lane == lanes - 1
    last_two = lane >= lanes - 2
    face_open = fo_ref[...]
    north_open = wn_ref[...]

    def forward(k, carry):
        fwd_prev, rate_prev, coef_prev = carry
        east_sc[...] = kernel_flux(
            ec_ref[k],
            s_ref[0, k, pl.ds(0, rows + 1), :],
            s_ref[0, k, pl.ds(1, rows + 1), :],
            s_ref[0, k, pl.ds(2, rows + 1), :],
            s_ref[0, k, pl.ds(3, rows + 1), :],
            face_open,
        )
        interior = s_ref[0, k, pl.ds(2, rows), :]
        lower = jnp.where(first_lane, 0.0, pltpu.roll(interior, 1, 1))
        upper = jnp.where(last_lane, 0.0, pltpu.roll(interior, lanes - 1, 1))
        upper_two = jnp.where(last_two, 0.0, pltpu.roll(interior, lanes - 2, 1))
        north = kernel_flux(v_ref[k], lower, interior, upper, upper_two, north_open)
        south = jnp.where(first_lane, 0.0, pltpu.roll(north, 1, 1))
        advected = (
            interior
            - (east_sc[pl.ds(1, rows), :] - east_sc[pl.ds(0, rows), :])
            - (north - south)
        )
        rate = jnp.where(k < levels - 1, scale * d_ref[jnp.minimum(k, levels - 2)], 0.0)
        diagonal = 1.0 + rate_prev + rate + rate_prev * coef_prev
        inverse = 1.0 / diagonal
        coef = -rate * inverse
        fwd = (advected + rate_prev * fwd_prev) * inverse
        fwd_sc[k] = fwd
        coef_sc[k] = coef
        return fwd, rate, coef

    zero = jnp.zeros((rows, lanes), jnp.float32)
    last, _, _ = lax.fori_loop(0, levels, forward, (zero, zero, zero))
    o_ref[0, levels - 1] = last

    def backward(j, below):
        k = levels - 2 - j
        value = fwd_sc[k] - coef_sc[k] * below
        o_ref[0, k] = value
        return value

    lax.fori_loop(0, levels - 1, backward, last)


def advect_and_solve(scale, padded, east_courant, face_open, v_courant, north_open, diffusion):
    members, levels, rows = padded.shape[0], padded.shape[1], padded.shape[2] - 4
    lanes = padded.shape[3]
    whole = lambda shape: pl.BlockSpec(shape, lambda m: (0,) * len(shape))
    return pl.pallas_call(
        step_kernel,
        grid=(members,),
        out_shape=jax.ShapeDtypeStruct((members, levels, rows, lanes), jnp.float32),
        in_specs=[
            pl.BlockSpec(memory_space=pltpu.SMEM),
            pl.BlockSpec((1,) + padded.shape[1:], lambda m: (m, 0, 0, 0)),
            whole(east_courant.shape),
            whole(face_open.shape),
            whole(v_courant.shape),
            whole(north_open.shape),
            whole(diffusion.shape),
        ],
        out_specs=pl.BlockSpec((1, levels, rows, lanes), lambda m: (m, 0, 0, 0)),
        scratch_shapes=[
            pltpu.VMEM((rows + 1, lanes), jnp.float32),
            pltpu.VMEM((levels, rows, lanes), jnp.float32),
            pltpu.VMEM((levels, rows, lanes), jnp.float32),
        ],
    )(scale, padded, east_courant, face_open, v_courant, north_open, diffusion)


def per_device(members, control, u_courant, v_courant, diffusion, group_scale, group_of, wet):
    levels = members.shape[1]
    columns = members.shape[2]
    realisation_total = members.shape[0] * lax.axis_size("mem")
    group_ids = jnp.arange(group_scale.shape[0], dtype=jnp.int32)
    spread_multiplier = jnp.sum(
        jnp.where(group_of[:, None] == group_ids[None, :], group_scale[None, :], 0.0), 1
    )
    wet_float = wet.astype(jnp.float32)
    local_total = jnp.sum(members, 0)
    member_total = member_allreduce(local_total)
    recentre_shift = control - member_total / realisation_total
    salinity = members + recentre_shift[None]
    extended = with_halo(jnp.concatenate([u_courant, wet_float[None]], 0), (("tile", 1),), 1)
    east_courant = extended[:levels, 0 : columns + 1]
    wet_ext = extended[levels]
    eastern_face_open = wet_ext[0 : columns + 1] * wet_ext[1 : columns + 2]
    wet_next = jnp.concatenate([wet_float[:, 1:], jnp.zeros_like(wet_float[:, :1])], -1)
    north_open = wet_float * wet_next
    for time_step_index in range(2):
        padded = with_halo(salinity, (("tile", 2),), 2)
        salinity = advect_and_solve(
            spread_multiplier, padded, east_courant, eastern_face_open, v_courant, north_open,
            diffusion,
        )
    return salinity


def solution(mesh):
    placed = (
        P("mem", None, "tile", None),
        P(None, "tile", None),
        P(None, "tile", None),
        P(None, "tile", None),
        P(None, "tile", None),
        P(),
        P("mem"),
        P("tile", None),
    )
    return jax.shard_map(
        per_device,
        mesh=mesh,
        in_specs=placed,
        out_specs=P("mem", None, "tile", None),
        check_vma=False,
    )
```

```python
import functools

import jax
import jax.numpy as jnp
from jax import lax
from jax.experimental import pallas as pl
from jax.experimental.pallas import tpu as pltpu
from jax.sharding import PartitionSpec as P

MESH_ID = pl.DeviceIdType.MESH


def allreduce_kernel(n, x_ref, o_ref, recv, red, gath, s1, r1, s2, r2):
    me = lax.axis_index("mem")
    tile = lax.axis_index("tile")
    rows = x_ref.shape[0] // n
    peers = [lax.rem(me + d, n) for d in range(1, n)]
    barrier = pltpu.get_barrier_semaphore()
    for peer in peers:
        pl.semaphore_signal(barrier, inc=1, device_id=(tile, peer), device_id_type=MESH_ID)
    pl.semaphore_wait(barrier, n - 1)

    def scatter_copy(peer):
        return pltpu.make_async_remote_copy(
            src_ref=x_ref.at[pl.ds(peer * rows, rows)],
            dst_ref=recv.at[me],
            send_sem=s1.at[peer],
            recv_sem=r1.at[me],
            device_id=(tile, peer),
            device_id_type=MESH_ID,
        )

    def gather_copy(peer):
        return pltpu.make_async_remote_copy(
            src_ref=red,
            dst_ref=gath.at[me],
            send_sem=s2.at[peer],
            recv_sem=r2.at[me],
            device_id=(tile, peer),
            device_id_type=MESH_ID,
        )

    firsts = [scatter_copy(peer) for peer in peers]
    for copy in firsts:
        copy.start()
    for peer in peers:
        pltpu.make_async_remote_copy(
            src_ref=x_ref.at[pl.ds(0, rows)],
            dst_ref=recv.at[peer],
            send_sem=s1.at[peer],
            recv_sem=r1.at[peer],
            device_id=(tile, peer),
            device_id_type=MESH_ID,
        ).wait_recv()
    acc = x_ref[pl.ds(me * rows, rows)]
    for peer in peers:
        acc = acc + recv[peer]
    red[...] = acc
    o_ref[pl.ds(me * rows, rows)] = acc
    seconds = [gather_copy(peer) for peer in peers]
    for copy in seconds:
        copy.start()
    for peer in peers:
        pltpu.make_async_remote_copy(
            src_ref=red,
            dst_ref=gath.at[peer],
            send_sem=s2.at[peer],
            recv_sem=r2.at[peer],
            device_id=(tile, peer),
            device_id_type=MESH_ID,
        ).wait_recv()
        o_ref[pl.ds(peer * rows, rows)] = gath[peer]
    for copy in firsts + seconds:
        copy.wait_send()


def member_allreduce(total):
    n = lax.axis_size("mem")
    rows = total.shape[0] // n
    chunk = (rows,) + total.shape[1:]
    return pl.pallas_call(
        functools.partial(allreduce_kernel, n),
        out_shape=jax.ShapeDtypeStruct(total.shape, total.dtype),
        in_specs=[pl.BlockSpec(memory_space=pltpu.VMEM)],
        out_specs=pl.BlockSpec(memory_space=pltpu.VMEM),
        scratch_shapes=[
            pltpu.VMEM((n,) + chunk, total.dtype),
            pltpu.VMEM(chunk, total.dtype),
            pltpu.VMEM((n,) + chunk, total.dtype),
            pltpu.SemaphoreType.DMA((n,)),
            pltpu.SemaphoreType.DMA((n,)),
            pltpu.SemaphoreType.DMA((n,)),
            pltpu.SemaphoreType.DMA((n,)),
        ],
        compiler_params=pltpu.CompilerParams(collective_id=0, has_side_effects=True),
    )(total)


def with_halo(block, sides, width):
    for axis, dim in sides:
        count = lax.axis_size(axis)
        forward = [(i, i + 1) for i in range(count - 1)]
        backward = [(target, source) for source, target in forward]
        low = lax.ppermute(
            lax.slice_in_dim(block, block.shape[dim] - width, None, axis=dim), axis, forward
        )
        high = lax.ppermute(lax.slice_in_dim(block, 0, width, axis=dim), axis, backward)
        block = jnp.concatenate([low, block, high], axis=dim)
    return block


def minmod(first_diff, second_diff):
    return (
        0.5
        * (jnp.sign(first_diff) + jnp.sign(second_diff))
        * jnp.minimum(jnp.abs(first_diff), jnp.abs(second_diff))
    )


def face_flux(courant, far_back, near_back, near_ahead, far_ahead, open_face):
    positive = courant > 0.0
    upwind = jnp.where(positive, near_back, near_ahead)
    side_diff = jnp.where(positive, near_back - far_back, far_ahead - near_ahead)
    limited = minmod(near_ahead - near_back, side_diff)
    magnitude = jnp.abs(courant)
    return (courant * upwind + 0.5 * magnitude * (1.0 - magnitude) * limited) * open_face


def advect(salinity, east_courant, eastern_face_open, north_courant, wet_cells):
    columns = salinity.shape[2]
    east_flux = face_flux(
        east_courant,
        salinity[:, :, 0 : columns - 3],
        salinity[:, :, 1 : columns - 2],
        salinity[:, :, 2 : columns - 1],
        salinity[:, :, 3:columns],
        eastern_face_open,
    )
    interior = salinity[:, :, 2 : columns - 2]
    zero_col = jnp.zeros_like(interior[..., :1])
    lower_cells = jnp.concatenate([zero_col, interior[..., :-1]], -1)
    upper_cells = jnp.concatenate([interior[..., 1:], zero_col], -1)
    upper_two = jnp.concatenate([interior[..., 2:], zero_col, zero_col], -1)
    wet_next = jnp.concatenate([wet_cells[:, 1:], jnp.zeros_like(wet_cells[:, :1])], -1)
    poleward_transport = face_flux(
        north_courant, lower_cells, interior, upper_cells, upper_two, wet_cells * wet_next
    )
    equatorward_transport = jnp.concatenate([zero_col, poleward_transport[..., :-1]], -1)
    return (
        interior
        - (east_flux[:, :, 1:] - east_flux[:, :, :-1])
        - (poleward_transport - equatorward_transport)
    )


def factor(diff_rates):
    levels = diff_rates.shape[1] + 1
    thomas_coefficients = []
    inverse_terms = []
    previous = None
    for level_index in range(levels):
        diagonal = jnp.ones_like(diff_rates[:, 0])
        if level_index > 0:
            diagonal = diagonal + diff_rates[:, level_index - 1]
        if level_index < levels - 1:
            diagonal = diagonal + diff_rates[:, level_index]
        if level_index > 0:
            diagonal = diagonal + diff_rates[:, level_index - 1] * previous
        inverse_den = 1.0 / diagonal
        inverse_terms.append(inverse_den)
        if level_index < levels - 1:
            previous = -diff_rates[:, level_index] * inverse_den
            thomas_coefficients.append(previous)
    return (diff_rates, thomas_coefficients, inverse_terms)


def solve_columns(values, tridiag_terms):
    diff_rates, thomas_coefficients, inverse_terms = tridiag_terms
    levels = values.shape[1]
    forward = [values[:, 0] * inverse_terms[0]]
    for level_index in range(1, levels):
        forward.append(
            (values[:, level_index] + diff_rates[:, level_index - 1] * forward[-1])
            * inverse_terms[level_index]
        )
    solution = [None] * levels
    solution[levels - 1] = forward[levels - 1]
    for level_index in range(levels - 2, -1, -1):
        solution[level_index] = (
            forward[level_index] - thomas_coefficients[level_index] * solution[level_index + 1]
        )
    return jnp.stack(solution, 1)


def per_device(members, control, u_courant, v_courant, diffusion, group_scale, group_of, wet):
    levels = members.shape[1]
    columns = members.shape[2]
    realisation_total = members.shape[0] * lax.axis_size("mem")
    group_ids = jnp.arange(group_scale.shape[0], dtype=jnp.int32)
    spread_multiplier = jnp.sum(
        jnp.where(group_of[:, None] == group_ids[None, :], group_scale[None, :], 0.0), 1
    )
    wet_float = wet.astype(jnp.float32)
    local_total = jnp.sum(members, 0)
    member_total = member_allreduce(local_total)
    recentre_shift = control - member_total / realisation_total
    salinity = members + recentre_shift[None]
    extended = with_halo(jnp.concatenate([u_courant, wet_float[None]], 0), (("tile", 1),), 1)
    east_courant = extended[:levels, 0 : columns + 1]
    wet_ext = extended[levels]
    eastern_face_open = wet_ext[0 : columns + 1] * wet_ext[1 : columns + 2]
    tridiag_terms = factor(spread_multiplier[:, None, None, None] * diffusion[None])

    def rows_of(terms, start, stop):
        return jax.tree.map(lambda a: a[..., start:stop, :], terms)

    def piece(padded, start, stop):
        advected = advect(
            padded,
            east_courant[:, start : stop + 1],
            eastern_face_open[start : stop + 1],
            v_courant[:, start:stop],
            wet_float[start:stop],
        )
        return solve_columns(advected, rows_of(tridiag_terms, start, stop))

    count = lax.axis_size("tile")
    forward = [(i, i + 1) for i in range(count - 1)]
    backward = [(target, source) for source, target in forward]
    for time_step_index in range(2):
        low = lax.ppermute(salinity[:, :, columns - 2 :], "tile", forward)
        high = lax.ppermute(salinity[:, :, :2], "tile", backward)
        middle = piece(salinity, 2, columns - 2)
        first = piece(jnp.concatenate([low, salinity[:, :, :4]], 2), 0, 2)
        last = piece(jnp.concatenate([salinity[:, :, columns - 4 :], high], 2), columns - 2, columns)
        salinity = jnp.concatenate([first, middle, last], 2)
    return salinity


def solution(mesh):
    placed = (
        P("mem", None, "tile", None),
        P(None, "tile", None),
        P(None, "tile", None),
        P(None, "tile", None),
        P(None, "tile", None),
        P(),
        P("mem"),
        P("tile", None),
    )
    return jax.shard_map(
        per_device,
        mesh=mesh,
        in_specs=placed,
        out_specs=P("mem", None, "tile", None),
        check_vma=False,
    )
```

```python
import functools

import jax
import jax.numpy as jnp
from jax import lax
from jax.experimental import pallas as pl
from jax.experimental.pallas import tpu as pltpu
from jax.sharding import PartitionSpec as P

MESH_ID = pl.DeviceIdType.MESH


def recentre_kernel(n, members_ref, control_ref, o_ref, total, recv, full, s1, r1, s2, r2):
    me = lax.axis_index("mem")
    tile = lax.axis_index("tile")
    rows = total.shape[0] // n
    peers = [lax.rem(me + d, n) for d in range(1, n)]
    barrier = pltpu.get_barrier_semaphore()
    for peer in peers:
        pl.semaphore_signal(barrier, inc=1, device_id=(tile, peer), device_id_type=MESH_ID)
    pl.semaphore_wait(barrier, n - 1)

    local = members_ref[0]
    for m in range(1, members_ref.shape[0]):
        local = local + members_ref[m]
    total[...] = local

    def copy_to(src, dst, send, recv_sem, peer):
        return pltpu.make_async_remote_copy(
            src_ref=src,
            dst_ref=dst,
            send_sem=send,
            recv_sem=recv_sem,
            device_id=(tile, peer),
            device_id_type=MESH_ID,
        )

    own = pl.ds(me * rows, rows)
    firsts = [
        copy_to(total.at[pl.ds(peer * rows, rows)], recv.at[me], s1.at[peer], r1.at[me], peer)
        for peer in peers
    ]
    for copy in firsts:
        copy.start()
    for peer in peers:
        copy_to(total.at[own], recv.at[peer], s1.at[peer], r1.at[peer], peer).wait_recv()
    acc = total[own]
    for peer in peers:
        acc = acc + recv[peer]
    full[own] = acc
    seconds = [copy_to(full.at[own], full.at[own], s2.at[peer], r2.at[me], peer) for peer in peers]
    for copy in seconds:
        copy.start()
    for peer in peers:
        part = pl.ds(peer * rows, rows)
        copy_to(full.at[part], full.at[part], s2.at[peer], r2.at[peer], peer).wait_recv()
    for copy in firsts + seconds:
        copy.wait_send()

    def recentre(k, carry):
        shift = control_ref[k] - full[k] * (1.0 / (n * members_ref.shape[0]))
        for m in range(members_ref.shape[0]):
            o_ref[m, k] = members_ref[m, k] + shift
        return carry

    lax.fori_loop(0, total.shape[0], recentre, 0)


def recentre_members(members, control):
    n = lax.axis_size("mem")
    rows = control.shape[0] // n
    chunk = (rows,) + control.shape[1:]
    return pl.pallas_call(
        functools.partial(recentre_kernel, n),
        out_shape=jax.ShapeDtypeStruct(members.shape, members.dtype),
        in_specs=[pl.BlockSpec(memory_space=pltpu.VMEM)] * 2,
        out_specs=pl.BlockSpec(memory_space=pltpu.VMEM),
        scratch_shapes=[
            pltpu.VMEM(control.shape, jnp.float32),
            pltpu.VMEM((n,) + chunk, jnp.float32),
            pltpu.VMEM(control.shape, jnp.float32),
            pltpu.SemaphoreType.DMA((n,)),
            pltpu.SemaphoreType.DMA((n,)),
            pltpu.SemaphoreType.DMA((n,)),
            pltpu.SemaphoreType.DMA((n,)),
        ],
        compiler_params=pltpu.CompilerParams(collective_id=0, has_side_effects=True),
    )(members, control)


def with_halo(block, sides, width):
    for axis, dim in sides:
        count = lax.axis_size(axis)
        forward = [(i, i + 1) for i in range(count - 1)]
        backward = [(target, source) for source, target in forward]
        low = lax.ppermute(
            lax.slice_in_dim(block, block.shape[dim] - width, None, axis=dim), axis, forward
        )
        high = lax.ppermute(lax.slice_in_dim(block, 0, width, axis=dim), axis, backward)
        block = jnp.concatenate([low, block, high], axis=dim)
    return block


def minmod(first_diff, second_diff):
    return (
        0.5
        * (jnp.sign(first_diff) + jnp.sign(second_diff))
        * jnp.minimum(jnp.abs(first_diff), jnp.abs(second_diff))
    )


def face_flux(courant, far_back, near_back, near_ahead, far_ahead, open_face):
    positive = courant > 0.0
    upwind = jnp.where(positive, near_back, near_ahead)
    side_diff = jnp.where(positive, near_back - far_back, far_ahead - near_ahead)
    limited = minmod(near_ahead - near_back, side_diff)
    magnitude = jnp.abs(courant)
    return (courant * upwind + 0.5 * magnitude * (1.0 - magnitude) * limited) * open_face


def advect(salinity, east_courant, eastern_face_open, north_courant, wet_cells):
    columns = salinity.shape[2]
    east_flux = face_flux(
        east_courant,
        salinity[:, :, 0 : columns - 3],
        salinity[:, :, 1 : columns - 2],
        salinity[:, :, 2 : columns - 1],
        salinity[:, :, 3:columns],
        eastern_face_open,
    )
    interior = salinity[:, :, 2 : columns - 2]
    zero_col = jnp.zeros_like(interior[..., :1])
    lower_cells = jnp.concatenate([zero_col, interior[..., :-1]], -1)
    upper_cells = jnp.concatenate([interior[..., 1:], zero_col], -1)
    upper_two = jnp.concatenate([interior[..., 2:], zero_col, zero_col], -1)
    wet_next = jnp.concatenate([wet_cells[:, 1:], jnp.zeros_like(wet_cells[:, :1])], -1)
    poleward_transport = face_flux(
        north_courant, lower_cells, interior, upper_cells, upper_two, wet_cells * wet_next
    )
    equatorward_transport = jnp.concatenate([zero_col, poleward_transport[..., :-1]], -1)
    return (
        interior
        - (east_flux[:, :, 1:] - east_flux[:, :, :-1])
        - (poleward_transport - equatorward_transport)
    )


def factor(diff_rates):
    levels = diff_rates.shape[1] + 1
    thomas_coefficients = []
    inverse_terms = []
    previous = None
    for level_index in range(levels):
        diagonal = jnp.ones_like(diff_rates[:, 0])
        if level_index > 0:
            diagonal = diagonal + diff_rates[:, level_index - 1]
        if level_index < levels - 1:
            diagonal = diagonal + diff_rates[:, level_index]
        if level_index > 0:
            diagonal = diagonal + diff_rates[:, level_index - 1] * previous
        inverse_den = 1.0 / diagonal
        inverse_terms.append(inverse_den)
        if level_index < levels - 1:
            previous = -diff_rates[:, level_index] * inverse_den
            thomas_coefficients.append(previous)
    return (diff_rates, thomas_coefficients, inverse_terms)


def solve_columns(values, tridiag_terms):
    diff_rates, thomas_coefficients, inverse_terms = tridiag_terms
    levels = values.shape[1]
    forward = [values[:, 0] * inverse_terms[0]]
    for level_index in range(1, levels):
        forward.append(
            (values[:, level_index] + diff_rates[:, level_index - 1] * forward[-1])
            * inverse_terms[level_index]
        )
    solution = [None] * levels
    solution[levels - 1] = forward[levels - 1]
    for level_index in range(levels - 2, -1, -1):
        solution[level_index] = (
            forward[level_index] - thomas_coefficients[level_index] * solution[level_index + 1]
        )
    return jnp.stack(solution, 1)


def per_device(members, control, u_courant, v_courant, diffusion, group_scale, group_of, wet):
    levels = members.shape[1]
    columns = members.shape[2]
    realisation_total = members.shape[0] * lax.axis_size("mem")
    group_ids = jnp.arange(group_scale.shape[0], dtype=jnp.int32)
    spread_multiplier = jnp.sum(
        jnp.where(group_of[:, None] == group_ids[None, :], group_scale[None, :], 0.0), 1
    )
    wet_float = wet.astype(jnp.float32)
    salinity = recentre_members(members, control)
    extended = with_halo(jnp.concatenate([u_courant, wet_float[None]], 0), (("tile", 1),), 1)
    east_courant = extended[:levels, 0 : columns + 1]
    wet_ext = extended[levels]
    eastern_face_open = wet_ext[0 : columns + 1] * wet_ext[1 : columns + 2]
    tridiag_terms = factor(spread_multiplier[:, None, None, None] * diffusion[None])
    for time_step_index in range(2):
        padded = with_halo(salinity, (("tile", 2),), 2)
        salinity = solve_columns(
            advect(padded, east_courant, eastern_face_open, v_courant, wet_float), tridiag_terms
        )
    return salinity


def solution(mesh):
    placed = (
        P("mem", None, "tile", None),
        P(None, "tile", None),
        P(None, "tile", None),
        P(None, "tile", None),
        P(None, "tile", None),
        P(),
        P("mem"),
        P("tile", None),
    )
    return jax.shard_map(
        per_device,
        mesh=mesh,
        in_specs=placed,
        out_specs=P("mem", None, "tile", None),
        check_vma=False,
    )
```

```python
import functools

import jax
import jax.numpy as jnp
from jax import lax
from jax.experimental import pallas as pl
from jax.experimental.pallas import tpu as pltpu
from jax.sharding import PartitionSpec as P

MESH_ID = pl.DeviceIdType.MESH


def allreduce_kernel(n, x_ref, o_ref, recv, red, gath, s1, r1, s2, r2):
    me = lax.axis_index("mem")
    tile = lax.axis_index("tile")
    rows = x_ref.shape[0] // n
    peers = [lax.rem(me + d, n) for d in range(1, n)]
    barrier = pltpu.get_barrier_semaphore()
    for peer in peers:
        pl.semaphore_signal(barrier, inc=1, device_id=(tile, peer), device_id_type=MESH_ID)
    pl.semaphore_wait(barrier, n - 1)

    def scatter_copy(peer):
        return pltpu.make_async_remote_copy(
            src_ref=x_ref.at[pl.ds(peer * rows, rows)],
            dst_ref=recv.at[me],
            send_sem=s1.at[peer],
            recv_sem=r1.at[me],
            device_id=(tile, peer),
            device_id_type=MESH_ID,
        )

    def gather_copy(peer):
        return pltpu.make_async_remote_copy(
            src_ref=red,
            dst_ref=gath.at[me],
            send_sem=s2.at[peer],
            recv_sem=r2.at[me],
            device_id=(tile, peer),
            device_id_type=MESH_ID,
        )

    firsts = [scatter_copy(peer) for peer in peers]
    for copy in firsts:
        copy.start()
    for peer in peers:
        pltpu.make_async_remote_copy(
            src_ref=x_ref.at[pl.ds(0, rows)],
            dst_ref=recv.at[peer],
            send_sem=s1.at[peer],
            recv_sem=r1.at[peer],
            device_id=(tile, peer),
            device_id_type=MESH_ID,
        ).wait_recv()
    acc = x_ref[pl.ds(me * rows, rows)]
    for peer in peers:
        acc = acc + recv[peer]
    red[...] = acc
    o_ref[pl.ds(me * rows, rows)] = acc
    seconds = [gather_copy(peer) for peer in peers]
    for copy in seconds:
        copy.start()
    for peer in peers:
        pltpu.make_async_remote_copy(
            src_ref=red,
            dst_ref=gath.at[peer],
            send_sem=s2.at[peer],
            recv_sem=r2.at[peer],
            device_id=(tile, peer),
            device_id_type=MESH_ID,
        ).wait_recv()
        o_ref[pl.ds(peer * rows, rows)] = gath[peer]
    for copy in firsts + seconds:
        copy.wait_send()


def member_allreduce(total):
    n = lax.axis_size("mem")
    rows = total.shape[0] // n
    chunk = (rows,) + total.shape[1:]
    return pl.pallas_call(
        functools.partial(allreduce_kernel, n),
        out_shape=jax.ShapeDtypeStruct(total.shape, total.dtype),
        in_specs=[pl.BlockSpec(memory_space=pltpu.VMEM)],
        out_specs=pl.BlockSpec(memory_space=pltpu.VMEM),
        scratch_shapes=[
            pltpu.VMEM((n,) + chunk, total.dtype),
            pltpu.VMEM(chunk, total.dtype),
            pltpu.VMEM((n,) + chunk, total.dtype),
            pltpu.SemaphoreType.DMA((n,)),
            pltpu.SemaphoreType.DMA((n,)),
            pltpu.SemaphoreType.DMA((n,)),
            pltpu.SemaphoreType.DMA((n,)),
        ],
        compiler_params=pltpu.CompilerParams(collective_id=0, has_side_effects=True),
    )(total)


def with_halo(block, sides, width):
    for axis, dim in sides:
        count = lax.axis_size(axis)
        forward = [(i, i + 1) for i in range(count - 1)]
        backward = [(target, source) for source, target in forward]
        low = lax.ppermute(
            lax.slice_in_dim(block, block.shape[dim] - width, None, axis=dim), axis, forward
        )
        high = lax.ppermute(lax.slice_in_dim(block, 0, width, axis=dim), axis, backward)
        block = jnp.concatenate([low, block, high], axis=dim)
    return block


def minmod(first_diff, second_diff):
    return (
        0.5
        * (jnp.sign(first_diff) + jnp.sign(second_diff))
        * jnp.minimum(jnp.abs(first_diff), jnp.abs(second_diff))
    )


def face_flux(courant, far_back, near_back, near_ahead, far_ahead, open_face):
    positive = courant > 0.0
    upwind = jnp.where(positive, near_back, near_ahead)
    side_diff = jnp.where(positive, near_back - far_back, far_ahead - near_ahead)
    limited = minmod(near_ahead - near_back, side_diff)
    magnitude = jnp.abs(courant)
    return (courant * upwind + 0.5 * magnitude * (1.0 - magnitude) * limited) * open_face


def advect(salinity, east_courant, eastern_face_open, north_courant, wet_cells):
    columns = salinity.shape[2]
    east_flux = face_flux(
        east_courant,
        salinity[:, :, 0 : columns - 3],
        salinity[:, :, 1 : columns - 2],
        salinity[:, :, 2 : columns - 1],
        salinity[:, :, 3:columns],
        eastern_face_open,
    )
    interior = salinity[:, :, 2 : columns - 2]
    zero_col = jnp.zeros_like(interior[..., :1])
    lower_cells = jnp.concatenate([zero_col, interior[..., :-1]], -1)
    upper_cells = jnp.concatenate([interior[..., 1:], zero_col], -1)
    upper_two = jnp.concatenate([interior[..., 2:], zero_col, zero_col], -1)
    wet_next = jnp.concatenate([wet_cells[:, 1:], jnp.zeros_like(wet_cells[:, :1])], -1)
    poleward_transport = face_flux(
        north_courant, lower_cells, interior, upper_cells, upper_two, wet_cells * wet_next
    )
    equatorward_transport = jnp.concatenate([zero_col, poleward_transport[..., :-1]], -1)
    return (
        interior
        - (east_flux[:, :, 1:] - east_flux[:, :, :-1])
        - (poleward_transport - equatorward_transport)
    )


def factor(diff_rates):
    levels = diff_rates.shape[1] + 1
    thomas_coefficients = []
    inverse_terms = []
    previous = None
    for level_index in range(levels):
        diagonal = jnp.ones_like(diff_rates[:, 0])
        if level_index > 0:
            diagonal = diagonal + diff_rates[:, level_index - 1]
        if level_index < levels - 1:
            diagonal = diagonal + diff_rates[:, level_index]
        if level_index > 0:
            diagonal = diagonal + diff_rates[:, level_index - 1] * previous
        inverse_den = 1.0 / diagonal
        inverse_terms.append(inverse_den)
        if level_index < levels - 1:
            previous = -diff_rates[:, level_index] * inverse_den
            thomas_coefficients.append(previous)
    return (diff_rates, thomas_coefficients, inverse_terms)


def solve_columns(values, tridiag_terms):
    diff_rates, thomas_coefficients, inverse_terms = tridiag_terms
    levels = values.shape[1]
    forward = [values[:, 0] * inverse_terms[0]]
    for level_index in range(1, levels):
        forward.append(
            (values[:, level_index] + diff_rates[:, level_index - 1] * forward[-1])
            * inverse_terms[level_index]
        )
    solution = [None] * levels
    solution[levels - 1] = forward[levels - 1]
    for level_index in range(levels - 2, -1, -1):
        solution[level_index] = (
            forward[level_index] - thomas_coefficients[level_index] * solution[level_index + 1]
        )
    return jnp.stack(solution, 1)


def per_device(members, control, u_courant, v_courant, diffusion, group_scale, group_of, wet):
    levels = members.shape[1]
    columns = members.shape[2]
    realisation_total = members.shape[0] * lax.axis_size("mem")
    group_ids = jnp.arange(group_scale.shape[0], dtype=jnp.int32)
    spread_multiplier = jnp.sum(
        jnp.where(group_of[:, None] == group_ids[None, :], group_scale[None, :], 0.0), 1
    )
    wet_float = wet.astype(jnp.float32)
    local_total = jnp.sum(members, 0)
    member_total = member_allreduce(local_total)
    recentre_shift = control - member_total / realisation_total
    salinity = members + recentre_shift[None]
    count = lax.axis_size("tile")
    forward = [(i, i + 1) for i in range(count - 1)]
    backward = [(target, source) for source, target in forward]
    low_edge = lax.ppermute(
        jnp.concatenate([u_courant[:, columns - 1 :], wet_float[None, columns - 1 :]], 0),
        "tile",
        forward,
    )
    high_wet = lax.ppermute(wet_float[:1], "tile", backward)
    east_courant = jnp.concatenate([low_edge[:levels], u_courant], 1)
    wet_ext = jnp.concatenate([low_edge[levels], wet_float, high_wet], 0)
    eastern_face_open = wet_ext[0 : columns + 1] * wet_ext[1 : columns + 2]
    tridiag_terms = factor(spread_multiplier[:, None, None, None] * diffusion[None])
    for time_step_index in range(2):
        padded = with_halo(salinity, (("tile", 2),), 2)
        salinity = solve_columns(
            advect(padded, east_courant, eastern_face_open, v_courant, wet_float), tridiag_terms
        )
    return salinity


def solution(mesh):
    placed = (
        P("mem", None, "tile", None),
        P(None, "tile", None),
        P(None, "tile", None),
        P(None, "tile", None),
        P(None, "tile", None),
        P(),
        P("mem"),
        P("tile", None),
    )
    return jax.shard_map(
        per_device,
        mesh=mesh,
        in_specs=placed,
        out_specs=P("mem", None, "tile", None),
        check_vma=False,
    )
```

```python
import functools

import jax
import jax.numpy as jnp
from jax import lax
from jax.experimental import pallas as pl
from jax.experimental.pallas import tpu as pltpu
from jax.sharding import PartitionSpec as P

MESH_ID = pl.DeviceIdType.MESH


def allreduce_kernel(
    n, x_ref, u_ref, wet_ref, o_ref, ulow_ref, wlow_ref, whigh_ref,
    recv, red, gath, uedge, wedge, ubuf, wbuf, s1, r1, s2, r2, se, re,
):
    me = lax.axis_index("mem")
    tile = lax.axis_index("tile")
    tiles = lax.axis_size("tile")
    has_left = tile > 0
    has_right = tile < tiles - 1
    rows = x_ref.shape[0] // n
    columns = u_ref.shape[1]
    peers = [lax.rem(me + d, n) for d in range(1, n)]
    barrier = pltpu.get_barrier_semaphore()
    for peer in peers:
        pl.semaphore_signal(barrier, inc=1, device_id=(tile, peer), device_id_type=MESH_ID)

    @pl.when(has_left)
    def _():
        pl.semaphore_signal(barrier, inc=1, device_id=(tile - 1, me), device_id_type=MESH_ID)

    @pl.when(has_right)
    def _():
        pl.semaphore_signal(barrier, inc=1, device_id=(tile + 1, me), device_id_type=MESH_ID)

    uedge[...] = u_ref[:, columns - 1, :]
    wedge[0] = wet_ref[pl.ds(columns - 1, 1), :]
    wedge[1] = wet_ref[pl.ds(0, 1), :]
    pl.semaphore_wait(
        barrier, n - 1 + has_left.astype(jnp.int32) + has_right.astype(jnp.int32)
    )

    def copy_to(src, dst, send, recv_sem, device):
        return pltpu.make_async_remote_copy(
            src_ref=src,
            dst_ref=dst,
            send_sem=send,
            recv_sem=recv_sem,
            device_id=device,
            device_id_type=MESH_ID,
        )

    right_copies = [
        copy_to(uedge, ubuf, se.at[0], re.at[0], (tile + 1, me)),
        copy_to(wedge.at[0], wbuf.at[0], se.at[1], re.at[1], (tile + 1, me)),
    ]
    left_copy = copy_to(wedge.at[1], wbuf.at[1], se.at[2], re.at[2], (tile - 1, me))

    @pl.when(has_right)
    def _():
        for copy in right_copies:
            copy.start()

    @pl.when(has_left)
    def _():
        left_copy.start()

    firsts = [
        copy_to(x_ref.at[pl.ds(peer * rows, rows)], recv.at[me], s1.at[peer], r1.at[me], (tile, peer))
        for peer in peers
    ]
    for copy in firsts:
        copy.start()
    for peer in peers:
        copy_to(x_ref.at[pl.ds(0, rows)], recv.at[peer], s1.at[peer], r1.at[peer], (tile, peer)).wait_recv()
    acc = x_ref[pl.ds(me * rows, rows)]
    for peer in peers:
        acc = acc + recv[peer]
    red[...] = acc
    o_ref[pl.ds(me * rows, rows)] = acc
    seconds = [copy_to(red, gath.at[me], s2.at[peer], r2.at[me], (tile, peer)) for peer in peers]
    for copy in seconds:
        copy.start()
    for peer in peers:
        copy_to(red, gath.at[peer], s2.at[peer], r2.at[peer], (tile, peer)).wait_recv()
        o_ref[pl.ds(peer * rows, rows)] = gath[peer]
    for copy in firsts + seconds:
        copy.wait_send()

    @pl.when(has_right)
    def _():
        for copy in right_copies:
            copy.wait_send()

    @pl.when(has_left)
    def _():
        left_copy.wait_send()
        for copy in right_copies:
            copy.wait_recv()
        ulow_ref[...] = ubuf[...]
        wlow_ref[...] = wbuf[0]

    @pl.when(jnp.logical_not(has_left))
    def _():
        ulow_ref[...] = jnp.zeros_like(ulow_ref)
        wlow_ref[...] = jnp.zeros_like(wlow_ref)

    @pl.when(has_right)
    def _():
        left_copy.wait_recv()
        whigh_ref[...] = wbuf[1]

    @pl.when(jnp.logical_not(has_right))
    def _():
        whigh_ref[...] = jnp.zeros_like(whigh_ref)


def member_allreduce(total, u_courant, wet):
    n = lax.axis_size("mem")
    rows = total.shape[0] // n
    chunk = (rows,) + total.shape[1:]
    levels, lanes = u_courant.shape[0], u_courant.shape[2]
    vmem = pl.BlockSpec(memory_space=pltpu.VMEM)
    return pl.pallas_call(
        functools.partial(allreduce_kernel, n),
        out_shape=(
            jax.ShapeDtypeStruct(total.shape, total.dtype),
            jax.ShapeDtypeStruct((levels, lanes), u_courant.dtype),
            jax.ShapeDtypeStruct((1, lanes), wet.dtype),
            jax.ShapeDtypeStruct((1, lanes), wet.dtype),
        ),
        in_specs=[vmem] * 3,
        out_specs=(vmem,) * 4,
        scratch_shapes=[
            pltpu.VMEM((n,) + chunk, total.dtype),
            pltpu.VMEM(chunk, total.dtype),
            pltpu.VMEM((n,) + chunk, total.dtype),
            pltpu.VMEM((levels, lanes), u_courant.dtype),
            pltpu.VMEM((2, 1, lanes), wet.dtype),
            pltpu.VMEM((levels, lanes), u_courant.dtype),
            pltpu.VMEM((2, 1, lanes), wet.dtype),
            pltpu.SemaphoreType.DMA((n,)),
            pltpu.SemaphoreType.DMA((n,)),
            pltpu.SemaphoreType.DMA((n,)),
            pltpu.SemaphoreType.DMA((n,)),
            pltpu.SemaphoreType.DMA((3,)),
            pltpu.SemaphoreType.DMA((3,)),
        ],
        compiler_params=pltpu.CompilerParams(collective_id=0, has_side_effects=True),
    )(total, u_courant, wet)


def with_halo(block, sides, width):
    for axis, dim in sides:
        count = lax.axis_size(axis)
        forward = [(i, i + 1) for i in range(count - 1)]
        backward = [(target, source) for source, target in forward]
        low = lax.ppermute(
            lax.slice_in_dim(block, block.shape[dim] - width, None, axis=dim), axis, forward
        )
        high = lax.ppermute(lax.slice_in_dim(block, 0, width, axis=dim), axis, backward)
        block = jnp.concatenate([low, block, high], axis=dim)
    return block


def minmod(first_diff, second_diff):
    return (
        0.5
        * (jnp.sign(first_diff) + jnp.sign(second_diff))
        * jnp.minimum(jnp.abs(first_diff), jnp.abs(second_diff))
    )


def face_flux(courant, far_back, near_back, near_ahead, far_ahead, open_face):
    positive = courant > 0.0
    upwind = jnp.where(positive, near_back, near_ahead)
    side_diff = jnp.where(positive, near_back - far_back, far_ahead - near_ahead)
    limited = minmod(near_ahead - near_back, side_diff)
    magnitude = jnp.abs(courant)
    return (courant * upwind + 0.5 * magnitude * (1.0 - magnitude) * limited) * open_face


def advect(salinity, east_courant, eastern_face_open, north_courant, wet_cells):
    columns = salinity.shape[2]
    east_flux = face_flux(
        east_courant,
        salinity[:, :, 0 : columns - 3],
        salinity[:, :, 1 : columns - 2],
        salinity[:, :, 2 : columns - 1],
        salinity[:, :, 3:columns],
        eastern_face_open,
    )
    interior = salinity[:, :, 2 : columns - 2]
    zero_col = jnp.zeros_like(interior[..., :1])
    lower_cells = jnp.concatenate([zero_col, interior[..., :-1]], -1)
    upper_cells = jnp.concatenate([interior[..., 1:], zero_col], -1)
    upper_two = jnp.concatenate([interior[..., 2:], zero_col, zero_col], -1)
    wet_next = jnp.concatenate([wet_cells[:, 1:], jnp.zeros_like(wet_cells[:, :1])], -1)
    poleward_transport = face_flux(
        north_courant, lower_cells, interior, upper_cells, upper_two, wet_cells * wet_next
    )
    equatorward_transport = jnp.concatenate([zero_col, poleward_transport[..., :-1]], -1)
    return (
        interior
        - (east_flux[:, :, 1:] - east_flux[:, :, :-1])
        - (poleward_transport - equatorward_transport)
    )


def factor(diff_rates):
    levels = diff_rates.shape[1] + 1
    thomas_coefficients = []
    inverse_terms = []
    previous = None
    for level_index in range(levels):
        diagonal = jnp.ones_like(diff_rates[:, 0])
        if level_index > 0:
            diagonal = diagonal + diff_rates[:, level_index - 1]
        if level_index < levels - 1:
            diagonal = diagonal + diff_rates[:, level_index]
        if level_index > 0:
            diagonal = diagonal + diff_rates[:, level_index - 1] * previous
        inverse_den = 1.0 / diagonal
        inverse_terms.append(inverse_den)
        if level_index < levels - 1:
            previous = -diff_rates[:, level_index] * inverse_den
            thomas_coefficients.append(previous)
    return (diff_rates, thomas_coefficients, inverse_terms)


def solve_columns(values, tridiag_terms):
    diff_rates, thomas_coefficients, inverse_terms = tridiag_terms
    levels = values.shape[1]
    forward = [values[:, 0] * inverse_terms[0]]
    for level_index in range(1, levels):
        forward.append(
            (values[:, level_index] + diff_rates[:, level_index - 1] * forward[-1])
            * inverse_terms[level_index]
        )
    solution = [None] * levels
    solution[levels - 1] = forward[levels - 1]
    for level_index in range(levels - 2, -1, -1):
        solution[level_index] = (
            forward[level_index] - thomas_coefficients[level_index] * solution[level_index + 1]
        )
    return jnp.stack(solution, 1)


def per_device(members, control, u_courant, v_courant, diffusion, group_scale, group_of, wet):
    levels = members.shape[1]
    columns = members.shape[2]
    realisation_total = members.shape[0] * lax.axis_size("mem")
    group_ids = jnp.arange(group_scale.shape[0], dtype=jnp.int32)
    spread_multiplier = jnp.sum(
        jnp.where(group_of[:, None] == group_ids[None, :], group_scale[None, :], 0.0), 1
    )
    wet_float = wet.astype(jnp.float32)
    local_total = jnp.sum(members, 0)
    member_total, u_low, wet_low, wet_high = member_allreduce(local_total, u_courant, wet)
    recentre_shift = control - member_total / realisation_total
    salinity = members + recentre_shift[None]
    east_courant = jnp.concatenate([u_low[:, None], u_courant], 1)
    wet_ext = jnp.concatenate([wet_low, wet, wet_high], 0).astype(jnp.float32)
    eastern_face_open = wet_ext[0 : columns + 1] * wet_ext[1 : columns + 2]
    tridiag_terms = factor(spread_multiplier[:, None, None, None] * diffusion[None])
    for time_step_index in range(2):
        padded = with_halo(salinity, (("tile", 2),), 2)
        salinity = solve_columns(
            advect(padded, east_courant, eastern_face_open, v_courant, wet_float), tridiag_terms
        )
    return salinity


def solution(mesh):
    placed = (
        P("mem", None, "tile", None),
        P(None, "tile", None),
        P(None, "tile", None),
        P(None, "tile", None),
        P(None, "tile", None),
        P(),
        P("mem"),
        P("tile", None),
    )
    return jax.shard_map(
        per_device,
        mesh=mesh,
        in_specs=placed,
        out_specs=P("mem", None, "tile", None),
        check_vma=False,
    )
```

```python
import functools

import jax
import jax.numpy as jnp
from jax import lax
from jax.experimental import pallas as pl
from jax.experimental.pallas import tpu as pltpu
from jax.sharding import PartitionSpec as P

MESH_ID = pl.DeviceIdType.MESH


def allreduce_kernel(
    n, count, x_ref, u_ref, wet_ref, mlo_ref, mhi_ref, c_ref,
    o_ref, ulow_ref, wlow_ref, whigh_ref, mlow_ref, mhigh_ref, slow_ref, shigh_ref,
    recv, red, gath, uedge, wedge, ubuf, wbuf, mlo_buf, mhi_buf, sedge, slo_buf, shi_buf,
    s1, r1, s2, r2, se, re,
):
    me = lax.axis_index("mem")
    tile = lax.axis_index("tile")
    tiles = lax.axis_size("tile")
    has_left = tile > 0
    has_right = tile < tiles - 1
    rows = x_ref.shape[0] // n
    columns = u_ref.shape[1]
    width = mlo_ref.shape[2]
    peers = [lax.rem(me + d, n) for d in range(1, n)]
    barrier = pltpu.get_barrier_semaphore()
    for peer in peers:
        pl.semaphore_signal(barrier, inc=1, device_id=(tile, peer), device_id_type=MESH_ID)

    @pl.when(has_left)
    def _():
        pl.semaphore_signal(barrier, inc=1, device_id=(tile - 1, me), device_id_type=MESH_ID)

    @pl.when(has_right)
    def _():
        pl.semaphore_signal(barrier, inc=1, device_id=(tile + 1, me), device_id_type=MESH_ID)

    uedge[...] = u_ref[:, columns - 1, :]
    wedge[0] = wet_ref[pl.ds(columns - 1, 1), :]
    wedge[1] = wet_ref[pl.ds(0, 1), :]
    pl.semaphore_wait(
        barrier, n - 1 + has_left.astype(jnp.int32) + has_right.astype(jnp.int32)
    )

    def copy_to(src, dst, send, recv_sem, device):
        return pltpu.make_async_remote_copy(
            src_ref=src,
            dst_ref=dst,
            send_sem=send,
            recv_sem=recv_sem,
            device_id=device,
            device_id_type=MESH_ID,
        )

    right = (tile + 1, me)
    left = (tile - 1, me)
    right_early = [
        copy_to(uedge, ubuf, se.at[0], re.at[0], right),
        copy_to(wedge.at[0], wbuf.at[0], se.at[1], re.at[1], right),
        copy_to(mlo_ref, mlo_buf, se.at[3], re.at[3], right),
    ]
    left_early = [
        copy_to(wedge.at[1], wbuf.at[1], se.at[2], re.at[2], left),
        copy_to(mhi_ref, mhi_buf, se.at[4], re.at[4], left),
    ]
    right_late = copy_to(sedge.at[0], slo_buf, se.at[5], re.at[5], right)
    left_late = copy_to(sedge.at[1], shi_buf, se.at[6], re.at[6], left)

    @pl.when(has_right)
    def _():
        for copy in right_early:
            copy.start()

    @pl.when(has_left)
    def _():
        for copy in left_early:
            copy.start()

    firsts = [
        copy_to(x_ref.at[pl.ds(peer * rows, rows)], recv.at[me], s1.at[peer], r1.at[me], (tile, peer))
        for peer in peers
    ]
    for copy in firsts:
        copy.start()
    for peer in peers:
        copy_to(x_ref.at[pl.ds(0, rows)], recv.at[peer], s1.at[peer], r1.at[peer], (tile, peer)).wait_recv()
    acc = x_ref[pl.ds(me * rows, rows)]
    for peer in peers:
        acc = acc + recv[peer]
    red[...] = acc
    o_ref[pl.ds(me * rows, rows)] = acc
    seconds = [copy_to(red, gath.at[me], s2.at[peer], r2.at[me], (tile, peer)) for peer in peers]
    for copy in seconds:
        copy.start()
    for peer in peers:
        copy_to(red, gath.at[peer], s2.at[peer], r2.at[peer], (tile, peer)).wait_recv()
        o_ref[pl.ds(peer * rows, rows)] = gath[peer]

    scale = 1.0 / count
    low_rows = pl.ds(columns - width, width)
    high_rows = pl.ds(0, width)
    sedge[0] = c_ref[:, low_rows, :] - o_ref[:, low_rows, :] * scale
    sedge[1] = c_ref[:, high_rows, :] - o_ref[:, high_rows, :] * scale

    @pl.when(has_right)
    def _():
        right_late.start()

    @pl.when(has_left)
    def _():
        left_late.start()

    for copy in firsts + seconds:
        copy.wait_send()

    @pl.when(has_right)
    def _():
        for copy in right_early + [right_late]:
            copy.wait_send()

    @pl.when(has_left)
    def _():
        for copy in left_early + [left_late]:
            copy.wait_send()
        for copy in right_early + [right_late]:
            copy.wait_recv()
        ulow_ref[...] = ubuf[...]
        wlow_ref[...] = wbuf[0]
        mlow_ref[...] = mlo_buf[...]
        slow_ref[...] = slo_buf[...]

    @pl.when(jnp.logical_not(has_left))
    def _():
        ulow_ref[...] = jnp.zeros_like(ulow_ref)
        wlow_ref[...] = jnp.zeros_like(wlow_ref)
        mlow_ref[...] = jnp.zeros_like(mlow_ref)
        slow_ref[...] = jnp.zeros_like(slow_ref)

    @pl.when(has_right)
    def _():
        for copy in left_early + [left_late]:
            copy.wait_recv()
        whigh_ref[...] = wbuf[1]
        mhigh_ref[...] = mhi_buf[...]
        shigh_ref[...] = shi_buf[...]

    @pl.when(jnp.logical_not(has_right))
    def _():
        whigh_ref[...] = jnp.zeros_like(whigh_ref)
        mhigh_ref[...] = jnp.zeros_like(mhigh_ref)
        shigh_ref[...] = jnp.zeros_like(shigh_ref)


def member_allreduce(total, u_courant, wet, members, control, width, count):
    n = lax.axis_size("mem")
    rows = total.shape[0] // n
    chunk = (rows,) + total.shape[1:]
    levels, columns, lanes = u_courant.shape
    mlo = members[:, :, columns - width :]
    mhi = members[:, :, :width]
    edge = (levels, width, lanes)
    vmem = pl.BlockSpec(memory_space=pltpu.VMEM)
    shape = lambda s, d: jax.ShapeDtypeStruct(s, d)
    return pl.pallas_call(
        functools.partial(allreduce_kernel, n, count),
        out_shape=(
            shape(total.shape, total.dtype),
            shape((levels, lanes), u_courant.dtype),
            shape((1, lanes), wet.dtype),
            shape((1, lanes), wet.dtype),
            shape(mlo.shape, mlo.dtype),
            shape(mhi.shape, mhi.dtype),
            shape(edge, control.dtype),
            shape(edge, control.dtype),
        ),
        in_specs=[vmem] * 6,
        out_specs=(vmem,) * 8,
        scratch_shapes=[
            pltpu.VMEM((n,) + chunk, total.dtype),
            pltpu.VMEM(chunk, total.dtype),
            pltpu.VMEM((n,) + chunk, total.dtype),
            pltpu.VMEM((levels, lanes), u_courant.dtype),
            pltpu.VMEM((2, 1, lanes), wet.dtype),
            pltpu.VMEM((levels, lanes), u_courant.dtype),
            pltpu.VMEM((2, 1, lanes), wet.dtype),
            pltpu.VMEM(mlo.shape, mlo.dtype),
            pltpu.VMEM(mhi.shape, mhi.dtype),
            pltpu.VMEM((2,) + edge, control.dtype),
            pltpu.VMEM(edge, control.dtype),
            pltpu.VMEM(edge, control.dtype),
            pltpu.SemaphoreType.DMA((n,)),
            pltpu.SemaphoreType.DMA((n,)),
            pltpu.SemaphoreType.DMA((n,)),
            pltpu.SemaphoreType.DMA((n,)),
            pltpu.SemaphoreType.DMA((7,)),
            pltpu.SemaphoreType.DMA((7,)),
        ],
        compiler_params=pltpu.CompilerParams(collective_id=0, has_side_effects=True),
    )(total, u_courant, wet, mlo, mhi, control)


def with_halo(block, sides, width):
    for axis, dim in sides:
        count = lax.axis_size(axis)
        forward = [(i, i + 1) for i in range(count - 1)]
        backward = [(target, source) for source, target in forward]
        low = lax.ppermute(
            lax.slice_in_dim(block, block.shape[dim] - width, None, axis=dim), axis, forward
        )
        high = lax.ppermute(lax.slice_in_dim(block, 0, width, axis=dim), axis, backward)
        block = jnp.concatenate([low, block, high], axis=dim)
    return block


def minmod(first_diff, second_diff):
    return (
        0.5
        * (jnp.sign(first_diff) + jnp.sign(second_diff))
        * jnp.minimum(jnp.abs(first_diff), jnp.abs(second_diff))
    )


def face_flux(courant, far_back, near_back, near_ahead, far_ahead, open_face):
    positive = courant > 0.0
    upwind = jnp.where(positive, near_back, near_ahead)
    side_diff = jnp.where(positive, near_back - far_back, far_ahead - near_ahead)
    limited = minmod(near_ahead - near_back, side_diff)
    magnitude = jnp.abs(courant)
    return (courant * upwind + 0.5 * magnitude * (1.0 - magnitude) * limited) * open_face


def advect(salinity, east_courant, eastern_face_open, north_courant, wet_cells):
    columns = salinity.shape[2]
    east_flux = face_flux(
        east_courant,
        salinity[:, :, 0 : columns - 3],
        salinity[:, :, 1 : columns - 2],
        salinity[:, :, 2 : columns - 1],
        salinity[:, :, 3:columns],
        eastern_face_open,
    )
    interior = salinity[:, :, 2 : columns - 2]
    zero_col = jnp.zeros_like(interior[..., :1])
    lower_cells = jnp.concatenate([zero_col, interior[..., :-1]], -1)
    upper_cells = jnp.concatenate([interior[..., 1:], zero_col], -1)
    upper_two = jnp.concatenate([interior[..., 2:], zero_col, zero_col], -1)
    wet_next = jnp.concatenate([wet_cells[:, 1:], jnp.zeros_like(wet_cells[:, :1])], -1)
    poleward_transport = face_flux(
        north_courant, lower_cells, interior, upper_cells, upper_two, wet_cells * wet_next
    )
    equatorward_transport = jnp.concatenate([zero_col, poleward_transport[..., :-1]], -1)
    return (
        interior
        - (east_flux[:, :, 1:] - east_flux[:, :, :-1])
        - (poleward_transport - equatorward_transport)
    )


def factor(diff_rates):
    levels = diff_rates.shape[1] + 1
    thomas_coefficients = []
    inverse_terms = []
    previous = None
    for level_index in range(levels):
        diagonal = jnp.ones_like(diff_rates[:, 0])
        if level_index > 0:
            diagonal = diagonal + diff_rates[:, level_index - 1]
        if level_index < levels - 1:
            diagonal = diagonal + diff_rates[:, level_index]
        if level_index > 0:
            diagonal = diagonal + diff_rates[:, level_index - 1] * previous
        inverse_den = 1.0 / diagonal
        inverse_terms.append(inverse_den)
        if level_index < levels - 1:
            previous = -diff_rates[:, level_index] * inverse_den
            thomas_coefficients.append(previous)
    return (diff_rates, thomas_coefficients, inverse_terms)


def solve_columns(values, tridiag_terms):
    diff_rates, thomas_coefficients, inverse_terms = tridiag_terms
    levels = values.shape[1]
    forward = [values[:, 0] * inverse_terms[0]]
    for level_index in range(1, levels):
        forward.append(
            (values[:, level_index] + diff_rates[:, level_index - 1] * forward[-1])
            * inverse_terms[level_index]
        )
    solution = [None] * levels
    solution[levels - 1] = forward[levels - 1]
    for level_index in range(levels - 2, -1, -1):
        solution[level_index] = (
            forward[level_index] - thomas_coefficients[level_index] * solution[level_index + 1]
        )
    return jnp.stack(solution, 1)


def per_device(members, control, u_courant, v_courant, diffusion, group_scale, group_of, wet):
    levels = members.shape[1]
    columns = members.shape[2]
    realisation_total = members.shape[0] * lax.axis_size("mem")
    group_ids = jnp.arange(group_scale.shape[0], dtype=jnp.int32)
    spread_multiplier = jnp.sum(
        jnp.where(group_of[:, None] == group_ids[None, :], group_scale[None, :], 0.0), 1
    )
    wet_float = wet.astype(jnp.float32)
    local_total = jnp.sum(members, 0)
    member_total, u_low, wet_low, wet_high, m_low, m_high, s_low, s_high = member_allreduce(
        local_total, u_courant, wet, members, control, 2, realisation_total
    )
    recentre_shift = control - member_total / realisation_total
    salinity = members + recentre_shift[None]
    east_courant = jnp.concatenate([u_low[:, None], u_courant], 1)
    wet_ext = jnp.concatenate([wet_low, wet, wet_high], 0).astype(jnp.float32)
    eastern_face_open = wet_ext[0 : columns + 1] * wet_ext[1 : columns + 2]
    tridiag_terms = factor(spread_multiplier[:, None, None, None] * diffusion[None])
    for time_step_index in range(2):
        if time_step_index == 0:
            padded = jnp.concatenate(
                [m_low + s_low[None], salinity, m_high + s_high[None]], 2
            )
        else:
            padded = with_halo(salinity, (("tile", 2),), 2)
        salinity = solve_columns(
            advect(padded, east_courant, eastern_face_open, v_courant, wet_float), tridiag_terms
        )
    return salinity


def solution(mesh):
    placed = (
        P("mem", None, "tile", None),
        P(None, "tile", None),
        P(None, "tile", None),
        P(None, "tile", None),
        P(None, "tile", None),
        P(),
        P("mem"),
        P("tile", None),
    )
    return jax.shard_map(
        per_device,
        mesh=mesh,
        in_specs=placed,
        out_specs=P("mem", None, "tile", None),
        check_vma=False,
    )
```

```python
import functools

import jax
import jax.numpy as jnp
from jax import lax
from jax.experimental import pallas as pl
from jax.experimental.pallas import tpu as pltpu
from jax.sharding import PartitionSpec as P

MESH_ID = pl.DeviceIdType.MESH


def allreduce_kernel(
    n, members_ref, u_ref, wet_ref, o_ref, ulow_ref, wlow_ref, whigh_ref,
    x_ref, recv, red, gath, uedge, wedge, ubuf, wbuf, s1, r1, s2, r2, se, re,
):
    me = lax.axis_index("mem")
    tile = lax.axis_index("tile")
    tiles = lax.axis_size("tile")
    has_left = tile > 0
    has_right = tile < tiles - 1
    rows = x_ref.shape[0] // n
    columns = u_ref.shape[1]
    peers = [lax.rem(me + d, n) for d in range(1, n)]
    barrier = pltpu.get_barrier_semaphore()
    for peer in peers:
        pl.semaphore_signal(barrier, inc=1, device_id=(tile, peer), device_id_type=MESH_ID)

    @pl.when(has_left)
    def _():
        pl.semaphore_signal(barrier, inc=1, device_id=(tile - 1, me), device_id_type=MESH_ID)

    @pl.when(has_right)
    def _():
        pl.semaphore_signal(barrier, inc=1, device_id=(tile + 1, me), device_id_type=MESH_ID)

    uedge[...] = u_ref[:, columns - 1, :]
    wedge[0] = wet_ref[pl.ds(columns - 1, 1), :]
    wedge[1] = wet_ref[pl.ds(0, 1), :]

    def local_sum(k, carry):
        level = members_ref[0, k]
        for m in range(1, members_ref.shape[0]):
            level = level + members_ref[m, k]
        x_ref[k] = level
        return carry

    lax.fori_loop(0, x_ref.shape[0], local_sum, 0)
    pl.semaphore_wait(
        barrier, n - 1 + has_left.astype(jnp.int32) + has_right.astype(jnp.int32)
    )

    def copy_to(src, dst, send, recv_sem, device):
        return pltpu.make_async_remote_copy(
            src_ref=src,
            dst_ref=dst,
            send_sem=send,
            recv_sem=recv_sem,
            device_id=device,
            device_id_type=MESH_ID,
        )

    right_copies = [
        copy_to(uedge, ubuf, se.at[0], re.at[0], (tile + 1, me)),
        copy_to(wedge.at[0], wbuf.at[0], se.at[1], re.at[1], (tile + 1, me)),
    ]
    left_copy = copy_to(wedge.at[1], wbuf.at[1], se.at[2], re.at[2], (tile - 1, me))

    @pl.when(has_right)
    def _():
        for copy in right_copies:
            copy.start()

    @pl.when(has_left)
    def _():
        left_copy.start()

    firsts = [
        copy_to(x_ref.at[pl.ds(peer * rows, rows)], recv.at[me], s1.at[peer], r1.at[me], (tile, peer))
        for peer in peers
    ]
    for copy in firsts:
        copy.start()
    for peer in peers:
        copy_to(x_ref.at[pl.ds(0, rows)], recv.at[peer], s1.at[peer], r1.at[peer], (tile, peer)).wait_recv()
    acc = x_ref[pl.ds(me * rows, rows)]
    for peer in peers:
        acc = acc + recv[peer]
    red[...] = acc
    o_ref[pl.ds(me * rows, rows)] = acc
    seconds = [copy_to(red, gath.at[me], s2.at[peer], r2.at[me], (tile, peer)) for peer in peers]
    for copy in seconds:
        copy.start()
    for peer in peers:
        copy_to(red, gath.at[peer], s2.at[peer], r2.at[peer], (tile, peer)).wait_recv()
        o_ref[pl.ds(peer * rows, rows)] = gath[peer]
    for copy in firsts + seconds:
        copy.wait_send()

    @pl.when(has_right)
    def _():
        for copy in right_copies:
            copy.wait_send()

    @pl.when(has_left)
    def _():
        left_copy.wait_send()
        for copy in right_copies:
            copy.wait_recv()
        ulow_ref[...] = ubuf[...]
        wlow_ref[...] = wbuf[0]

    @pl.when(jnp.logical_not(has_left))
    def _():
        ulow_ref[...] = jnp.zeros_like(ulow_ref)
        wlow_ref[...] = jnp.zeros_like(wlow_ref)

    @pl.when(has_right)
    def _():
        left_copy.wait_recv()
        whigh_ref[...] = wbuf[1]

    @pl.when(jnp.logical_not(has_right))
    def _():
        whigh_ref[...] = jnp.zeros_like(whigh_ref)


def member_allreduce(members, u_courant, wet):
    total = jax.ShapeDtypeStruct(members.shape[1:], members.dtype)
    n = lax.axis_size("mem")
    rows = total.shape[0] // n
    chunk = (rows,) + total.shape[1:]
    levels, lanes = u_courant.shape[0], u_courant.shape[2]
    vmem = pl.BlockSpec(memory_space=pltpu.VMEM)
    return pl.pallas_call(
        functools.partial(allreduce_kernel, n),
        out_shape=(
            jax.ShapeDtypeStruct(total.shape, total.dtype),
            jax.ShapeDtypeStruct((levels, lanes), u_courant.dtype),
            jax.ShapeDtypeStruct((1, lanes), wet.dtype),
            jax.ShapeDtypeStruct((1, lanes), wet.dtype),
        ),
        in_specs=[vmem] * 3,
        out_specs=(vmem,) * 4,
        scratch_shapes=[
            pltpu.VMEM(total.shape, total.dtype),
            pltpu.VMEM((n,) + chunk, total.dtype),
            pltpu.VMEM(chunk, total.dtype),
            pltpu.VMEM((n,) + chunk, total.dtype),
            pltpu.VMEM((levels, lanes), u_courant.dtype),
            pltpu.VMEM((2, 1, lanes), wet.dtype),
            pltpu.VMEM((levels, lanes), u_courant.dtype),
            pltpu.VMEM((2, 1, lanes), wet.dtype),
            pltpu.SemaphoreType.DMA((n,)),
            pltpu.SemaphoreType.DMA((n,)),
            pltpu.SemaphoreType.DMA((n,)),
            pltpu.SemaphoreType.DMA((n,)),
            pltpu.SemaphoreType.DMA((3,)),
            pltpu.SemaphoreType.DMA((3,)),
        ],
        compiler_params=pltpu.CompilerParams(collective_id=0, has_side_effects=True),
    )(members, u_courant, wet)


def with_halo(block, sides, width):
    for axis, dim in sides:
        count = lax.axis_size(axis)
        forward = [(i, i + 1) for i in range(count - 1)]
        backward = [(target, source) for source, target in forward]
        low = lax.ppermute(
            lax.slice_in_dim(block, block.shape[dim] - width, None, axis=dim), axis, forward
        )
        high = lax.ppermute(lax.slice_in_dim(block, 0, width, axis=dim), axis, backward)
        block = jnp.concatenate([low, block, high], axis=dim)
    return block


def minmod(first_diff, second_diff):
    return (
        0.5
        * (jnp.sign(first_diff) + jnp.sign(second_diff))
        * jnp.minimum(jnp.abs(first_diff), jnp.abs(second_diff))
    )


def face_flux(courant, far_back, near_back, near_ahead, far_ahead, open_face):
    positive = courant > 0.0
    upwind = jnp.where(positive, near_back, near_ahead)
    side_diff = jnp.where(positive, near_back - far_back, far_ahead - near_ahead)
    limited = minmod(near_ahead - near_back, side_diff)
    magnitude = jnp.abs(courant)
    return (courant * upwind + 0.5 * magnitude * (1.0 - magnitude) * limited) * open_face


def advect(salinity, east_courant, eastern_face_open, north_courant, wet_cells):
    columns = salinity.shape[2]
    east_flux = face_flux(
        east_courant,
        salinity[:, :, 0 : columns - 3],
        salinity[:, :, 1 : columns - 2],
        salinity[:, :, 2 : columns - 1],
        salinity[:, :, 3:columns],
        eastern_face_open,
    )
    interior = salinity[:, :, 2 : columns - 2]
    zero_col = jnp.zeros_like(interior[..., :1])
    lower_cells = jnp.concatenate([zero_col, interior[..., :-1]], -1)
    upper_cells = jnp.concatenate([interior[..., 1:], zero_col], -1)
    upper_two = jnp.concatenate([interior[..., 2:], zero_col, zero_col], -1)
    wet_next = jnp.concatenate([wet_cells[:, 1:], jnp.zeros_like(wet_cells[:, :1])], -1)
    poleward_transport = face_flux(
        north_courant, lower_cells, interior, upper_cells, upper_two, wet_cells * wet_next
    )
    equatorward_transport = jnp.concatenate([zero_col, poleward_transport[..., :-1]], -1)
    return (
        interior
        - (east_flux[:, :, 1:] - east_flux[:, :, :-1])
        - (poleward_transport - equatorward_transport)
    )


def factor(diff_rates):
    levels = diff_rates.shape[1] + 1
    thomas_coefficients = []
    inverse_terms = []
    previous = None
    for level_index in range(levels):
        diagonal = jnp.ones_like(diff_rates[:, 0])
        if level_index > 0:
            diagonal = diagonal + diff_rates[:, level_index - 1]
        if level_index < levels - 1:
            diagonal = diagonal + diff_rates[:, level_index]
        if level_index > 0:
            diagonal = diagonal + diff_rates[:, level_index - 1] * previous
        inverse_den = 1.0 / diagonal
        inverse_terms.append(inverse_den)
        if level_index < levels - 1:
            previous = -diff_rates[:, level_index] * inverse_den
            thomas_coefficients.append(previous)
    return (diff_rates, thomas_coefficients, inverse_terms)


def solve_columns(values, tridiag_terms):
    diff_rates, thomas_coefficients, inverse_terms = tridiag_terms
    levels = values.shape[1]
    forward = [values[:, 0] * inverse_terms[0]]
    for level_index in range(1, levels):
        forward.append(
            (values[:, level_index] + diff_rates[:, level_index - 1] * forward[-1])
            * inverse_terms[level_index]
        )
    solution = [None] * levels
    solution[levels - 1] = forward[levels - 1]
    for level_index in range(levels - 2, -1, -1):
        solution[level_index] = (
            forward[level_index] - thomas_coefficients[level_index] * solution[level_index + 1]
        )
    return jnp.stack(solution, 1)


def per_device(members, control, u_courant, v_courant, diffusion, group_scale, group_of, wet):
    levels = members.shape[1]
    columns = members.shape[2]
    realisation_total = members.shape[0] * lax.axis_size("mem")
    group_ids = jnp.arange(group_scale.shape[0], dtype=jnp.int32)
    spread_multiplier = jnp.sum(
        jnp.where(group_of[:, None] == group_ids[None, :], group_scale[None, :], 0.0), 1
    )
    wet_float = wet.astype(jnp.float32)
    member_total, u_low, wet_low, wet_high = member_allreduce(members, u_courant, wet)
    recentre_shift = control - member_total / realisation_total
    salinity = members + recentre_shift[None]
    east_courant = jnp.concatenate([u_low[:, None], u_courant], 1)
    wet_ext = jnp.concatenate([wet_low, wet, wet_high], 0).astype(jnp.float32)
    eastern_face_open = wet_ext[0 : columns + 1] * wet_ext[1 : columns + 2]
    tridiag_terms = factor(spread_multiplier[:, None, None, None] * diffusion[None])
    for time_step_index in range(2):
        padded = with_halo(salinity, (("tile", 2),), 2)
        salinity = solve_columns(
            advect(padded, east_courant, eastern_face_open, v_courant, wet_float), tridiag_terms
        )
    return salinity


def solution(mesh):
    placed = (
        P("mem", None, "tile", None),
        P(None, "tile", None),
        P(None, "tile", None),
        P(None, "tile", None),
        P(None, "tile", None),
        P(),
        P("mem"),
        P("tile", None),
    )
    return jax.shard_map(
        per_device,
        mesh=mesh,
        in_specs=placed,
        out_specs=P("mem", None, "tile", None),
        check_vma=False,
    )
```

```python
import functools

import jax
import jax.numpy as jnp
from jax import lax
from jax.experimental import pallas as pl
from jax.experimental.pallas import tpu as pltpu
from jax.sharding import PartitionSpec as P

MESH_ID = pl.DeviceIdType.MESH


def allreduce_kernel(
    n, members_ref, u_ref, wet_ref, o_ref, ulow_ref, wlow_ref, whigh_ref,
    x_ref, recv, red, gath, uedge, wedge, ubuf, wbuf, s1, r1, s2, r2, se, re,
):
    me = lax.axis_index("mem")
    tile = lax.axis_index("tile")
    tiles = lax.axis_size("tile")
    has_left = tile > 0
    has_right = tile < tiles - 1
    rows = x_ref.shape[0] // n
    columns = u_ref.shape[1]
    peers = [lax.rem(me + d, n) for d in range(1, n)]
    uedge[...] = u_ref[:, columns - 1, :]
    wedge[0] = wet_ref[pl.ds(columns - 1, 1), :]
    wedge[1] = wet_ref[pl.ds(0, 1), :]

    def local_sum(k, carry):
        level = members_ref[0, k]
        for m in range(1, members_ref.shape[0]):
            level = level + members_ref[m, k]
        x_ref[k] = level
        return carry

    lax.fori_loop(0, x_ref.shape[0], local_sum, 0)

    def copy_to(src, dst, send, recv_sem, device):
        return pltpu.make_async_remote_copy(
            src_ref=src,
            dst_ref=dst,
            send_sem=send,
            recv_sem=recv_sem,
            device_id=device,
            device_id_type=MESH_ID,
        )

    right_copies = [
        copy_to(uedge, ubuf, se.at[0], re.at[0], (tile + 1, me)),
        copy_to(wedge.at[0], wbuf.at[0], se.at[1], re.at[1], (tile + 1, me)),
    ]
    left_copy = copy_to(wedge.at[1], wbuf.at[1], se.at[2], re.at[2], (tile - 1, me))

    @pl.when(has_right)
    def _():
        for copy in right_copies:
            copy.start()

    @pl.when(has_left)
    def _():
        left_copy.start()

    firsts = [
        copy_to(x_ref.at[pl.ds(peer * rows, rows)], recv.at[me], s1.at[peer], r1.at[me], (tile, peer))
        for peer in peers
    ]
    for copy in firsts:
        copy.start()
    for peer in peers:
        copy_to(x_ref.at[pl.ds(0, rows)], recv.at[peer], s1.at[peer], r1.at[peer], (tile, peer)).wait_recv()
    acc = x_ref[pl.ds(me * rows, rows)]
    for peer in peers:
        acc = acc + recv[peer]
    red[...] = acc
    o_ref[pl.ds(me * rows, rows)] = acc
    seconds = [copy_to(red, gath.at[me], s2.at[peer], r2.at[me], (tile, peer)) for peer in peers]
    for copy in seconds:
        copy.start()
    for peer in peers:
        copy_to(red, gath.at[peer], s2.at[peer], r2.at[peer], (tile, peer)).wait_recv()
        o_ref[pl.ds(peer * rows, rows)] = gath[peer]
    for copy in firsts + seconds:
        copy.wait_send()

    @pl.when(has_right)
    def _():
        for copy in right_copies:
            copy.wait_send()

    @pl.when(has_left)
    def _():
        left_copy.wait_send()
        for copy in right_copies:
            copy.wait_recv()
        ulow_ref[...] = ubuf[...]
        wlow_ref[...] = wbuf[0]

    @pl.when(jnp.logical_not(has_left))
    def _():
        ulow_ref[...] = jnp.zeros_like(ulow_ref)
        wlow_ref[...] = jnp.zeros_like(wlow_ref)

    @pl.when(has_right)
    def _():
        left_copy.wait_recv()
        whigh_ref[...] = wbuf[1]

    @pl.when(jnp.logical_not(has_right))
    def _():
        whigh_ref[...] = jnp.zeros_like(whigh_ref)


def member_allreduce(members, u_courant, wet):
    total = jax.ShapeDtypeStruct(members.shape[1:], members.dtype)
    n = lax.axis_size("mem")
    rows = total.shape[0] // n
    chunk = (rows,) + total.shape[1:]
    levels, lanes = u_courant.shape[0], u_courant.shape[2]
    vmem = pl.BlockSpec(memory_space=pltpu.VMEM)
    return pl.pallas_call(
        functools.partial(allreduce_kernel, n),
        out_shape=(
            jax.ShapeDtypeStruct(total.shape, total.dtype),
            jax.ShapeDtypeStruct((levels, lanes), u_courant.dtype),
            jax.ShapeDtypeStruct((1, lanes), wet.dtype),
            jax.ShapeDtypeStruct((1, lanes), wet.dtype),
        ),
        in_specs=[vmem] * 3,
        out_specs=(vmem,) * 4,
        scratch_shapes=[
            pltpu.VMEM(total.shape, total.dtype),
            pltpu.VMEM((n,) + chunk, total.dtype),
            pltpu.VMEM(chunk, total.dtype),
            pltpu.VMEM((n,) + chunk, total.dtype),
            pltpu.VMEM((levels, lanes), u_courant.dtype),
            pltpu.VMEM((2, 1, lanes), wet.dtype),
            pltpu.VMEM((levels, lanes), u_courant.dtype),
            pltpu.VMEM((2, 1, lanes), wet.dtype),
            pltpu.SemaphoreType.DMA((n,)),
            pltpu.SemaphoreType.DMA((n,)),
            pltpu.SemaphoreType.DMA((n,)),
            pltpu.SemaphoreType.DMA((n,)),
            pltpu.SemaphoreType.DMA((3,)),
            pltpu.SemaphoreType.DMA((3,)),
        ],
        compiler_params=pltpu.CompilerParams(has_side_effects=True),
    )(members, u_courant, wet)


def with_halo(block, sides, width):
    for axis, dim in sides:
        count = lax.axis_size(axis)
        forward = [(i, i + 1) for i in range(count - 1)]
        backward = [(target, source) for source, target in forward]
        low = lax.ppermute(
            lax.slice_in_dim(block, block.shape[dim] - width, None, axis=dim), axis, forward
        )
        high = lax.ppermute(lax.slice_in_dim(block, 0, width, axis=dim), axis, backward)
        block = jnp.concatenate([low, block, high], axis=dim)
    return block


def minmod(first_diff, second_diff):
    return (
        0.5
        * (jnp.sign(first_diff) + jnp.sign(second_diff))
        * jnp.minimum(jnp.abs(first_diff), jnp.abs(second_diff))
    )


def face_flux(courant, far_back, near_back, near_ahead, far_ahead, open_face):
    positive = courant > 0.0
    upwind = jnp.where(positive, near_back, near_ahead)
    side_diff = jnp.where(positive, near_back - far_back, far_ahead - near_ahead)
    limited = minmod(near_ahead - near_back, side_diff)
    magnitude = jnp.abs(courant)
    return (courant * upwind + 0.5 * magnitude * (1.0 - magnitude) * limited) * open_face


def advect(salinity, east_courant, eastern_face_open, north_courant, wet_cells):
    columns = salinity.shape[2]
    east_flux = face_flux(
        east_courant,
        salinity[:, :, 0 : columns - 3],
        salinity[:, :, 1 : columns - 2],
        salinity[:, :, 2 : columns - 1],
        salinity[:, :, 3:columns],
        eastern_face_open,
    )
    interior = salinity[:, :, 2 : columns - 2]
    zero_col = jnp.zeros_like(interior[..., :1])
    lower_cells = jnp.concatenate([zero_col, interior[..., :-1]], -1)
    upper_cells = jnp.concatenate([interior[..., 1:], zero_col], -1)
    upper_two = jnp.concatenate([interior[..., 2:], zero_col, zero_col], -1)
    wet_next = jnp.concatenate([wet_cells[:, 1:], jnp.zeros_like(wet_cells[:, :1])], -1)
    poleward_transport = face_flux(
        north_courant, lower_cells, interior, upper_cells, upper_two, wet_cells * wet_next
    )
    equatorward_transport = jnp.concatenate([zero_col, poleward_transport[..., :-1]], -1)
    return (
        interior
        - (east_flux[:, :, 1:] - east_flux[:, :, :-1])
        - (poleward_transport - equatorward_transport)
    )


def factor(diff_rates):
    levels = diff_rates.shape[1] + 1
    thomas_coefficients = []
    inverse_terms = []
    previous = None
    for level_index in range(levels):
        diagonal = jnp.ones_like(diff_rates[:, 0])
        if level_index > 0:
            diagonal = diagonal + diff_rates[:, level_index - 1]
        if level_index < levels - 1:
            diagonal = diagonal + diff_rates[:, level_index]
        if level_index > 0:
            diagonal = diagonal + diff_rates[:, level_index - 1] * previous
        inverse_den = 1.0 / diagonal
        inverse_terms.append(inverse_den)
        if level_index < levels - 1:
            previous = -diff_rates[:, level_index] * inverse_den
            thomas_coefficients.append(previous)
    return (diff_rates, thomas_coefficients, inverse_terms)


def solve_columns(values, tridiag_terms):
    diff_rates, thomas_coefficients, inverse_terms = tridiag_terms
    levels = values.shape[1]
    forward = [values[:, 0] * inverse_terms[0]]
    for level_index in range(1, levels):
        forward.append(
            (values[:, level_index] + diff_rates[:, level_index - 1] * forward[-1])
            * inverse_terms[level_index]
        )
    solution = [None] * levels
    solution[levels - 1] = forward[levels - 1]
    for level_index in range(levels - 2, -1, -1):
        solution[level_index] = (
            forward[level_index] - thomas_coefficients[level_index] * solution[level_index + 1]
        )
    return jnp.stack(solution, 1)


def per_device(members, control, u_courant, v_courant, diffusion, group_scale, group_of, wet):
    levels = members.shape[1]
    columns = members.shape[2]
    realisation_total = members.shape[0] * lax.axis_size("mem")
    group_ids = jnp.arange(group_scale.shape[0], dtype=jnp.int32)
    spread_multiplier = jnp.sum(
        jnp.where(group_of[:, None] == group_ids[None, :], group_scale[None, :], 0.0), 1
    )
    wet_float = wet.astype(jnp.float32)
    member_total, u_low, wet_low, wet_high = member_allreduce(members, u_courant, wet)
    recentre_shift = control - member_total / realisation_total
    salinity = members + recentre_shift[None]
    east_courant = jnp.concatenate([u_low[:, None], u_courant], 1)
    wet_ext = jnp.concatenate([wet_low, wet, wet_high], 0).astype(jnp.float32)
    eastern_face_open = wet_ext[0 : columns + 1] * wet_ext[1 : columns + 2]
    tridiag_terms = factor(spread_multiplier[:, None, None, None] * diffusion[None])
    for time_step_index in range(2):
        padded = with_halo(salinity, (("tile", 2),), 2)
        salinity = solve_columns(
            advect(padded, east_courant, eastern_face_open, v_courant, wet_float), tridiag_terms
        )
    return salinity


def solution(mesh):
    placed = (
        P("mem", None, "tile", None),
        P(None, "tile", None),
        P(None, "tile", None),
        P(None, "tile", None),
        P(None, "tile", None),
        P(),
        P("mem"),
        P("tile", None),
    )
    return jax.shard_map(
        per_device,
        mesh=mesh,
        in_specs=placed,
        out_specs=P("mem", None, "tile", None),
        check_vma=False,
    )
```

```python
import functools

import jax
import jax.numpy as jnp
from jax import lax
from jax.experimental import pallas as pl
from jax.experimental.pallas import tpu as pltpu
from jax.sharding import PartitionSpec as P

MESH_ID = pl.DeviceIdType.MESH


def allreduce_kernel(
    n, members_ref, u_ref, wet_ref, o_ref, ulow_ref, wlow_ref, whigh_ref,
    x_ref, recv, red, gath, uedge, wedge, ubuf, wbuf, s1, r1, s2, r2, se, re,
):
    me = lax.axis_index("mem")
    tile = lax.axis_index("tile")
    tiles = lax.axis_size("tile")
    has_left = tile > 0
    has_right = tile < tiles - 1
    rows = x_ref.shape[0] // n
    columns = u_ref.shape[1]
    peers = [lax.rem(me + d, n) for d in range(1, n)]
    barrier = pltpu.get_barrier_semaphore()
    for peer in peers:
        pl.semaphore_signal(barrier, inc=1, device_id=(tile, peer), device_id_type=MESH_ID)

    @pl.when(has_left)
    def _():
        pl.semaphore_signal(barrier, inc=1, device_id=(tile - 1, me), device_id_type=MESH_ID)

    @pl.when(has_right)
    def _():
        pl.semaphore_signal(barrier, inc=1, device_id=(tile + 1, me), device_id_type=MESH_ID)

    uedge[...] = u_ref[:, columns - 1, :]
    wedge[0] = wet_ref[pl.ds(columns - 1, 1), :]
    wedge[1] = wet_ref[pl.ds(0, 1), :]

    def local_sum(k, carry):
        level = members_ref[0, k]
        for m in range(1, members_ref.shape[0]):
            level = level + members_ref[m, k]
        x_ref[k] = level
        return carry

    lax.fori_loop(0, x_ref.shape[0], local_sum, 0)
    pl.semaphore_wait(
        barrier, n - 1 + has_left.astype(jnp.int32) + has_right.astype(jnp.int32)
    )

    def copy_to(src, dst, send, recv_sem, device):
        return pltpu.make_async_remote_copy(
            src_ref=src,
            dst_ref=dst,
            send_sem=send,
            recv_sem=recv_sem,
            device_id=device,
            device_id_type=MESH_ID,
        )

    right_copies = [
        copy_to(uedge, ubuf, se.at[0], re.at[0], (tile + 1, me)),
        copy_to(wedge.at[0], wbuf.at[0], se.at[1], re.at[1], (tile + 1, me)),
    ]
    left_copy = copy_to(wedge.at[1], wbuf.at[1], se.at[2], re.at[2], (tile - 1, me))

    @pl.when(has_right)
    def _():
        for copy in right_copies:
            copy.start()

    @pl.when(has_left)
    def _():
        left_copy.start()

    firsts = [
        copy_to(x_ref.at[pl.ds(peer * rows, rows)], recv.at[me], s1.at[peer], r1.at[me], (tile, peer))
        for peer in peers
    ]
    for copy in firsts:
        copy.start()
    for peer in peers:
        copy_to(x_ref.at[pl.ds(0, rows)], recv.at[peer], s1.at[peer], r1.at[peer], (tile, peer)).wait_recv()
    acc = x_ref[pl.ds(me * rows, rows)]
    for peer in peers:
        acc = acc + recv[peer]
    red[...] = acc
    o_ref[pl.ds(me * rows, rows)] = acc
    seconds = [copy_to(red, gath.at[me], s2.at[peer], r2.at[me], (tile, peer)) for peer in peers]
    for copy in seconds:
        copy.start()
    for peer in peers:
        copy_to(red, gath.at[peer], s2.at[peer], r2.at[peer], (tile, peer)).wait_recv()
        o_ref[pl.ds(peer * rows, rows)] = gath[peer]
    for copy in firsts + seconds:
        copy.wait_send()

    @pl.when(has_right)
    def _():
        for copy in right_copies:
            copy.wait_send()

    @pl.when(has_left)
    def _():
        left_copy.wait_send()
        for copy in right_copies:
            copy.wait_recv()
        ulow_ref[...] = ubuf[...]
        wlow_ref[...] = wbuf[0]

    @pl.when(jnp.logical_not(has_left))
    def _():
        ulow_ref[...] = jnp.zeros_like(ulow_ref)
        wlow_ref[...] = jnp.zeros_like(wlow_ref)

    @pl.when(has_right)
    def _():
        left_copy.wait_recv()
        whigh_ref[...] = wbuf[1]

    @pl.when(jnp.logical_not(has_right))
    def _():
        whigh_ref[...] = jnp.zeros_like(whigh_ref)


def member_allreduce(members, u_courant, wet):
    total = jax.ShapeDtypeStruct(members.shape[1:], members.dtype)
    n = lax.axis_size("mem")
    rows = total.shape[0] // n
    chunk = (rows,) + total.shape[1:]
    levels, lanes = u_courant.shape[0], u_courant.shape[2]
    vmem = pl.BlockSpec(memory_space=pltpu.VMEM)
    return pl.pallas_call(
        functools.partial(allreduce_kernel, n),
        out_shape=(
            jax.ShapeDtypeStruct(total.shape, total.dtype),
            jax.ShapeDtypeStruct((levels, lanes), u_courant.dtype),
            jax.ShapeDtypeStruct((1, lanes), wet.dtype),
            jax.ShapeDtypeStruct((1, lanes), wet.dtype),
        ),
        in_specs=[vmem] * 3,
        out_specs=(vmem,) * 4,
        scratch_shapes=[
            pltpu.VMEM(total.shape, total.dtype),
            pltpu.VMEM((n,) + chunk, total.dtype),
            pltpu.VMEM(chunk, total.dtype),
            pltpu.VMEM((n,) + chunk, total.dtype),
            pltpu.VMEM((levels, lanes), u_courant.dtype),
            pltpu.VMEM((2, 1, lanes), wet.dtype),
            pltpu.VMEM((levels, lanes), u_courant.dtype),
            pltpu.VMEM((2, 1, lanes), wet.dtype),
            pltpu.SemaphoreType.DMA((n,)),
            pltpu.SemaphoreType.DMA((n,)),
            pltpu.SemaphoreType.DMA((n,)),
            pltpu.SemaphoreType.DMA((n,)),
            pltpu.SemaphoreType.DMA((3,)),
            pltpu.SemaphoreType.DMA((3,)),
        ],
        compiler_params=pltpu.CompilerParams(collective_id=0, has_side_effects=True),
    )(members, u_courant, wet)


def halo_kernel(lo_ref, hi_ref, low_ref, high_ref, lo_buf, hi_buf, se, re):
    me = lax.axis_index("mem")
    tile = lax.axis_index("tile")
    tiles = lax.axis_size("tile")
    has_left = tile > 0
    has_right = tile < tiles - 1
    barrier = pltpu.get_barrier_semaphore()

    @pl.when(has_left)
    def _():
        pl.semaphore_signal(barrier, inc=1, device_id=(tile - 1, me), device_id_type=MESH_ID)

    @pl.when(has_right)
    def _():
        pl.semaphore_signal(barrier, inc=1, device_id=(tile + 1, me), device_id_type=MESH_ID)

    pl.semaphore_wait(barrier, has_left.astype(jnp.int32) + has_right.astype(jnp.int32))
    to_right = pltpu.make_async_remote_copy(
        src_ref=lo_ref, dst_ref=lo_buf, send_sem=se.at[0], recv_sem=re.at[0],
        device_id=(tile + 1, me), device_id_type=MESH_ID,
    )
    to_left = pltpu.make_async_remote_copy(
        src_ref=hi_ref, dst_ref=hi_buf, send_sem=se.at[1], recv_sem=re.at[1],
        device_id=(tile - 1, me), device_id_type=MESH_ID,
    )

    @pl.when(has_right)
    def _():
        to_right.start()

    @pl.when(has_left)
    def _():
        to_left.start()

    @pl.when(has_right)
    def _():
        to_right.wait_send()

    @pl.when(has_left)
    def _():
        to_left.wait_send()
        to_right.wait_recv()
        low_ref[...] = lo_buf[...]

    @pl.when(jnp.logical_not(has_left))
    def _():
        low_ref[...] = jnp.zeros_like(low_ref)

    @pl.when(has_right)
    def _():
        to_left.wait_recv()
        high_ref[...] = hi_buf[...]

    @pl.when(jnp.logical_not(has_right))
    def _():
        high_ref[...] = jnp.zeros_like(high_ref)


def halo_pad(block, width, collective):
    columns = block.shape[2]
    lo = block[:, :, columns - width :]
    hi = block[:, :, :width]
    vmem = pl.BlockSpec(memory_space=pltpu.VMEM)
    edge = jax.ShapeDtypeStruct(lo.shape, lo.dtype)
    low, high = pl.pallas_call(
        halo_kernel,
        out_shape=(edge, edge),
        in_specs=[vmem, vmem],
        out_specs=(vmem, vmem),
        scratch_shapes=[
            pltpu.VMEM(lo.shape, lo.dtype),
            pltpu.VMEM(lo.shape, lo.dtype),
            pltpu.SemaphoreType.DMA((2,)),
            pltpu.SemaphoreType.DMA((2,)),
        ],
        compiler_params=pltpu.CompilerParams(collective_id=collective, has_side_effects=True),
    )(lo, hi)
    return jnp.concatenate([low, block, high], 2)


def with_halo(block, sides, width):
    for axis, dim in sides:
        count = lax.axis_size(axis)
        forward = [(i, i + 1) for i in range(count - 1)]
        backward = [(target, source) for source, target in forward]
        low = lax.ppermute(
            lax.slice_in_dim(block, block.shape[dim] - width, None, axis=dim), axis, forward
        )
        high = lax.ppermute(lax.slice_in_dim(block, 0, width, axis=dim), axis, backward)
        block = jnp.concatenate([low, block, high], axis=dim)
    return block


def minmod(first_diff, second_diff):
    return (
        0.5
        * (jnp.sign(first_diff) + jnp.sign(second_diff))
        * jnp.minimum(jnp.abs(first_diff), jnp.abs(second_diff))
    )


def face_flux(courant, far_back, near_back, near_ahead, far_ahead, open_face):
    positive = courant > 0.0
    upwind = jnp.where(positive, near_back, near_ahead)
    side_diff = jnp.where(positive, near_back - far_back, far_ahead - near_ahead)
    limited = minmod(near_ahead - near_back, side_diff)
    magnitude = jnp.abs(courant)
    return (courant * upwind + 0.5 * magnitude * (1.0 - magnitude) * limited) * open_face


def advect(salinity, east_courant, eastern_face_open, north_courant, wet_cells):
    columns = salinity.shape[2]
    east_flux = face_flux(
        east_courant,
        salinity[:, :, 0 : columns - 3],
        salinity[:, :, 1 : columns - 2],
        salinity[:, :, 2 : columns - 1],
        salinity[:, :, 3:columns],
        eastern_face_open,
    )
    interior = salinity[:, :, 2 : columns - 2]
    zero_col = jnp.zeros_like(interior[..., :1])
    lower_cells = jnp.concatenate([zero_col, interior[..., :-1]], -1)
    upper_cells = jnp.concatenate([interior[..., 1:], zero_col], -1)
    upper_two = jnp.concatenate([interior[..., 2:], zero_col, zero_col], -1)
    wet_next = jnp.concatenate([wet_cells[:, 1:], jnp.zeros_like(wet_cells[:, :1])], -1)
    poleward_transport = face_flux(
        north_courant, lower_cells, interior, upper_cells, upper_two, wet_cells * wet_next
    )
    equatorward_transport = jnp.concatenate([zero_col, poleward_transport[..., :-1]], -1)
    return (
        interior
        - (east_flux[:, :, 1:] - east_flux[:, :, :-1])
        - (poleward_transport - equatorward_transport)
    )


def factor(diff_rates):
    levels = diff_rates.shape[1] + 1
    thomas_coefficients = []
    inverse_terms = []
    previous = None
    for level_index in range(levels):
        diagonal = jnp.ones_like(diff_rates[:, 0])
        if level_index > 0:
            diagonal = diagonal + diff_rates[:, level_index - 1]
        if level_index < levels - 1:
            diagonal = diagonal + diff_rates[:, level_index]
        if level_index > 0:
            diagonal = diagonal + diff_rates[:, level_index - 1] * previous
        inverse_den = 1.0 / diagonal
        inverse_terms.append(inverse_den)
        if level_index < levels - 1:
            previous = -diff_rates[:, level_index] * inverse_den
            thomas_coefficients.append(previous)
    return (diff_rates, thomas_coefficients, inverse_terms)


def solve_columns(values, tridiag_terms):
    diff_rates, thomas_coefficients, inverse_terms = tridiag_terms
    levels = values.shape[1]
    forward = [values[:, 0] * inverse_terms[0]]
    for level_index in range(1, levels):
        forward.append(
            (values[:, level_index] + diff_rates[:, level_index - 1] * forward[-1])
            * inverse_terms[level_index]
        )
    solution = [None] * levels
    solution[levels - 1] = forward[levels - 1]
    for level_index in range(levels - 2, -1, -1):
        solution[level_index] = (
            forward[level_index] - thomas_coefficients[level_index] * solution[level_index + 1]
        )
    return jnp.stack(solution, 1)


def per_device(members, control, u_courant, v_courant, diffusion, group_scale, group_of, wet):
    levels = members.shape[1]
    columns = members.shape[2]
    realisation_total = members.shape[0] * lax.axis_size("mem")
    group_ids = jnp.arange(group_scale.shape[0], dtype=jnp.int32)
    spread_multiplier = jnp.sum(
        jnp.where(group_of[:, None] == group_ids[None, :], group_scale[None, :], 0.0), 1
    )
    wet_float = wet.astype(jnp.float32)
    member_total, u_low, wet_low, wet_high = member_allreduce(members, u_courant, wet)
    recentre_shift = control - member_total / realisation_total
    salinity = members + recentre_shift[None]
    east_courant = jnp.concatenate([u_low[:, None], u_courant], 1)
    wet_ext = jnp.concatenate([wet_low, wet, wet_high], 0).astype(jnp.float32)
    eastern_face_open = wet_ext[0 : columns + 1] * wet_ext[1 : columns + 2]
    tridiag_terms = factor(spread_multiplier[:, None, None, None] * diffusion[None])
    for time_step_index in range(2):
        padded = halo_pad(salinity, 2, 1 + time_step_index)
        salinity = solve_columns(
            advect(padded, east_courant, eastern_face_open, v_courant, wet_float), tridiag_terms
        )
    return salinity


def solution(mesh):
    placed = (
        P("mem", None, "tile", None),
        P(None, "tile", None),
        P(None, "tile", None),
        P(None, "tile", None),
        P(None, "tile", None),
        P(),
        P("mem"),
        P("tile", None),
    )
    return jax.shard_map(
        per_device,
        mesh=mesh,
        in_specs=placed,
        out_specs=P("mem", None, "tile", None),
        check_vma=False,
    )
```

```python
import functools

import jax
import jax.numpy as jnp
from jax import lax
from jax.experimental import pallas as pl
from jax.experimental.pallas import tpu as pltpu
from jax.sharding import PartitionSpec as P

MESH_ID = pl.DeviceIdType.MESH


def allreduce_kernel(
    n, members_ref, u_ref, wet_ref, c_ref, o_ref, ulow_ref, wlow_ref, whigh_ref,
    x_ref, recv, red, gath, uedge, wedge, ubuf, wbuf, s1, r1, s2, r2, se, re,
):
    me = lax.axis_index("mem")
    tile = lax.axis_index("tile")
    tiles = lax.axis_size("tile")
    has_left = tile > 0
    has_right = tile < tiles - 1
    rows = x_ref.shape[0] // n
    columns = u_ref.shape[1]
    peers = [lax.rem(me + d, n) for d in range(1, n)]
    barrier = pltpu.get_barrier_semaphore()
    for peer in peers:
        pl.semaphore_signal(barrier, inc=1, device_id=(tile, peer), device_id_type=MESH_ID)

    @pl.when(has_left)
    def _():
        pl.semaphore_signal(barrier, inc=1, device_id=(tile - 1, me), device_id_type=MESH_ID)

    @pl.when(has_right)
    def _():
        pl.semaphore_signal(barrier, inc=1, device_id=(tile + 1, me), device_id_type=MESH_ID)

    uedge[...] = u_ref[:, columns - 1, :]
    wedge[0] = wet_ref[pl.ds(columns - 1, 1), :]
    wedge[1] = wet_ref[pl.ds(0, 1), :]

    def local_sum(k, carry):
        level = members_ref[0, k]
        for m in range(1, members_ref.shape[0]):
            level = level + members_ref[m, k]
        x_ref[k] = level
        return carry

    lax.fori_loop(0, x_ref.shape[0], local_sum, 0)
    pl.semaphore_wait(
        barrier, n - 1 + has_left.astype(jnp.int32) + has_right.astype(jnp.int32)
    )

    def copy_to(src, dst, send, recv_sem, device):
        return pltpu.make_async_remote_copy(
            src_ref=src,
            dst_ref=dst,
            send_sem=send,
            recv_sem=recv_sem,
            device_id=device,
            device_id_type=MESH_ID,
        )

    right_copies = [
        copy_to(uedge, ubuf, se.at[0], re.at[0], (tile + 1, me)),
        copy_to(wedge.at[0], wbuf.at[0], se.at[1], re.at[1], (tile + 1, me)),
    ]
    left_copy = copy_to(wedge.at[1], wbuf.at[1], se.at[2], re.at[2], (tile - 1, me))

    @pl.when(has_right)
    def _():
        for copy in right_copies:
            copy.start()

    @pl.when(has_left)
    def _():
        left_copy.start()

    firsts = [
        copy_to(x_ref.at[pl.ds(peer * rows, rows)], recv.at[me], s1.at[peer], r1.at[me], (tile, peer))
        for peer in peers
    ]
    for copy in firsts:
        copy.start()
    for peer in peers:
        copy_to(x_ref.at[pl.ds(0, rows)], recv.at[peer], s1.at[peer], r1.at[peer], (tile, peer)).wait_recv()
    acc = x_ref[pl.ds(me * rows, rows)]
    for peer in peers:
        acc = acc + recv[peer]
    red[...] = acc
    scale = 1.0 / (n * members_ref.shape[0])
    own = pl.ds(me * rows, rows)
    o_ref[own] = c_ref[own] - acc * scale
    seconds = [copy_to(red, gath.at[me], s2.at[peer], r2.at[me], (tile, peer)) for peer in peers]
    for copy in seconds:
        copy.start()
    for peer in peers:
        copy_to(red, gath.at[peer], s2.at[peer], r2.at[peer], (tile, peer)).wait_recv()
        part = pl.ds(peer * rows, rows)
        o_ref[part] = c_ref[part] - gath[peer] * scale
    for copy in firsts + seconds:
        copy.wait_send()

    @pl.when(has_right)
    def _():
        for copy in right_copies:
            copy.wait_send()

    @pl.when(has_left)
    def _():
        left_copy.wait_send()
        for copy in right_copies:
            copy.wait_recv()
        ulow_ref[...] = ubuf[...]
        wlow_ref[...] = wbuf[0]

    @pl.when(jnp.logical_not(has_left))
    def _():
        ulow_ref[...] = jnp.zeros_like(ulow_ref)
        wlow_ref[...] = jnp.zeros_like(wlow_ref)

    @pl.when(has_right)
    def _():
        left_copy.wait_recv()
        whigh_ref[...] = wbuf[1]

    @pl.when(jnp.logical_not(has_right))
    def _():
        whigh_ref[...] = jnp.zeros_like(whigh_ref)


def member_allreduce(members, u_courant, wet, control):
    total = jax.ShapeDtypeStruct(members.shape[1:], members.dtype)
    n = lax.axis_size("mem")
    rows = total.shape[0] // n
    chunk = (rows,) + total.shape[1:]
    levels, lanes = u_courant.shape[0], u_courant.shape[2]
    vmem = pl.BlockSpec(memory_space=pltpu.VMEM)
    return pl.pallas_call(
        functools.partial(allreduce_kernel, n),
        out_shape=(
            jax.ShapeDtypeStruct(total.shape, total.dtype),
            jax.ShapeDtypeStruct((levels, lanes), u_courant.dtype),
            jax.ShapeDtypeStruct((1, lanes), wet.dtype),
            jax.ShapeDtypeStruct((1, lanes), wet.dtype),
        ),
        in_specs=[vmem] * 4,
        out_specs=(vmem,) * 4,
        scratch_shapes=[
            pltpu.VMEM(total.shape, total.dtype),
            pltpu.VMEM((n,) + chunk, total.dtype),
            pltpu.VMEM(chunk, total.dtype),
            pltpu.VMEM((n,) + chunk, total.dtype),
            pltpu.VMEM((levels, lanes), u_courant.dtype),
            pltpu.VMEM((2, 1, lanes), wet.dtype),
            pltpu.VMEM((levels, lanes), u_courant.dtype),
            pltpu.VMEM((2, 1, lanes), wet.dtype),
            pltpu.SemaphoreType.DMA((n,)),
            pltpu.SemaphoreType.DMA((n,)),
            pltpu.SemaphoreType.DMA((n,)),
            pltpu.SemaphoreType.DMA((n,)),
            pltpu.SemaphoreType.DMA((3,)),
            pltpu.SemaphoreType.DMA((3,)),
        ],
        compiler_params=pltpu.CompilerParams(collective_id=0, has_side_effects=True),
    )(members, u_courant, wet, control)


def with_halo(block, sides, width):
    for axis, dim in sides:
        count = lax.axis_size(axis)
        forward = [(i, i + 1) for i in range(count - 1)]
        backward = [(target, source) for source, target in forward]
        low = lax.ppermute(
            lax.slice_in_dim(block, block.shape[dim] - width, None, axis=dim), axis, forward
        )
        high = lax.ppermute(lax.slice_in_dim(block, 0, width, axis=dim), axis, backward)
        block = jnp.concatenate([low, block, high], axis=dim)
    return block


def minmod(first_diff, second_diff):
    return (
        0.5
        * (jnp.sign(first_diff) + jnp.sign(second_diff))
        * jnp.minimum(jnp.abs(first_diff), jnp.abs(second_diff))
    )


def face_flux(courant, far_back, near_back, near_ahead, far_ahead, open_face):
    positive = courant > 0.0
    upwind = jnp.where(positive, near_back, near_ahead)
    side_diff = jnp.where(positive, near_back - far_back, far_ahead - near_ahead)
    limited = minmod(near_ahead - near_back, side_diff)
    magnitude = jnp.abs(courant)
    return (courant * upwind + 0.5 * magnitude * (1.0 - magnitude) * limited) * open_face


def advect(salinity, east_courant, eastern_face_open, north_courant, wet_cells):
    columns = salinity.shape[2]
    east_flux = face_flux(
        east_courant,
        salinity[:, :, 0 : columns - 3],
        salinity[:, :, 1 : columns - 2],
        salinity[:, :, 2 : columns - 1],
        salinity[:, :, 3:columns],
        eastern_face_open,
    )
    interior = salinity[:, :, 2 : columns - 2]
    zero_col = jnp.zeros_like(interior[..., :1])
    lower_cells = jnp.concatenate([zero_col, interior[..., :-1]], -1)
    upper_cells = jnp.concatenate([interior[..., 1:], zero_col], -1)
    upper_two = jnp.concatenate([interior[..., 2:], zero_col, zero_col], -1)
    wet_next = jnp.concatenate([wet_cells[:, 1:], jnp.zeros_like(wet_cells[:, :1])], -1)
    poleward_transport = face_flux(
        north_courant, lower_cells, interior, upper_cells, upper_two, wet_cells * wet_next
    )
    equatorward_transport = jnp.concatenate([zero_col, poleward_transport[..., :-1]], -1)
    return (
        interior
        - (east_flux[:, :, 1:] - east_flux[:, :, :-1])
        - (poleward_transport - equatorward_transport)
    )


def factor(diff_rates):
    levels = diff_rates.shape[1] + 1
    thomas_coefficients = []
    inverse_terms = []
    previous = None
    for level_index in range(levels):
        diagonal = jnp.ones_like(diff_rates[:, 0])
        if level_index > 0:
            diagonal = diagonal + diff_rates[:, level_index - 1]
        if level_index < levels - 1:
            diagonal = diagonal + diff_rates[:, level_index]
        if level_index > 0:
            diagonal = diagonal + diff_rates[:, level_index - 1] * previous
        inverse_den = 1.0 / diagonal
        inverse_terms.append(inverse_den)
        if level_index < levels - 1:
            previous = -diff_rates[:, level_index] * inverse_den
            thomas_coefficients.append(previous)
    return (diff_rates, thomas_coefficients, inverse_terms)


def solve_columns(values, tridiag_terms):
    diff_rates, thomas_coefficients, inverse_terms = tridiag_terms
    levels = values.shape[1]
    forward = [values[:, 0] * inverse_terms[0]]
    for level_index in range(1, levels):
        forward.append(
            (values[:, level_index] + diff_rates[:, level_index - 1] * forward[-1])
            * inverse_terms[level_index]
        )
    solution = [None] * levels
    solution[levels - 1] = forward[levels - 1]
    for level_index in range(levels - 2, -1, -1):
        solution[level_index] = (
            forward[level_index] - thomas_coefficients[level_index] * solution[level_index + 1]
        )
    return jnp.stack(solution, 1)


def per_device(members, control, u_courant, v_courant, diffusion, group_scale, group_of, wet):
    levels = members.shape[1]
    columns = members.shape[2]
    realisation_total = members.shape[0] * lax.axis_size("mem")
    group_ids = jnp.arange(group_scale.shape[0], dtype=jnp.int32)
    spread_multiplier = jnp.sum(
        jnp.where(group_of[:, None] == group_ids[None, :], group_scale[None, :], 0.0), 1
    )
    wet_float = wet.astype(jnp.float32)
    recentre_shift, u_low, wet_low, wet_high = member_allreduce(members, u_courant, wet, control)
    salinity = members + recentre_shift[None]
    east_courant = jnp.concatenate([u_low[:, None], u_courant], 1)
    wet_ext = jnp.concatenate([wet_low, wet, wet_high], 0).astype(jnp.float32)
    eastern_face_open = wet_ext[0 : columns + 1] * wet_ext[1 : columns + 2]
    tridiag_terms = factor(spread_multiplier[:, None, None, None] * diffusion[None])
    for time_step_index in range(2):
        padded = with_halo(salinity, (("tile", 2),), 2)
        salinity = solve_columns(
            advect(padded, east_courant, eastern_face_open, v_courant, wet_float), tridiag_terms
        )
    return salinity


def solution(mesh):
    placed = (
        P("mem", None, "tile", None),
        P(None, "tile", None),
        P(None, "tile", None),
        P(None, "tile", None),
        P(None, "tile", None),
        P(),
        P("mem"),
        P("tile", None),
    )
    return jax.shard_map(
        per_device,
        mesh=mesh,
        in_specs=placed,
        out_specs=P("mem", None, "tile", None),
        check_vma=False,
    )
```

```python
import functools

import jax
import jax.numpy as jnp
from jax import lax
from jax.experimental import pallas as pl
from jax.experimental.pallas import tpu as pltpu
from jax.sharding import PartitionSpec as P

MESH_ID = pl.DeviceIdType.MESH


def allreduce_kernel(
    n, members_ref, u_ref, wet_ref, c_ref, o_ref, ulow_ref, wlow_ref, whigh_ref,
    x_ref, recv, red, gath, uedge, wedge, ubuf, wbuf, s1, r1, s2, r2, se, re,
):
    me = lax.axis_index("mem")
    tile = lax.axis_index("tile")
    tiles = lax.axis_size("tile")
    has_left = tile > 0
    has_right = tile < tiles - 1
    rows = x_ref.shape[0] // n
    columns = u_ref.shape[1]
    half = n // 2
    ring_y, ring_z = me // 2, lax.rem(me, 2)
    offsets = [(2, 1), (2, 0), (1, 1), (3, 1), (1, 0), (3, 0), (0, 1)]
    peers = [lax.rem(ring_y + dy, half) * 2 + lax.rem(ring_z + dz, 2) for dy, dz in offsets]
    barrier = pltpu.get_barrier_semaphore()
    for peer in peers:
        pl.semaphore_signal(barrier, inc=1, device_id=(tile, peer), device_id_type=MESH_ID)

    @pl.when(has_left)
    def _():
        pl.semaphore_signal(barrier, inc=1, device_id=(tile - 1, me), device_id_type=MESH_ID)

    @pl.when(has_right)
    def _():
        pl.semaphore_signal(barrier, inc=1, device_id=(tile + 1, me), device_id_type=MESH_ID)

    uedge[...] = u_ref[:, columns - 1, :]
    wedge[0] = wet_ref[pl.ds(columns - 1, 1), :]
    wedge[1] = wet_ref[pl.ds(0, 1), :]

    def local_sum(k, carry):
        level = members_ref[0, k]
        for m in range(1, members_ref.shape[0]):
            level = level + members_ref[m, k]
        x_ref[k] = level
        return carry

    lax.fori_loop(0, x_ref.shape[0], local_sum, 0)
    pl.semaphore_wait(
        barrier, n - 1 + has_left.astype(jnp.int32) + has_right.astype(jnp.int32)
    )

    def copy_to(src, dst, send, recv_sem, device):
        return pltpu.make_async_remote_copy(
            src_ref=src,
            dst_ref=dst,
            send_sem=send,
            recv_sem=recv_sem,
            device_id=device,
            device_id_type=MESH_ID,
        )

    right_copies = [
        copy_to(uedge, ubuf, se.at[0], re.at[0], (tile + 1, me)),
        copy_to(wedge.at[0], wbuf.at[0], se.at[1], re.at[1], (tile + 1, me)),
    ]
    left_copy = copy_to(wedge.at[1], wbuf.at[1], se.at[2], re.at[2], (tile - 1, me))

    @pl.when(has_right)
    def _():
        for copy in right_copies:
            copy.start()

    @pl.when(has_left)
    def _():
        left_copy.start()

    firsts = [
        copy_to(x_ref.at[pl.ds(peer * rows, rows)], recv.at[me], s1.at[peer], r1.at[me], (tile, peer))
        for peer in peers
    ]
    for copy in firsts:
        copy.start()
    for peer in peers:
        copy_to(x_ref.at[pl.ds(0, rows)], recv.at[peer], s1.at[peer], r1.at[peer], (tile, peer)).wait_recv()
    acc = x_ref[pl.ds(me * rows, rows)]
    for peer in peers:
        acc = acc + recv[peer]
    red[...] = acc
    scale = 1.0 / (n * members_ref.shape[0])
    own = pl.ds(me * rows, rows)
    o_ref[own] = c_ref[own] - acc * scale
    seconds = [copy_to(red, gath.at[me], s2.at[peer], r2.at[me], (tile, peer)) for peer in peers]
    for copy in seconds:
        copy.start()
    for peer in peers:
        copy_to(red, gath.at[peer], s2.at[peer], r2.at[peer], (tile, peer)).wait_recv()
        part = pl.ds(peer * rows, rows)
        o_ref[part] = c_ref[part] - gath[peer] * scale
    for copy in firsts + seconds:
        copy.wait_send()

    @pl.when(has_right)
    def _():
        for copy in right_copies:
            copy.wait_send()

    @pl.when(has_left)
    def _():
        left_copy.wait_send()
        for copy in right_copies:
            copy.wait_recv()
        ulow_ref[...] = ubuf[...]
        wlow_ref[...] = wbuf[0]

    @pl.when(jnp.logical_not(has_left))
    def _():
        ulow_ref[...] = jnp.zeros_like(ulow_ref)
        wlow_ref[...] = jnp.zeros_like(wlow_ref)

    @pl.when(has_right)
    def _():
        left_copy.wait_recv()
        whigh_ref[...] = wbuf[1]

    @pl.when(jnp.logical_not(has_right))
    def _():
        whigh_ref[...] = jnp.zeros_like(whigh_ref)


def member_allreduce(members, u_courant, wet, control):
    total = jax.ShapeDtypeStruct(members.shape[1:], members.dtype)
    n = lax.axis_size("mem")
    rows = total.shape[0] // n
    chunk = (rows,) + total.shape[1:]
    levels, lanes = u_courant.shape[0], u_courant.shape[2]
    vmem = pl.BlockSpec(memory_space=pltpu.VMEM)
    return pl.pallas_call(
        functools.partial(allreduce_kernel, n),
        out_shape=(
            jax.ShapeDtypeStruct(total.shape, total.dtype),
            jax.ShapeDtypeStruct((levels, lanes), u_courant.dtype),
            jax.ShapeDtypeStruct((1, lanes), wet.dtype),
            jax.ShapeDtypeStruct((1, lanes), wet.dtype),
        ),
        in_specs=[vmem] * 4,
        out_specs=(vmem,) * 4,
        scratch_shapes=[
            pltpu.VMEM(total.shape, total.dtype),
            pltpu.VMEM((n,) + chunk, total.dtype),
            pltpu.VMEM(chunk, total.dtype),
            pltpu.VMEM((n,) + chunk, total.dtype),
            pltpu.VMEM((levels, lanes), u_courant.dtype),
            pltpu.VMEM((2, 1, lanes), wet.dtype),
            pltpu.VMEM((levels, lanes), u_courant.dtype),
            pltpu.VMEM((2, 1, lanes), wet.dtype),
            pltpu.SemaphoreType.DMA((n,)),
            pltpu.SemaphoreType.DMA((n,)),
            pltpu.SemaphoreType.DMA((n,)),
            pltpu.SemaphoreType.DMA((n,)),
            pltpu.SemaphoreType.DMA((3,)),
            pltpu.SemaphoreType.DMA((3,)),
        ],
        compiler_params=pltpu.CompilerParams(collective_id=0, has_side_effects=True),
    )(members, u_courant, wet, control)


def with_halo(block, sides, width):
    for axis, dim in sides:
        count = lax.axis_size(axis)
        forward = [(i, i + 1) for i in range(count - 1)]
        backward = [(target, source) for source, target in forward]
        low = lax.ppermute(
            lax.slice_in_dim(block, block.shape[dim] - width, None, axis=dim), axis, forward
        )
        high = lax.ppermute(lax.slice_in_dim(block, 0, width, axis=dim), axis, backward)
        block = jnp.concatenate([low, block, high], axis=dim)
    return block


def minmod(first_diff, second_diff):
    return (
        0.5
        * (jnp.sign(first_diff) + jnp.sign(second_diff))
        * jnp.minimum(jnp.abs(first_diff), jnp.abs(second_diff))
    )


def face_flux(courant, far_back, near_back, near_ahead, far_ahead, open_face):
    positive = courant > 0.0
    upwind = jnp.where(positive, near_back, near_ahead)
    side_diff = jnp.where(positive, near_back - far_back, far_ahead - near_ahead)
    limited = minmod(near_ahead - near_back, side_diff)
    magnitude = jnp.abs(courant)
    return (courant * upwind + 0.5 * magnitude * (1.0 - magnitude) * limited) * open_face


def advect(salinity, east_courant, eastern_face_open, north_courant, wet_cells):
    columns = salinity.shape[2]
    east_flux = face_flux(
        east_courant,
        salinity[:, :, 0 : columns - 3],
        salinity[:, :, 1 : columns - 2],
        salinity[:, :, 2 : columns - 1],
        salinity[:, :, 3:columns],
        eastern_face_open,
    )
    interior = salinity[:, :, 2 : columns - 2]
    zero_col = jnp.zeros_like(interior[..., :1])
    lower_cells = jnp.concatenate([zero_col, interior[..., :-1]], -1)
    upper_cells = jnp.concatenate([interior[..., 1:], zero_col], -1)
    upper_two = jnp.concatenate([interior[..., 2:], zero_col, zero_col], -1)
    wet_next = jnp.concatenate([wet_cells[:, 1:], jnp.zeros_like(wet_cells[:, :1])], -1)
    poleward_transport = face_flux(
        north_courant, lower_cells, interior, upper_cells, upper_two, wet_cells * wet_next
    )
    equatorward_transport = jnp.concatenate([zero_col, poleward_transport[..., :-1]], -1)
    return (
        interior
        - (east_flux[:, :, 1:] - east_flux[:, :, :-1])
        - (poleward_transport - equatorward_transport)
    )


def factor(diff_rates):
    levels = diff_rates.shape[1] + 1
    thomas_coefficients = []
    inverse_terms = []
    previous = None
    for level_index in range(levels):
        diagonal = jnp.ones_like(diff_rates[:, 0])
        if level_index > 0:
            diagonal = diagonal + diff_rates[:, level_index - 1]
        if level_index < levels - 1:
            diagonal = diagonal + diff_rates[:, level_index]
        if level_index > 0:
            diagonal = diagonal + diff_rates[:, level_index - 1] * previous
        inverse_den = 1.0 / diagonal
        inverse_terms.append(inverse_den)
        if level_index < levels - 1:
            previous = -diff_rates[:, level_index] * inverse_den
            thomas_coefficients.append(previous)
    return (diff_rates, thomas_coefficients, inverse_terms)


def solve_columns(values, tridiag_terms):
    diff_rates, thomas_coefficients, inverse_terms = tridiag_terms
    levels = values.shape[1]
    forward = [values[:, 0] * inverse_terms[0]]
    for level_index in range(1, levels):
        forward.append(
            (values[:, level_index] + diff_rates[:, level_index - 1] * forward[-1])
            * inverse_terms[level_index]
        )
    solution = [None] * levels
    solution[levels - 1] = forward[levels - 1]
    for level_index in range(levels - 2, -1, -1):
        solution[level_index] = (
            forward[level_index] - thomas_coefficients[level_index] * solution[level_index + 1]
        )
    return jnp.stack(solution, 1)


def per_device(members, control, u_courant, v_courant, diffusion, group_scale, group_of, wet):
    levels = members.shape[1]
    columns = members.shape[2]
    realisation_total = members.shape[0] * lax.axis_size("mem")
    group_ids = jnp.arange(group_scale.shape[0], dtype=jnp.int32)
    spread_multiplier = jnp.sum(
        jnp.where(group_of[:, None] == group_ids[None, :], group_scale[None, :], 0.0), 1
    )
    wet_float = wet.astype(jnp.float32)
    recentre_shift, u_low, wet_low, wet_high = member_allreduce(members, u_courant, wet, control)
    salinity = members + recentre_shift[None]
    east_courant = jnp.concatenate([u_low[:, None], u_courant], 1)
    wet_ext = jnp.concatenate([wet_low, wet, wet_high], 0).astype(jnp.float32)
    eastern_face_open = wet_ext[0 : columns + 1] * wet_ext[1 : columns + 2]
    tridiag_terms = factor(spread_multiplier[:, None, None, None] * diffusion[None])
    for time_step_index in range(2):
        padded = with_halo(salinity, (("tile", 2),), 2)
        salinity = solve_columns(
            advect(padded, east_courant, eastern_face_open, v_courant, wet_float), tridiag_terms
        )
    return salinity


def solution(mesh):
    placed = (
        P("mem", None, "tile", None),
        P(None, "tile", None),
        P(None, "tile", None),
        P(None, "tile", None),
        P(None, "tile", None),
        P(),
        P("mem"),
        P("tile", None),
    )
    return jax.shard_map(
        per_device,
        mesh=mesh,
        in_specs=placed,
        out_specs=P("mem", None, "tile", None),
        check_vma=False,
    )
```

```python
import functools

import jax
import jax.numpy as jnp
from jax import lax
from jax.experimental import pallas as pl
from jax.experimental.pallas import tpu as pltpu
from jax.sharding import PartitionSpec as P

MESH_ID = pl.DeviceIdType.MESH


def allreduce_kernel(
    n, members_ref, u_ref, wet_ref, c_ref, o_ref, ulow_ref, wlow_ref, whigh_ref,
    x_ref, recv, red, gath, uedge, wedge, ubuf, wbuf, s1, r1, s2, r2, se, re,
):
    me = lax.axis_index("mem")
    tile = lax.axis_index("tile")
    tiles = lax.axis_size("tile")
    has_left = tile > 0
    has_right = tile < tiles - 1
    rows = x_ref.shape[0] // n
    columns = u_ref.shape[1]
    half = n // 2
    ring_y, ring_z = me // 2, lax.rem(me, 2)
    offsets = [(2, 1), (3, 1), (2, 0), (1, 1), (3, 0), (1, 0), (0, 1)]
    peers = [lax.rem(ring_y + dy, half) * 2 + lax.rem(ring_z + dz, 2) for dy, dz in offsets]
    barrier = pltpu.get_barrier_semaphore()
    for peer in peers:
        pl.semaphore_signal(barrier, inc=1, device_id=(tile, peer), device_id_type=MESH_ID)

    @pl.when(has_left)
    def _():
        pl.semaphore_signal(barrier, inc=1, device_id=(tile - 1, me), device_id_type=MESH_ID)

    @pl.when(has_right)
    def _():
        pl.semaphore_signal(barrier, inc=1, device_id=(tile + 1, me), device_id_type=MESH_ID)

    uedge[...] = u_ref[:, columns - 1, :]
    wedge[0] = wet_ref[pl.ds(columns - 1, 1), :]
    wedge[1] = wet_ref[pl.ds(0, 1), :]

    def local_sum(k, carry):
        level = members_ref[0, k]
        for m in range(1, members_ref.shape[0]):
            level = level + members_ref[m, k]
        x_ref[k] = level
        return carry

    lax.fori_loop(0, x_ref.shape[0], local_sum, 0)
    pl.semaphore_wait(
        barrier, n - 1 + has_left.astype(jnp.int32) + has_right.astype(jnp.int32)
    )

    def copy_to(src, dst, send, recv_sem, device):
        return pltpu.make_async_remote_copy(
            src_ref=src,
            dst_ref=dst,
            send_sem=send,
            recv_sem=recv_sem,
            device_id=device,
            device_id_type=MESH_ID,
        )

    right_copies = [
        copy_to(uedge, ubuf, se.at[0], re.at[0], (tile + 1, me)),
        copy_to(wedge.at[0], wbuf.at[0], se.at[1], re.at[1], (tile + 1, me)),
    ]
    left_copy = copy_to(wedge.at[1], wbuf.at[1], se.at[2], re.at[2], (tile - 1, me))

    @pl.when(has_right)
    def _():
        for copy in right_copies:
            copy.start()

    @pl.when(has_left)
    def _():
        left_copy.start()

    firsts = [
        copy_to(x_ref.at[pl.ds(peer * rows, rows)], recv.at[me], s1.at[peer], r1.at[me], (tile, peer))
        for peer in peers
    ]
    for copy in firsts:
        copy.start()
    for peer in peers:
        copy_to(x_ref.at[pl.ds(0, rows)], recv.at[peer], s1.at[peer], r1.at[peer], (tile, peer)).wait_recv()
    acc = x_ref[pl.ds(me * rows, rows)]
    for peer in peers:
        acc = acc + recv[peer]
    red[...] = acc
    scale = 1.0 / (n * members_ref.shape[0])
    own = pl.ds(me * rows, rows)
    o_ref[own] = c_ref[own] - acc * scale
    seconds = [copy_to(red, gath.at[me], s2.at[peer], r2.at[me], (tile, peer)) for peer in peers]
    for copy in seconds:
        copy.start()
    for peer in peers:
        copy_to(red, gath.at[peer], s2.at[peer], r2.at[peer], (tile, peer)).wait_recv()
        part = pl.ds(peer * rows, rows)
        o_ref[part] = c_ref[part] - gath[peer] * scale
    for copy in firsts + seconds:
        copy.wait_send()

    @pl.when(has_right)
    def _():
        for copy in right_copies:
            copy.wait_send()

    @pl.when(has_left)
    def _():
        left_copy.wait_send()
        for copy in right_copies:
            copy.wait_recv()
        ulow_ref[...] = ubuf[...]
        wlow_ref[...] = wbuf[0]

    @pl.when(jnp.logical_not(has_left))
    def _():
        ulow_ref[...] = jnp.zeros_like(ulow_ref)
        wlow_ref[...] = jnp.zeros_like(wlow_ref)

    @pl.when(has_right)
    def _():
        left_copy.wait_recv()
        whigh_ref[...] = wbuf[1]

    @pl.when(jnp.logical_not(has_right))
    def _():
        whigh_ref[...] = jnp.zeros_like(whigh_ref)


def member_allreduce(members, u_courant, wet, control):
    total = jax.ShapeDtypeStruct(members.shape[1:], members.dtype)
    n = lax.axis_size("mem")
    rows = total.shape[0] // n
    chunk = (rows,) + total.shape[1:]
    levels, lanes = u_courant.shape[0], u_courant.shape[2]
    vmem = pl.BlockSpec(memory_space=pltpu.VMEM)
    return pl.pallas_call(
        functools.partial(allreduce_kernel, n),
        out_shape=(
            jax.ShapeDtypeStruct(total.shape, total.dtype),
            jax.ShapeDtypeStruct((levels, lanes), u_courant.dtype),
            jax.ShapeDtypeStruct((1, lanes), wet.dtype),
            jax.ShapeDtypeStruct((1, lanes), wet.dtype),
        ),
        in_specs=[vmem] * 4,
        out_specs=(vmem,) * 4,
        scratch_shapes=[
            pltpu.VMEM(total.shape, total.dtype),
            pltpu.VMEM((n,) + chunk, total.dtype),
            pltpu.VMEM(chunk, total.dtype),
            pltpu.VMEM((n,) + chunk, total.dtype),
            pltpu.VMEM((levels, lanes), u_courant.dtype),
            pltpu.VMEM((2, 1, lanes), wet.dtype),
            pltpu.VMEM((levels, lanes), u_courant.dtype),
            pltpu.VMEM((2, 1, lanes), wet.dtype),
            pltpu.SemaphoreType.DMA((n,)),
            pltpu.SemaphoreType.DMA((n,)),
            pltpu.SemaphoreType.DMA((n,)),
            pltpu.SemaphoreType.DMA((n,)),
            pltpu.SemaphoreType.DMA((3,)),
            pltpu.SemaphoreType.DMA((3,)),
        ],
        compiler_params=pltpu.CompilerParams(collective_id=0, has_side_effects=True),
    )(members, u_courant, wet, control)


def with_halo(block, sides, width):
    for axis, dim in sides:
        count = lax.axis_size(axis)
        forward = [(i, i + 1) for i in range(count - 1)]
        backward = [(target, source) for source, target in forward]
        low = lax.ppermute(
            lax.slice_in_dim(block, block.shape[dim] - width, None, axis=dim), axis, forward
        )
        high = lax.ppermute(lax.slice_in_dim(block, 0, width, axis=dim), axis, backward)
        block = jnp.concatenate([low, block, high], axis=dim)
    return block


def minmod(first_diff, second_diff):
    return (
        0.5
        * (jnp.sign(first_diff) + jnp.sign(second_diff))
        * jnp.minimum(jnp.abs(first_diff), jnp.abs(second_diff))
    )


def face_flux(courant, far_back, near_back, near_ahead, far_ahead, open_face):
    positive = courant > 0.0
    upwind = jnp.where(positive, near_back, near_ahead)
    side_diff = jnp.where(positive, near_back - far_back, far_ahead - near_ahead)
    limited = minmod(near_ahead - near_back, side_diff)
    magnitude = jnp.abs(courant)
    return (courant * upwind + 0.5 * magnitude * (1.0 - magnitude) * limited) * open_face


def advect(salinity, east_courant, eastern_face_open, north_courant, wet_cells):
    columns = salinity.shape[2]
    east_flux = face_flux(
        east_courant,
        salinity[:, :, 0 : columns - 3],
        salinity[:, :, 1 : columns - 2],
        salinity[:, :, 2 : columns - 1],
        salinity[:, :, 3:columns],
        eastern_face_open,
    )
    interior = salinity[:, :, 2 : columns - 2]
    zero_col = jnp.zeros_like(interior[..., :1])
    lower_cells = jnp.concatenate([zero_col, interior[..., :-1]], -1)
    upper_cells = jnp.concatenate([interior[..., 1:], zero_col], -1)
    upper_two = jnp.concatenate([interior[..., 2:], zero_col, zero_col], -1)
    wet_next = jnp.concatenate([wet_cells[:, 1:], jnp.zeros_like(wet_cells[:, :1])], -1)
    poleward_transport = face_flux(
        north_courant, lower_cells, interior, upper_cells, upper_two, wet_cells * wet_next
    )
    equatorward_transport = jnp.concatenate([zero_col, poleward_transport[..., :-1]], -1)
    return (
        interior
        - (east_flux[:, :, 1:] - east_flux[:, :, :-1])
        - (poleward_transport - equatorward_transport)
    )


def factor(diff_rates):
    levels = diff_rates.shape[1] + 1
    thomas_coefficients = []
    inverse_terms = []
    previous = None
    for level_index in range(levels):
        diagonal = jnp.ones_like(diff_rates[:, 0])
        if level_index > 0:
            diagonal = diagonal + diff_rates[:, level_index - 1]
        if level_index < levels - 1:
            diagonal = diagonal + diff_rates[:, level_index]
        if level_index > 0:
            diagonal = diagonal + diff_rates[:, level_index - 1] * previous
        inverse_den = 1.0 / diagonal
        inverse_terms.append(inverse_den)
        if level_index < levels - 1:
            previous = -diff_rates[:, level_index] * inverse_den
            thomas_coefficients.append(previous)
    return (diff_rates, thomas_coefficients, inverse_terms)


def solve_columns(values, tridiag_terms):
    diff_rates, thomas_coefficients, inverse_terms = tridiag_terms
    levels = values.shape[1]
    forward = [values[:, 0] * inverse_terms[0]]
    for level_index in range(1, levels):
        forward.append(
            (values[:, level_index] + diff_rates[:, level_index - 1] * forward[-1])
            * inverse_terms[level_index]
        )
    solution = [None] * levels
    solution[levels - 1] = forward[levels - 1]
    for level_index in range(levels - 2, -1, -1):
        solution[level_index] = (
            forward[level_index] - thomas_coefficients[level_index] * solution[level_index + 1]
        )
    return jnp.stack(solution, 1)


def per_device(members, control, u_courant, v_courant, diffusion, group_scale, group_of, wet):
    levels = members.shape[1]
    columns = members.shape[2]
    realisation_total = members.shape[0] * lax.axis_size("mem")
    group_ids = jnp.arange(group_scale.shape[0], dtype=jnp.int32)
    spread_multiplier = jnp.sum(
        jnp.where(group_of[:, None] == group_ids[None, :], group_scale[None, :], 0.0), 1
    )
    wet_float = wet.astype(jnp.float32)
    recentre_shift, u_low, wet_low, wet_high = member_allreduce(members, u_courant, wet, control)
    salinity = members + recentre_shift[None]
    east_courant = jnp.concatenate([u_low[:, None], u_courant], 1)
    wet_ext = jnp.concatenate([wet_low, wet, wet_high], 0).astype(jnp.float32)
    eastern_face_open = wet_ext[0 : columns + 1] * wet_ext[1 : columns + 2]
    tridiag_terms = factor(spread_multiplier[:, None, None, None] * diffusion[None])
    for time_step_index in range(2):
        padded = with_halo(salinity, (("tile", 2),), 2)
        salinity = solve_columns(
            advect(padded, east_courant, eastern_face_open, v_courant, wet_float), tridiag_terms
        )
    return salinity


def solution(mesh):
    placed = (
        P("mem", None, "tile", None),
        P(None, "tile", None),
        P(None, "tile", None),
        P(None, "tile", None),
        P(None, "tile", None),
        P(),
        P("mem"),
        P("tile", None),
    )
    return jax.shard_map(
        per_device,
        mesh=mesh,
        in_specs=placed,
        out_specs=P("mem", None, "tile", None),
        check_vma=False,
    )
```

```python
import functools

import jax
import jax.numpy as jnp
from jax import lax
from jax.experimental import pallas as pl
from jax.experimental.pallas import tpu as pltpu
from jax.sharding import PartitionSpec as P

MESH_ID = pl.DeviceIdType.MESH
RELAY_DY = 3


def allreduce_kernel(
    n, members_ref, u_ref, wet_ref, c_ref, o_ref, ulow_ref, wlow_ref, whigh_ref,
    x_ref, recv, red, gath, uedge, wedge, ubuf, wbuf, rbuf, s1, r1, s2, r2, se, re, sr, rr, sf, r1b,
):
    me = lax.axis_index("mem")
    tile = lax.axis_index("tile")
    tiles = lax.axis_size("tile")
    has_left = tile > 0
    has_right = tile < tiles - 1
    rows = x_ref.shape[0] // n
    columns = u_ref.shape[1]
    half = n // 2
    ring_y, ring_z = me // 2, lax.rem(me, 2)
    offsets = [(2, 1), (2, 0), (1, 1), (3, 1), (1, 0), (3, 0), (0, 1)]
    peers = [lax.rem(ring_y + dy, half) * 2 + lax.rem(ring_z + dz, 2) for dy, dz in offsets]
    barrier = pltpu.get_barrier_semaphore()
    for peer in peers:
        pl.semaphore_signal(barrier, inc=1, device_id=(tile, peer), device_id_type=MESH_ID)

    @pl.when(has_left)
    def _():
        pl.semaphore_signal(barrier, inc=1, device_id=(tile - 1, me), device_id_type=MESH_ID)

    @pl.when(has_right)
    def _():
        pl.semaphore_signal(barrier, inc=1, device_id=(tile + 1, me), device_id_type=MESH_ID)

    uedge[...] = u_ref[:, columns - 1, :]
    wedge[0] = wet_ref[pl.ds(columns - 1, 1), :]
    wedge[1] = wet_ref[pl.ds(0, 1), :]

    def local_sum(k, carry):
        level = members_ref[0, k]
        for m in range(1, members_ref.shape[0]):
            level = level + members_ref[m, k]
        x_ref[k] = level
        return carry

    lax.fori_loop(0, x_ref.shape[0], local_sum, 0)
    pl.semaphore_wait(
        barrier, n - 1 + has_left.astype(jnp.int32) + has_right.astype(jnp.int32)
    )

    def copy_to(src, dst, send, recv_sem, device):
        return pltpu.make_async_remote_copy(
            src_ref=src,
            dst_ref=dst,
            send_sem=send,
            recv_sem=recv_sem,
            device_id=device,
            device_id_type=MESH_ID,
        )

    right_copies = [
        copy_to(uedge, ubuf, se.at[0], re.at[0], (tile + 1, me)),
        copy_to(wedge.at[0], wbuf.at[0], se.at[1], re.at[1], (tile + 1, me)),
    ]
    left_copy = copy_to(wedge.at[1], wbuf.at[1], se.at[2], re.at[2], (tile - 1, me))

    @pl.when(has_right)
    def _():
        for copy in right_copies:
            copy.start()

    @pl.when(has_left)
    def _():
        left_copy.start()

    def peer_of(dy, dz):
        return lax.rem(ring_y + dy, half) * 2 + lax.rem(ring_z + dz, 2)

    split = rows // 2
    far = [peer_of(2, dz) for dz in (1, 0)]
    near = [peer_of(dy, dz) for dy, dz in offsets[2:]]
    relay = peer_of(RELAY_DY, 0)
    source = peer_of(half - RELAY_DY, 0)
    targets = [peer_of(half - RELAY_DY + 2, dz) for dz in (1, 0)]
    firsts = [
        copy_to(x_ref.at[pl.ds(p * rows, split)], recv.at[me, pl.ds(0, split)], s1.at[p], r1.at[me], (tile, p))
        for p in far
    ]
    firsts += [
        copy_to(x_ref.at[pl.ds(p * rows + split, split)], rbuf.at[i], sr.at[i], rr.at[i], (tile, relay))
        for i, p in enumerate(far)
    ]
    firsts += [
        copy_to(x_ref.at[pl.ds(p * rows, rows)], recv.at[me], s1.at[p], r1.at[me], (tile, p))
        for p in near
    ]
    for copy in firsts:
        copy.start()
    forwards = [
        copy_to(rbuf.at[i], recv.at[source, pl.ds(split, split)], sf.at[i], r1b.at[source], (tile, t))
        for i, t in enumerate(targets)
    ]
    for i, copy in enumerate(forwards):
        copy_to(x_ref.at[pl.ds(0, split)], rbuf.at[i], sr.at[i], rr.at[i], (tile, source)).wait_recv()
        copy.start()
    for p in far:
        copy_to(x_ref.at[pl.ds(0, split)], recv.at[p, pl.ds(0, split)], s1.at[p], r1.at[p], (tile, p)).wait_recv()
        copy_to(x_ref.at[pl.ds(0, split)], recv.at[p, pl.ds(split, split)], s1.at[p], r1b.at[p], (tile, p)).wait_recv()
    for p in near:
        copy_to(x_ref.at[pl.ds(0, rows)], recv.at[p], s1.at[p], r1.at[p], (tile, p)).wait_recv()
    firsts += forwards
    acc = x_ref[pl.ds(me * rows, rows)]
    for peer in peers:
        acc = acc + recv[peer]
    red[...] = acc
    scale = 1.0 / (n * members_ref.shape[0])
    own = pl.ds(me * rows, rows)
    o_ref[own] = c_ref[own] - acc * scale
    seconds = [copy_to(red, gath.at[me], s2.at[peer], r2.at[me], (tile, peer)) for peer in peers]
    for copy in seconds:
        copy.start()
    for peer in peers:
        copy_to(red, gath.at[peer], s2.at[peer], r2.at[peer], (tile, peer)).wait_recv()
        part = pl.ds(peer * rows, rows)
        o_ref[part] = c_ref[part] - gath[peer] * scale
    for copy in firsts + seconds:
        copy.wait_send()

    @pl.when(has_right)
    def _():
        for copy in right_copies:
            copy.wait_send()

    @pl.when(has_left)
    def _():
        left_copy.wait_send()
        for copy in right_copies:
            copy.wait_recv()
        ulow_ref[...] = ubuf[...]
        wlow_ref[...] = wbuf[0]

    @pl.when(jnp.logical_not(has_left))
    def _():
        ulow_ref[...] = jnp.zeros_like(ulow_ref)
        wlow_ref[...] = jnp.zeros_like(wlow_ref)

    @pl.when(has_right)
    def _():
        left_copy.wait_recv()
        whigh_ref[...] = wbuf[1]

    @pl.when(jnp.logical_not(has_right))
    def _():
        whigh_ref[...] = jnp.zeros_like(whigh_ref)


def member_allreduce(members, u_courant, wet, control):
    total = jax.ShapeDtypeStruct(members.shape[1:], members.dtype)
    n = lax.axis_size("mem")
    rows = total.shape[0] // n
    chunk = (rows,) + total.shape[1:]
    levels, lanes = u_courant.shape[0], u_courant.shape[2]
    vmem = pl.BlockSpec(memory_space=pltpu.VMEM)
    return pl.pallas_call(
        functools.partial(allreduce_kernel, n),
        out_shape=(
            jax.ShapeDtypeStruct(total.shape, total.dtype),
            jax.ShapeDtypeStruct((levels, lanes), u_courant.dtype),
            jax.ShapeDtypeStruct((1, lanes), wet.dtype),
            jax.ShapeDtypeStruct((1, lanes), wet.dtype),
        ),
        in_specs=[vmem] * 4,
        out_specs=(vmem,) * 4,
        scratch_shapes=[
            pltpu.VMEM(total.shape, total.dtype),
            pltpu.VMEM((n,) + chunk, total.dtype),
            pltpu.VMEM(chunk, total.dtype),
            pltpu.VMEM((n,) + chunk, total.dtype),
            pltpu.VMEM((levels, lanes), u_courant.dtype),
            pltpu.VMEM((2, 1, lanes), wet.dtype),
            pltpu.VMEM((levels, lanes), u_courant.dtype),
            pltpu.VMEM((2, 1, lanes), wet.dtype),
            pltpu.VMEM((2, rows // 2) + total.shape[1:], total.dtype),
            pltpu.SemaphoreType.DMA((n,)),
            pltpu.SemaphoreType.DMA((n,)),
            pltpu.SemaphoreType.DMA((n,)),
            pltpu.SemaphoreType.DMA((n,)),
            pltpu.SemaphoreType.DMA((3,)),
            pltpu.SemaphoreType.DMA((3,)),
            pltpu.SemaphoreType.DMA((2,)),
            pltpu.SemaphoreType.DMA((2,)),
            pltpu.SemaphoreType.DMA((2,)),
            pltpu.SemaphoreType.DMA((n,)),
        ],
        compiler_params=pltpu.CompilerParams(collective_id=0, has_side_effects=True),
    )(members, u_courant, wet, control)


def with_halo(block, sides, width):
    for axis, dim in sides:
        count = lax.axis_size(axis)
        forward = [(i, i + 1) for i in range(count - 1)]
        backward = [(target, source) for source, target in forward]
        low = lax.ppermute(
            lax.slice_in_dim(block, block.shape[dim] - width, None, axis=dim), axis, forward
        )
        high = lax.ppermute(lax.slice_in_dim(block, 0, width, axis=dim), axis, backward)
        block = jnp.concatenate([low, block, high], axis=dim)
    return block


def minmod(first_diff, second_diff):
    return (
        0.5
        * (jnp.sign(first_diff) + jnp.sign(second_diff))
        * jnp.minimum(jnp.abs(first_diff), jnp.abs(second_diff))
    )


def face_flux(courant, far_back, near_back, near_ahead, far_ahead, open_face):
    positive = courant > 0.0
    upwind = jnp.where(positive, near_back, near_ahead)
    side_diff = jnp.where(positive, near_back - far_back, far_ahead - near_ahead)
    limited = minmod(near_ahead - near_back, side_diff)
    magnitude = jnp.abs(courant)
    return (courant * upwind + 0.5 * magnitude * (1.0 - magnitude) * limited) * open_face


def advect(salinity, east_courant, eastern_face_open, north_courant, wet_cells):
    columns = salinity.shape[2]
    east_flux = face_flux(
        east_courant,
        salinity[:, :, 0 : columns - 3],
        salinity[:, :, 1 : columns - 2],
        salinity[:, :, 2 : columns - 1],
        salinity[:, :, 3:columns],
        eastern_face_open,
    )
    interior = salinity[:, :, 2 : columns - 2]
    zero_col = jnp.zeros_like(interior[..., :1])
    lower_cells = jnp.concatenate([zero_col, interior[..., :-1]], -1)
    upper_cells = jnp.concatenate([interior[..., 1:], zero_col], -1)
    upper_two = jnp.concatenate([interior[..., 2:], zero_col, zero_col], -1)
    wet_next = jnp.concatenate([wet_cells[:, 1:], jnp.zeros_like(wet_cells[:, :1])], -1)
    poleward_transport = face_flux(
        north_courant, lower_cells, interior, upper_cells, upper_two, wet_cells * wet_next
    )
    equatorward_transport = jnp.concatenate([zero_col, poleward_transport[..., :-1]], -1)
    return (
        interior
        - (east_flux[:, :, 1:] - east_flux[:, :, :-1])
        - (poleward_transport - equatorward_transport)
    )


def factor(diff_rates):
    levels = diff_rates.shape[1] + 1
    thomas_coefficients = []
    inverse_terms = []
    previous = None
    for level_index in range(levels):
        diagonal = jnp.ones_like(diff_rates[:, 0])
        if level_index > 0:
            diagonal = diagonal + diff_rates[:, level_index - 1]
        if level_index < levels - 1:
            diagonal = diagonal + diff_rates[:, level_index]
        if level_index > 0:
            diagonal = diagonal + diff_rates[:, level_index - 1] * previous
        inverse_den = 1.0 / diagonal
        inverse_terms.append(inverse_den)
        if level_index < levels - 1:
            previous = -diff_rates[:, level_index] * inverse_den
            thomas_coefficients.append(previous)
    return (diff_rates, thomas_coefficients, inverse_terms)


def solve_columns(values, tridiag_terms):
    diff_rates, thomas_coefficients, inverse_terms = tridiag_terms
    levels = values.shape[1]
    forward = [values[:, 0] * inverse_terms[0]]
    for level_index in range(1, levels):
        forward.append(
            (values[:, level_index] + diff_rates[:, level_index - 1] * forward[-1])
            * inverse_terms[level_index]
        )
    solution = [None] * levels
    solution[levels - 1] = forward[levels - 1]
    for level_index in range(levels - 2, -1, -1):
        solution[level_index] = (
            forward[level_index] - thomas_coefficients[level_index] * solution[level_index + 1]
        )
    return jnp.stack(solution, 1)


def per_device(members, control, u_courant, v_courant, diffusion, group_scale, group_of, wet):
    levels = members.shape[1]
    columns = members.shape[2]
    realisation_total = members.shape[0] * lax.axis_size("mem")
    group_ids = jnp.arange(group_scale.shape[0], dtype=jnp.int32)
    spread_multiplier = jnp.sum(
        jnp.where(group_of[:, None] == group_ids[None, :], group_scale[None, :], 0.0), 1
    )
    wet_float = wet.astype(jnp.float32)
    recentre_shift, u_low, wet_low, wet_high = member_allreduce(members, u_courant, wet, control)
    salinity = members + recentre_shift[None]
    east_courant = jnp.concatenate([u_low[:, None], u_courant], 1)
    wet_ext = jnp.concatenate([wet_low, wet, wet_high], 0).astype(jnp.float32)
    eastern_face_open = wet_ext[0 : columns + 1] * wet_ext[1 : columns + 2]
    tridiag_terms = factor(spread_multiplier[:, None, None, None] * diffusion[None])
    for time_step_index in range(2):
        padded = with_halo(salinity, (("tile", 2),), 2)
        salinity = solve_columns(
            advect(padded, east_courant, eastern_face_open, v_courant, wet_float), tridiag_terms
        )
    return salinity


def solution(mesh):
    placed = (
        P("mem", None, "tile", None),
        P(None, "tile", None),
        P(None, "tile", None),
        P(None, "tile", None),
        P(None, "tile", None),
        P(),
        P("mem"),
        P("tile", None),
    )
    return jax.shard_map(
        per_device,
        mesh=mesh,
        in_specs=placed,
        out_specs=P("mem", None, "tile", None),
        check_vma=False,
    )
```

```python
import functools

import jax
import jax.numpy as jnp
from jax import lax
from jax.experimental import pallas as pl
from jax.experimental.pallas import tpu as pltpu
from jax.sharding import PartitionSpec as P

MESH_ID = pl.DeviceIdType.MESH
RELAY_DY = 1


def allreduce_kernel(
    n, members_ref, u_ref, wet_ref, c_ref, o_ref, ulow_ref, wlow_ref, whigh_ref,
    x_ref, recv, red, gath, uedge, wedge, ubuf, wbuf, rbuf, s1, r1, s2, r2, se, re, sr, rr, sf, r1b,
):
    me = lax.axis_index("mem")
    tile = lax.axis_index("tile")
    tiles = lax.axis_size("tile")
    has_left = tile > 0
    has_right = tile < tiles - 1
    rows = x_ref.shape[0] // n
    columns = u_ref.shape[1]
    half = n // 2
    ring_y, ring_z = me // 2, lax.rem(me, 2)
    offsets = [(2, 1), (2, 0), (1, 1), (3, 1), (1, 0), (3, 0), (0, 1)]
    peers = [lax.rem(ring_y + dy, half) * 2 + lax.rem(ring_z + dz, 2) for dy, dz in offsets]
    barrier = pltpu.get_barrier_semaphore()
    for peer in peers:
        pl.semaphore_signal(barrier, inc=1, device_id=(tile, peer), device_id_type=MESH_ID)

    @pl.when(has_left)
    def _():
        pl.semaphore_signal(barrier, inc=1, device_id=(tile - 1, me), device_id_type=MESH_ID)

    @pl.when(has_right)
    def _():
        pl.semaphore_signal(barrier, inc=1, device_id=(tile + 1, me), device_id_type=MESH_ID)

    uedge[...] = u_ref[:, columns - 1, :]
    wedge[0] = wet_ref[pl.ds(columns - 1, 1), :]
    wedge[1] = wet_ref[pl.ds(0, 1), :]

    def local_sum(k, carry):
        level = members_ref[0, k]
        for m in range(1, members_ref.shape[0]):
            level = level + members_ref[m, k]
        x_ref[k] = level
        return carry

    lax.fori_loop(0, x_ref.shape[0], local_sum, 0)
    pl.semaphore_wait(
        barrier, n - 1 + has_left.astype(jnp.int32) + has_right.astype(jnp.int32)
    )

    def copy_to(src, dst, send, recv_sem, device):
        return pltpu.make_async_remote_copy(
            src_ref=src,
            dst_ref=dst,
            send_sem=send,
            recv_sem=recv_sem,
            device_id=device,
            device_id_type=MESH_ID,
        )

    right_copies = [
        copy_to(uedge, ubuf, se.at[0], re.at[0], (tile + 1, me)),
        copy_to(wedge.at[0], wbuf.at[0], se.at[1], re.at[1], (tile + 1, me)),
    ]
    left_copy = copy_to(wedge.at[1], wbuf.at[1], se.at[2], re.at[2], (tile - 1, me))

    @pl.when(has_right)
    def _():
        for copy in right_copies:
            copy.start()

    @pl.when(has_left)
    def _():
        left_copy.start()

    def peer_of(dy, dz):
        return lax.rem(ring_y + dy, half) * 2 + lax.rem(ring_z + dz, 2)

    split = rows // 2
    far = [peer_of(2, dz) for dz in (1, 0)]
    near = [peer_of(dy, dz) for dy, dz in offsets[2:]]
    relay = peer_of(RELAY_DY, 0)
    source = peer_of(half - RELAY_DY, 0)
    targets = [peer_of(half - RELAY_DY + 2, dz) for dz in (1, 0)]
    firsts = [
        copy_to(x_ref.at[pl.ds(p * rows, split)], recv.at[me, pl.ds(0, split)], s1.at[p], r1.at[me], (tile, p))
        for p in far
    ]
    firsts += [
        copy_to(x_ref.at[pl.ds(p * rows + split, split)], rbuf.at[i], sr.at[i], rr.at[i], (tile, relay))
        for i, p in enumerate(far)
    ]
    firsts += [
        copy_to(x_ref.at[pl.ds(p * rows, rows)], recv.at[me], s1.at[p], r1.at[me], (tile, p))
        for p in near
    ]
    for copy in firsts:
        copy.start()
    forwards = [
        copy_to(rbuf.at[i], recv.at[source, pl.ds(split, split)], sf.at[i], r1b.at[source], (tile, t))
        for i, t in enumerate(targets)
    ]
    for i, copy in enumerate(forwards):
        copy_to(x_ref.at[pl.ds(0, split)], rbuf.at[i], sr.at[i], rr.at[i], (tile, source)).wait_recv()
        copy.start()
    for p in far:
        copy_to(x_ref.at[pl.ds(0, split)], recv.at[p, pl.ds(0, split)], s1.at[p], r1.at[p], (tile, p)).wait_recv()
        copy_to(x_ref.at[pl.ds(0, split)], recv.at[p, pl.ds(split, split)], s1.at[p], r1b.at[p], (tile, p)).wait_recv()
    for p in near:
        copy_to(x_ref.at[pl.ds(0, rows)], recv.at[p], s1.at[p], r1.at[p], (tile, p)).wait_recv()
    firsts += forwards
    acc = x_ref[pl.ds(me * rows, rows)]
    for peer in peers:
        acc = acc + recv[peer]
    red[...] = acc
    scale = 1.0 / (n * members_ref.shape[0])
    own = pl.ds(me * rows, rows)
    o_ref[own] = c_ref[own] - acc * scale
    seconds = [copy_to(red, gath.at[me], s2.at[peer], r2.at[me], (tile, peer)) for peer in peers]
    for copy in seconds:
        copy.start()
    for peer in peers:
        copy_to(red, gath.at[peer], s2.at[peer], r2.at[peer], (tile, peer)).wait_recv()
        part = pl.ds(peer * rows, rows)
        o_ref[part] = c_ref[part] - gath[peer] * scale
    for copy in firsts + seconds:
        copy.wait_send()

    @pl.when(has_right)
    def _():
        for copy in right_copies:
            copy.wait_send()

    @pl.when(has_left)
    def _():
        left_copy.wait_send()
        for copy in right_copies:
            copy.wait_recv()
        ulow_ref[...] = ubuf[...]
        wlow_ref[...] = wbuf[0]

    @pl.when(jnp.logical_not(has_left))
    def _():
        ulow_ref[...] = jnp.zeros_like(ulow_ref)
        wlow_ref[...] = jnp.zeros_like(wlow_ref)

    @pl.when(has_right)
    def _():
        left_copy.wait_recv()
        whigh_ref[...] = wbuf[1]

    @pl.when(jnp.logical_not(has_right))
    def _():
        whigh_ref[...] = jnp.zeros_like(whigh_ref)


def member_allreduce(members, u_courant, wet, control):
    total = jax.ShapeDtypeStruct(members.shape[1:], members.dtype)
    n = lax.axis_size("mem")
    rows = total.shape[0] // n
    chunk = (rows,) + total.shape[1:]
    levels, lanes = u_courant.shape[0], u_courant.shape[2]
    vmem = pl.BlockSpec(memory_space=pltpu.VMEM)
    return pl.pallas_call(
        functools.partial(allreduce_kernel, n),
        out_shape=(
            jax.ShapeDtypeStruct(total.shape, total.dtype),
            jax.ShapeDtypeStruct((levels, lanes), u_courant.dtype),
            jax.ShapeDtypeStruct((1, lanes), wet.dtype),
            jax.ShapeDtypeStruct((1, lanes), wet.dtype),
        ),
        in_specs=[vmem] * 4,
        out_specs=(vmem,) * 4,
        scratch_shapes=[
            pltpu.VMEM(total.shape, total.dtype),
            pltpu.VMEM((n,) + chunk, total.dtype),
            pltpu.VMEM(chunk, total.dtype),
            pltpu.VMEM((n,) + chunk, total.dtype),
            pltpu.VMEM((levels, lanes), u_courant.dtype),
            pltpu.VMEM((2, 1, lanes), wet.dtype),
            pltpu.VMEM((levels, lanes), u_courant.dtype),
            pltpu.VMEM((2, 1, lanes), wet.dtype),
            pltpu.VMEM((2, rows // 2) + total.shape[1:], total.dtype),
            pltpu.SemaphoreType.DMA((n,)),
            pltpu.SemaphoreType.DMA((n,)),
            pltpu.SemaphoreType.DMA((n,)),
            pltpu.SemaphoreType.DMA((n,)),
            pltpu.SemaphoreType.DMA((3,)),
            pltpu.SemaphoreType.DMA((3,)),
            pltpu.SemaphoreType.DMA((2,)),
            pltpu.SemaphoreType.DMA((2,)),
            pltpu.SemaphoreType.DMA((2,)),
            pltpu.SemaphoreType.DMA((n,)),
        ],
        compiler_params=pltpu.CompilerParams(collective_id=0, has_side_effects=True),
    )(members, u_courant, wet, control)


def with_halo(block, sides, width):
    for axis, dim in sides:
        count = lax.axis_size(axis)
        forward = [(i, i + 1) for i in range(count - 1)]
        backward = [(target, source) for source, target in forward]
        low = lax.ppermute(
            lax.slice_in_dim(block, block.shape[dim] - width, None, axis=dim), axis, forward
        )
        high = lax.ppermute(lax.slice_in_dim(block, 0, width, axis=dim), axis, backward)
        block = jnp.concatenate([low, block, high], axis=dim)
    return block


def minmod(first_diff, second_diff):
    return (
        0.5
        * (jnp.sign(first_diff) + jnp.sign(second_diff))
        * jnp.minimum(jnp.abs(first_diff), jnp.abs(second_diff))
    )


def face_flux(courant, far_back, near_back, near_ahead, far_ahead, open_face):
    positive = courant > 0.0
    upwind = jnp.where(positive, near_back, near_ahead)
    side_diff = jnp.where(positive, near_back - far_back, far_ahead - near_ahead)
    limited = minmod(near_ahead - near_back, side_diff)
    magnitude = jnp.abs(courant)
    return (courant * upwind + 0.5 * magnitude * (1.0 - magnitude) * limited) * open_face


def advect(salinity, east_courant, eastern_face_open, north_courant, wet_cells):
    columns = salinity.shape[2]
    east_flux = face_flux(
        east_courant,
        salinity[:, :, 0 : columns - 3],
        salinity[:, :, 1 : columns - 2],
        salinity[:, :, 2 : columns - 1],
        salinity[:, :, 3:columns],
        eastern_face_open,
    )
    interior = salinity[:, :, 2 : columns - 2]
    zero_col = jnp.zeros_like(interior[..., :1])
    lower_cells = jnp.concatenate([zero_col, interior[..., :-1]], -1)
    upper_cells = jnp.concatenate([interior[..., 1:], zero_col], -1)
    upper_two = jnp.concatenate([interior[..., 2:], zero_col, zero_col], -1)
    wet_next = jnp.concatenate([wet_cells[:, 1:], jnp.zeros_like(wet_cells[:, :1])], -1)
    poleward_transport = face_flux(
        north_courant, lower_cells, interior, upper_cells, upper_two, wet_cells * wet_next
    )
    equatorward_transport = jnp.concatenate([zero_col, poleward_transport[..., :-1]], -1)
    return (
        interior
        - (east_flux[:, :, 1:] - east_flux[:, :, :-1])
        - (poleward_transport - equatorward_transport)
    )


def factor(diff_rates):
    levels = diff_rates.shape[1] + 1
    thomas_coefficients = []
    inverse_terms = []
    previous = None
    for level_index in range(levels):
        diagonal = jnp.ones_like(diff_rates[:, 0])
        if level_index > 0:
            diagonal = diagonal + diff_rates[:, level_index - 1]
        if level_index < levels - 1:
            diagonal = diagonal + diff_rates[:, level_index]
        if level_index > 0:
            diagonal = diagonal + diff_rates[:, level_index - 1] * previous
        inverse_den = 1.0 / diagonal
        inverse_terms.append(inverse_den)
        if level_index < levels - 1:
            previous = -diff_rates[:, level_index] * inverse_den
            thomas_coefficients.append(previous)
    return (diff_rates, thomas_coefficients, inverse_terms)


def solve_columns(values, tridiag_terms):
    diff_rates, thomas_coefficients, inverse_terms = tridiag_terms
    levels = values.shape[1]
    forward = [values[:, 0] * inverse_terms[0]]
    for level_index in range(1, levels):
        forward.append(
            (values[:, level_index] + diff_rates[:, level_index - 1] * forward[-1])
            * inverse_terms[level_index]
        )
    solution = [None] * levels
    solution[levels - 1] = forward[levels - 1]
    for level_index in range(levels - 2, -1, -1):
        solution[level_index] = (
            forward[level_index] - thomas_coefficients[level_index] * solution[level_index + 1]
        )
    return jnp.stack(solution, 1)


def per_device(members, control, u_courant, v_courant, diffusion, group_scale, group_of, wet):
    levels = members.shape[1]
    columns = members.shape[2]
    realisation_total = members.shape[0] * lax.axis_size("mem")
    group_ids = jnp.arange(group_scale.shape[0], dtype=jnp.int32)
    spread_multiplier = jnp.sum(
        jnp.where(group_of[:, None] == group_ids[None, :], group_scale[None, :], 0.0), 1
    )
    wet_float = wet.astype(jnp.float32)
    recentre_shift, u_low, wet_low, wet_high = member_allreduce(members, u_courant, wet, control)
    salinity = members + recentre_shift[None]
    east_courant = jnp.concatenate([u_low[:, None], u_courant], 1)
    wet_ext = jnp.concatenate([wet_low, wet, wet_high], 0).astype(jnp.float32)
    eastern_face_open = wet_ext[0 : columns + 1] * wet_ext[1 : columns + 2]
    tridiag_terms = factor(spread_multiplier[:, None, None, None] * diffusion[None])
    for time_step_index in range(2):
        padded = with_halo(salinity, (("tile", 2),), 2)
        salinity = solve_columns(
            advect(padded, east_courant, eastern_face_open, v_courant, wet_float), tridiag_terms
        )
    return salinity


def solution(mesh):
    placed = (
        P("mem", None, "tile", None),
        P(None, "tile", None),
        P(None, "tile", None),
        P(None, "tile", None),
        P(None, "tile", None),
        P(),
        P("mem"),
        P("tile", None),
    )
    return jax.shard_map(
        per_device,
        mesh=mesh,
        in_specs=placed,
        out_specs=P("mem", None, "tile", None),
        check_vma=False,
    )
```

```python
import functools

import jax
import jax.numpy as jnp
from jax import lax
from jax.experimental import pallas as pl
from jax.experimental.pallas import tpu as pltpu
from jax.sharding import PartitionSpec as P

MESH_ID = pl.DeviceIdType.MESH


def allreduce_kernel(
    n, members_ref, u_ref, wet_ref, c_ref, o_ref, ulow_ref, wlow_ref, whigh_ref,
    x_ref, recv, red, gath, uedge, wedge, ubuf, wbuf, s1, r1, s2, r2, se, re, s1b, r1b, s2b, r2b,
):
    me = lax.axis_index("mem")
    tile = lax.axis_index("tile")
    tiles = lax.axis_size("tile")
    has_left = tile > 0
    has_right = tile < tiles - 1
    rows = x_ref.shape[0] // n
    columns = u_ref.shape[1]
    half = n // 2
    ring_y, ring_z = me // 2, lax.rem(me, 2)
    offsets = [(2, 1), (2, 0), (1, 1), (3, 1), (1, 0), (3, 0), (0, 1)]
    peers = [lax.rem(ring_y + dy, half) * 2 + lax.rem(ring_z + dz, 2) for dy, dz in offsets]
    barrier = pltpu.get_barrier_semaphore()
    for peer in peers:
        pl.semaphore_signal(barrier, inc=1, device_id=(tile, peer), device_id_type=MESH_ID)

    @pl.when(has_left)
    def _():
        pl.semaphore_signal(barrier, inc=1, device_id=(tile - 1, me), device_id_type=MESH_ID)

    @pl.when(has_right)
    def _():
        pl.semaphore_signal(barrier, inc=1, device_id=(tile + 1, me), device_id_type=MESH_ID)

    uedge[...] = u_ref[:, columns - 1, :]
    wedge[0] = wet_ref[pl.ds(columns - 1, 1), :]
    wedge[1] = wet_ref[pl.ds(0, 1), :]

    def local_sum(k, carry):
        level = members_ref[0, k]
        for m in range(1, members_ref.shape[0]):
            level = level + members_ref[m, k]
        x_ref[k] = level
        return carry

    lax.fori_loop(0, x_ref.shape[0], local_sum, 0)
    pl.semaphore_wait(
        barrier, n - 1 + has_left.astype(jnp.int32) + has_right.astype(jnp.int32)
    )

    def copy_to(src, dst, send, recv_sem, device):
        return pltpu.make_async_remote_copy(
            src_ref=src,
            dst_ref=dst,
            send_sem=send,
            recv_sem=recv_sem,
            device_id=device,
            device_id_type=MESH_ID,
        )

    right_copies = [
        copy_to(uedge, ubuf, se.at[0], re.at[0], (tile + 1, me)),
        copy_to(wedge.at[0], wbuf.at[0], se.at[1], re.at[1], (tile + 1, me)),
    ]
    left_copy = copy_to(wedge.at[1], wbuf.at[1], se.at[2], re.at[2], (tile - 1, me))

    @pl.when(has_right)
    def _():
        for copy in right_copies:
            copy.start()

    @pl.when(has_left)
    def _():
        left_copy.start()

    split = rows // 2
    scale = 1.0 / (n * members_ref.shape[0])
    sems = [(s1, r1, s2, r2), (s1b, r1b, s2b, r2b)]
    firsts = []
    for part, (sa, ra, _, _) in enumerate(sems):
        lo = part * split
        for peer in peers:
            firsts.append(copy_to(
                x_ref.at[pl.ds(peer * rows + lo, split)], recv.at[me, pl.ds(lo, split)],
                sa.at[peer], ra.at[me], (tile, peer),
            ))
    for copy in firsts:
        copy.start()
    seconds = []
    for part, (sa, ra, sb, rb) in enumerate(sems):
        lo = part * split
        for peer in peers:
            copy_to(
                x_ref.at[pl.ds(lo, split)], recv.at[peer, pl.ds(lo, split)],
                sa.at[peer], ra.at[peer], (tile, peer),
            ).wait_recv()
        acc = x_ref[pl.ds(me * rows + lo, split)]
        for peer in peers:
            acc = acc + recv[peer, pl.ds(lo, split)]
        red[pl.ds(lo, split)] = acc
        own = pl.ds(me * rows + lo, split)
        o_ref[own] = c_ref[own] - acc * scale
        batch = [
            copy_to(red.at[pl.ds(lo, split)], gath.at[me, pl.ds(lo, split)], sb.at[peer], rb.at[me], (tile, peer))
            for peer in peers
        ]
        for copy in batch:
            copy.start()
        seconds += batch
    for part, (_, _, sb, rb) in enumerate(sems):
        lo = part * split
        for peer in peers:
            copy_to(
                red.at[pl.ds(lo, split)], gath.at[peer, pl.ds(lo, split)],
                sb.at[peer], rb.at[peer], (tile, peer),
            ).wait_recv()
            rows_here = pl.ds(peer * rows + lo, split)
            o_ref[rows_here] = c_ref[rows_here] - gath[peer, pl.ds(lo, split)] * scale
    for copy in firsts + seconds:
        copy.wait_send()

    @pl.when(has_right)
    def _():
        for copy in right_copies:
            copy.wait_send()

    @pl.when(has_left)
    def _():
        left_copy.wait_send()
        for copy in right_copies:
            copy.wait_recv()
        ulow_ref[...] = ubuf[...]
        wlow_ref[...] = wbuf[0]

    @pl.when(jnp.logical_not(has_left))
    def _():
        ulow_ref[...] = jnp.zeros_like(ulow_ref)
        wlow_ref[...] = jnp.zeros_like(wlow_ref)

    @pl.when(has_right)
    def _():
        left_copy.wait_recv()
        whigh_ref[...] = wbuf[1]

    @pl.when(jnp.logical_not(has_right))
    def _():
        whigh_ref[...] = jnp.zeros_like(whigh_ref)


def member_allreduce(members, u_courant, wet, control):
    total = jax.ShapeDtypeStruct(members.shape[1:], members.dtype)
    n = lax.axis_size("mem")
    rows = total.shape[0] // n
    chunk = (rows,) + total.shape[1:]
    levels, lanes = u_courant.shape[0], u_courant.shape[2]
    vmem = pl.BlockSpec(memory_space=pltpu.VMEM)
    return pl.pallas_call(
        functools.partial(allreduce_kernel, n),
        out_shape=(
            jax.ShapeDtypeStruct(total.shape, total.dtype),
            jax.ShapeDtypeStruct((levels, lanes), u_courant.dtype),
            jax.ShapeDtypeStruct((1, lanes), wet.dtype),
            jax.ShapeDtypeStruct((1, lanes), wet.dtype),
        ),
        in_specs=[vmem] * 4,
        out_specs=(vmem,) * 4,
        scratch_shapes=[
            pltpu.VMEM(total.shape, total.dtype),
            pltpu.VMEM((n,) + chunk, total.dtype),
            pltpu.VMEM(chunk, total.dtype),
            pltpu.VMEM((n,) + chunk, total.dtype),
            pltpu.VMEM((levels, lanes), u_courant.dtype),
            pltpu.VMEM((2, 1, lanes), wet.dtype),
            pltpu.VMEM((levels, lanes), u_courant.dtype),
            pltpu.VMEM((2, 1, lanes), wet.dtype),
            pltpu.SemaphoreType.DMA((n,)),
            pltpu.SemaphoreType.DMA((n,)),
            pltpu.SemaphoreType.DMA((n,)),
            pltpu.SemaphoreType.DMA((n,)),
            pltpu.SemaphoreType.DMA((3,)),
            pltpu.SemaphoreType.DMA((3,)),
            pltpu.SemaphoreType.DMA((n,)),
            pltpu.SemaphoreType.DMA((n,)),
            pltpu.SemaphoreType.DMA((n,)),
            pltpu.SemaphoreType.DMA((n,)),
        ],
        compiler_params=pltpu.CompilerParams(collective_id=0, has_side_effects=True),
    )(members, u_courant, wet, control)


def with_halo(block, sides, width):
    for axis, dim in sides:
        count = lax.axis_size(axis)
        forward = [(i, i + 1) for i in range(count - 1)]
        backward = [(target, source) for source, target in forward]
        low = lax.ppermute(
            lax.slice_in_dim(block, block.shape[dim] - width, None, axis=dim), axis, forward
        )
        high = lax.ppermute(lax.slice_in_dim(block, 0, width, axis=dim), axis, backward)
        block = jnp.concatenate([low, block, high], axis=dim)
    return block


def minmod(first_diff, second_diff):
    return (
        0.5
        * (jnp.sign(first_diff) + jnp.sign(second_diff))
        * jnp.minimum(jnp.abs(first_diff), jnp.abs(second_diff))
    )


def face_flux(courant, far_back, near_back, near_ahead, far_ahead, open_face):
    positive = courant > 0.0
    upwind = jnp.where(positive, near_back, near_ahead)
    side_diff = jnp.where(positive, near_back - far_back, far_ahead - near_ahead)
    limited = minmod(near_ahead - near_back, side_diff)
    magnitude = jnp.abs(courant)
    return (courant * upwind + 0.5 * magnitude * (1.0 - magnitude) * limited) * open_face


def advect(salinity, east_courant, eastern_face_open, north_courant, wet_cells):
    columns = salinity.shape[2]
    east_flux = face_flux(
        east_courant,
        salinity[:, :, 0 : columns - 3],
        salinity[:, :, 1 : columns - 2],
        salinity[:, :, 2 : columns - 1],
        salinity[:, :, 3:columns],
        eastern_face_open,
    )
    interior = salinity[:, :, 2 : columns - 2]
    zero_col = jnp.zeros_like(interior[..., :1])
    lower_cells = jnp.concatenate([zero_col, interior[..., :-1]], -1)
    upper_cells = jnp.concatenate([interior[..., 1:], zero_col], -1)
    upper_two = jnp.concatenate([interior[..., 2:], zero_col, zero_col], -1)
    wet_next = jnp.concatenate([wet_cells[:, 1:], jnp.zeros_like(wet_cells[:, :1])], -1)
    poleward_transport = face_flux(
        north_courant, lower_cells, interior, upper_cells, upper_two, wet_cells * wet_next
    )
    equatorward_transport = jnp.concatenate([zero_col, poleward_transport[..., :-1]], -1)
    return (
        interior
        - (east_flux[:, :, 1:] - east_flux[:, :, :-1])
        - (poleward_transport - equatorward_transport)
    )


def factor(diff_rates):
    levels = diff_rates.shape[1] + 1
    thomas_coefficients = []
    inverse_terms = []
    previous = None
    for level_index in range(levels):
        diagonal = jnp.ones_like(diff_rates[:, 0])
        if level_index > 0:
            diagonal = diagonal + diff_rates[:, level_index - 1]
        if level_index < levels - 1:
            diagonal = diagonal + diff_rates[:, level_index]
        if level_index > 0:
            diagonal = diagonal + diff_rates[:, level_index - 1] * previous
        inverse_den = 1.0 / diagonal
        inverse_terms.append(inverse_den)
        if level_index < levels - 1:
            previous = -diff_rates[:, level_index] * inverse_den
            thomas_coefficients.append(previous)
    return (diff_rates, thomas_coefficients, inverse_terms)


def solve_columns(values, tridiag_terms):
    diff_rates, thomas_coefficients, inverse_terms = tridiag_terms
    levels = values.shape[1]
    forward = [values[:, 0] * inverse_terms[0]]
    for level_index in range(1, levels):
        forward.append(
            (values[:, level_index] + diff_rates[:, level_index - 1] * forward[-1])
            * inverse_terms[level_index]
        )
    solution = [None] * levels
    solution[levels - 1] = forward[levels - 1]
    for level_index in range(levels - 2, -1, -1):
        solution[level_index] = (
            forward[level_index] - thomas_coefficients[level_index] * solution[level_index + 1]
        )
    return jnp.stack(solution, 1)


def per_device(members, control, u_courant, v_courant, diffusion, group_scale, group_of, wet):
    levels = members.shape[1]
    columns = members.shape[2]
    realisation_total = members.shape[0] * lax.axis_size("mem")
    group_ids = jnp.arange(group_scale.shape[0], dtype=jnp.int32)
    spread_multiplier = jnp.sum(
        jnp.where(group_of[:, None] == group_ids[None, :], group_scale[None, :], 0.0), 1
    )
    wet_float = wet.astype(jnp.float32)
    recentre_shift, u_low, wet_low, wet_high = member_allreduce(members, u_courant, wet, control)
    salinity = members + recentre_shift[None]
    east_courant = jnp.concatenate([u_low[:, None], u_courant], 1)
    wet_ext = jnp.concatenate([wet_low, wet, wet_high], 0).astype(jnp.float32)
    eastern_face_open = wet_ext[0 : columns + 1] * wet_ext[1 : columns + 2]
    tridiag_terms = factor(spread_multiplier[:, None, None, None] * diffusion[None])
    for time_step_index in range(2):
        padded = with_halo(salinity, (("tile", 2),), 2)
        salinity = solve_columns(
            advect(padded, east_courant, eastern_face_open, v_courant, wet_float), tridiag_terms
        )
    return salinity


def solution(mesh):
    placed = (
        P("mem", None, "tile", None),
        P(None, "tile", None),
        P(None, "tile", None),
        P(None, "tile", None),
        P(None, "tile", None),
        P(),
        P("mem"),
        P("tile", None),
    )
    return jax.shard_map(
        per_device,
        mesh=mesh,
        in_specs=placed,
        out_specs=P("mem", None, "tile", None),
        check_vma=False,
    )
```

```python
import functools

import jax
import jax.numpy as jnp
from jax import lax
from jax.experimental import pallas as pl
from jax.experimental.pallas import tpu as pltpu
from jax.sharding import PartitionSpec as P

MESH_ID = pl.DeviceIdType.MESH
PIECES = 4


def allreduce_kernel(
    n, members_ref, u_ref, wet_ref, c_ref, o_ref, ulow_ref, wlow_ref, whigh_ref,
    x_ref, recv, red, gath, uedge, wedge, ubuf, wbuf, se, re, *piece_sems,
):
    me = lax.axis_index("mem")
    tile = lax.axis_index("tile")
    tiles = lax.axis_size("tile")
    has_left = tile > 0
    has_right = tile < tiles - 1
    rows = x_ref.shape[0] // n
    columns = u_ref.shape[1]
    half = n // 2
    ring_y, ring_z = me // 2, lax.rem(me, 2)
    offsets = [(2, 1), (2, 0), (1, 1), (3, 1), (1, 0), (3, 0), (0, 1)]
    peers = [lax.rem(ring_y + dy, half) * 2 + lax.rem(ring_z + dz, 2) for dy, dz in offsets]
    barrier = pltpu.get_barrier_semaphore()
    for peer in peers:
        pl.semaphore_signal(barrier, inc=1, device_id=(tile, peer), device_id_type=MESH_ID)

    @pl.when(has_left)
    def _():
        pl.semaphore_signal(barrier, inc=1, device_id=(tile - 1, me), device_id_type=MESH_ID)

    @pl.when(has_right)
    def _():
        pl.semaphore_signal(barrier, inc=1, device_id=(tile + 1, me), device_id_type=MESH_ID)

    uedge[...] = u_ref[:, columns - 1, :]
    wedge[0] = wet_ref[pl.ds(columns - 1, 1), :]
    wedge[1] = wet_ref[pl.ds(0, 1), :]

    def local_sum(k, carry):
        level = members_ref[0, k]
        for m in range(1, members_ref.shape[0]):
            level = level + members_ref[m, k]
        x_ref[k] = level
        return carry

    lax.fori_loop(0, x_ref.shape[0], local_sum, 0)
    pl.semaphore_wait(
        barrier, n - 1 + has_left.astype(jnp.int32) + has_right.astype(jnp.int32)
    )

    def copy_to(src, dst, send, recv_sem, device):
        return pltpu.make_async_remote_copy(
            src_ref=src,
            dst_ref=dst,
            send_sem=send,
            recv_sem=recv_sem,
            device_id=device,
            device_id_type=MESH_ID,
        )

    right_copies = [
        copy_to(uedge, ubuf, se.at[0], re.at[0], (tile + 1, me)),
        copy_to(wedge.at[0], wbuf.at[0], se.at[1], re.at[1], (tile + 1, me)),
    ]
    left_copy = copy_to(wedge.at[1], wbuf.at[1], se.at[2], re.at[2], (tile - 1, me))

    @pl.when(has_right)
    def _():
        for copy in right_copies:
            copy.start()

    @pl.when(has_left)
    def _():
        left_copy.start()

    split = rows // PIECES
    scale = 1.0 / (n * members_ref.shape[0])
    sems = [piece_sems[4 * i : 4 * i + 4] for i in range(PIECES)]
    firsts = []
    for part, (sa, ra, _, _) in enumerate(sems):
        lo = part * split
        for peer in peers:
            firsts.append(copy_to(
                x_ref.at[pl.ds(peer * rows + lo, split)], recv.at[me, pl.ds(lo, split)],
                sa.at[peer], ra.at[me], (tile, peer),
            ))
    for copy in firsts:
        copy.start()
    seconds = []
    for part, (sa, ra, sb, rb) in enumerate(sems):
        lo = part * split
        for peer in peers:
            copy_to(
                x_ref.at[pl.ds(lo, split)], recv.at[peer, pl.ds(lo, split)],
                sa.at[peer], ra.at[peer], (tile, peer),
            ).wait_recv()
        acc = x_ref[pl.ds(me * rows + lo, split)]
        for peer in peers:
            acc = acc + recv[peer, pl.ds(lo, split)]
        red[pl.ds(lo, split)] = acc
        own = pl.ds(me * rows + lo, split)
        o_ref[own] = c_ref[own] - acc * scale
        batch = [
            copy_to(red.at[pl.ds(lo, split)], gath.at[me, pl.ds(lo, split)], sb.at[peer], rb.at[me], (tile, peer))
            for peer in peers
        ]
        for copy in batch:
            copy.start()
        seconds += batch
    for part, (_, _, sb, rb) in enumerate(sems):
        lo = part * split
        for peer in peers:
            copy_to(
                red.at[pl.ds(lo, split)], gath.at[peer, pl.ds(lo, split)],
                sb.at[peer], rb.at[peer], (tile, peer),
            ).wait_recv()
            rows_here = pl.ds(peer * rows + lo, split)
            o_ref[rows_here] = c_ref[rows_here] - gath[peer, pl.ds(lo, split)] * scale
    for copy in firsts + seconds:
        copy.wait_send()

    @pl.when(has_right)
    def _():
        for copy in right_copies:
            copy.wait_send()

    @pl.when(has_left)
    def _():
        left_copy.wait_send()
        for copy in right_copies:
            copy.wait_recv()
        ulow_ref[...] = ubuf[...]
        wlow_ref[...] = wbuf[0]

    @pl.when(jnp.logical_not(has_left))
    def _():
        ulow_ref[...] = jnp.zeros_like(ulow_ref)
        wlow_ref[...] = jnp.zeros_like(wlow_ref)

    @pl.when(has_right)
    def _():
        left_copy.wait_recv()
        whigh_ref[...] = wbuf[1]

    @pl.when(jnp.logical_not(has_right))
    def _():
        whigh_ref[...] = jnp.zeros_like(whigh_ref)


def member_allreduce(members, u_courant, wet, control):
    total = jax.ShapeDtypeStruct(members.shape[1:], members.dtype)
    n = lax.axis_size("mem")
    rows = total.shape[0] // n
    chunk = (rows,) + total.shape[1:]
    levels, lanes = u_courant.shape[0], u_courant.shape[2]
    vmem = pl.BlockSpec(memory_space=pltpu.VMEM)
    return pl.pallas_call(
        functools.partial(allreduce_kernel, n),
        out_shape=(
            jax.ShapeDtypeStruct(total.shape, total.dtype),
            jax.ShapeDtypeStruct((levels, lanes), u_courant.dtype),
            jax.ShapeDtypeStruct((1, lanes), wet.dtype),
            jax.ShapeDtypeStruct((1, lanes), wet.dtype),
        ),
        in_specs=[vmem] * 4,
        out_specs=(vmem,) * 4,
        scratch_shapes=[
            pltpu.VMEM(total.shape, total.dtype),
            pltpu.VMEM((n,) + chunk, total.dtype),
            pltpu.VMEM(chunk, total.dtype),
            pltpu.VMEM((n,) + chunk, total.dtype),
            pltpu.VMEM((levels, lanes), u_courant.dtype),
            pltpu.VMEM((2, 1, lanes), wet.dtype),
            pltpu.VMEM((levels, lanes), u_courant.dtype),
            pltpu.VMEM((2, 1, lanes), wet.dtype),
            pltpu.SemaphoreType.DMA((3,)),
            pltpu.SemaphoreType.DMA((3,)),
        ]
        + [pltpu.SemaphoreType.DMA((n,))] * (4 * PIECES),
        compiler_params=pltpu.CompilerParams(collective_id=0, has_side_effects=True),
    )(members, u_courant, wet, control)


def with_halo(block, sides, width):
    for axis, dim in sides:
        count = lax.axis_size(axis)
        forward = [(i, i + 1) for i in range(count - 1)]
        backward = [(target, source) for source, target in forward]
        low = lax.ppermute(
            lax.slice_in_dim(block, block.shape[dim] - width, None, axis=dim), axis, forward
        )
        high = lax.ppermute(lax.slice_in_dim(block, 0, width, axis=dim), axis, backward)
        block = jnp.concatenate([low, block, high], axis=dim)
    return block


def minmod(first_diff, second_diff):
    return (
        0.5
        * (jnp.sign(first_diff) + jnp.sign(second_diff))
        * jnp.minimum(jnp.abs(first_diff), jnp.abs(second_diff))
    )


def face_flux(courant, far_back, near_back, near_ahead, far_ahead, open_face):
    positive = courant > 0.0
    upwind = jnp.where(positive, near_back, near_ahead)
    side_diff = jnp.where(positive, near_back - far_back, far_ahead - near_ahead)
    limited = minmod(near_ahead - near_back, side_diff)
    magnitude = jnp.abs(courant)
    return (courant * upwind + 0.5 * magnitude * (1.0 - magnitude) * limited) * open_face


def advect(salinity, east_courant, eastern_face_open, north_courant, wet_cells):
    columns = salinity.shape[2]
    east_flux = face_flux(
        east_courant,
        salinity[:, :, 0 : columns - 3],
        salinity[:, :, 1 : columns - 2],
        salinity[:, :, 2 : columns - 1],
        salinity[:, :, 3:columns],
        eastern_face_open,
    )
    interior = salinity[:, :, 2 : columns - 2]
    zero_col = jnp.zeros_like(interior[..., :1])
    lower_cells = jnp.concatenate([zero_col, interior[..., :-1]], -1)
    upper_cells = jnp.concatenate([interior[..., 1:], zero_col], -1)
    upper_two = jnp.concatenate([interior[..., 2:], zero_col, zero_col], -1)
    wet_next = jnp.concatenate([wet_cells[:, 1:], jnp.zeros_like(wet_cells[:, :1])], -1)
    poleward_transport = face_flux(
        north_courant, lower_cells, interior, upper_cells, upper_two, wet_cells * wet_next
    )
    equatorward_transport = jnp.concatenate([zero_col, poleward_transport[..., :-1]], -1)
    return (
        interior
        - (east_flux[:, :, 1:] - east_flux[:, :, :-1])
        - (poleward_transport - equatorward_transport)
    )


def factor(diff_rates):
    levels = diff_rates.shape[1] + 1
    thomas_coefficients = []
    inverse_terms = []
    previous = None
    for level_index in range(levels):
        diagonal = jnp.ones_like(diff_rates[:, 0])
        if level_index > 0:
            diagonal = diagonal + diff_rates[:, level_index - 1]
        if level_index < levels - 1:
            diagonal = diagonal + diff_rates[:, level_index]
        if level_index > 0:
            diagonal = diagonal + diff_rates[:, level_index - 1] * previous
        inverse_den = 1.0 / diagonal
        inverse_terms.append(inverse_den)
        if level_index < levels - 1:
            previous = -diff_rates[:, level_index] * inverse_den
            thomas_coefficients.append(previous)
    return (diff_rates, thomas_coefficients, inverse_terms)


def solve_columns(values, tridiag_terms):
    diff_rates, thomas_coefficients, inverse_terms = tridiag_terms
    levels = values.shape[1]
    forward = [values[:, 0] * inverse_terms[0]]
    for level_index in range(1, levels):
        forward.append(
            (values[:, level_index] + diff_rates[:, level_index - 1] * forward[-1])
            * inverse_terms[level_index]
        )
    solution = [None] * levels
    solution[levels - 1] = forward[levels - 1]
    for level_index in range(levels - 2, -1, -1):
        solution[level_index] = (
            forward[level_index] - thomas_coefficients[level_index] * solution[level_index + 1]
        )
    return jnp.stack(solution, 1)


def per_device(members, control, u_courant, v_courant, diffusion, group_scale, group_of, wet):
    levels = members.shape[1]
    columns = members.shape[2]
    realisation_total = members.shape[0] * lax.axis_size("mem")
    group_ids = jnp.arange(group_scale.shape[0], dtype=jnp.int32)
    spread_multiplier = jnp.sum(
        jnp.where(group_of[:, None] == group_ids[None, :], group_scale[None, :], 0.0), 1
    )
    wet_float = wet.astype(jnp.float32)
    recentre_shift, u_low, wet_low, wet_high = member_allreduce(members, u_courant, wet, control)
    salinity = members + recentre_shift[None]
    east_courant = jnp.concatenate([u_low[:, None], u_courant], 1)
    wet_ext = jnp.concatenate([wet_low, wet, wet_high], 0).astype(jnp.float32)
    eastern_face_open = wet_ext[0 : columns + 1] * wet_ext[1 : columns + 2]
    tridiag_terms = factor(spread_multiplier[:, None, None, None] * diffusion[None])
    for time_step_index in range(2):
        padded = with_halo(salinity, (("tile", 2),), 2)
        salinity = solve_columns(
            advect(padded, east_courant, eastern_face_open, v_courant, wet_float), tridiag_terms
        )
    return salinity


def solution(mesh):
    placed = (
        P("mem", None, "tile", None),
        P(None, "tile", None),
        P(None, "tile", None),
        P(None, "tile", None),
        P(None, "tile", None),
        P(),
        P("mem"),
        P("tile", None),
    )
    return jax.shard_map(
        per_device,
        mesh=mesh,
        in_specs=placed,
        out_specs=P("mem", None, "tile", None),
        check_vma=False,
    )
```

```python
import functools

import jax
import jax.numpy as jnp
from jax import lax
from jax.experimental import pallas as pl
from jax.experimental.pallas import tpu as pltpu
from jax.sharding import PartitionSpec as P

MESH_ID = pl.DeviceIdType.MESH


def allreduce_kernel(
    n, members_ref, u_ref, wet_ref, c_ref, o_ref, ulow_ref, wlow_ref, whigh_ref,
    x_ref, recv, red, gath, uedge, wedge, ubuf, wbuf, s1, r1, s2, r2, se, re, s1b, r1b, s2b, r2b,
):
    me = lax.axis_index("mem")
    tile = lax.axis_index("tile")
    tiles = lax.axis_size("tile")
    has_left = tile > 0
    has_right = tile < tiles - 1
    rows = x_ref.shape[0] // n
    columns = u_ref.shape[1]
    half = n // 2
    ring_y, ring_z = me // 2, lax.rem(me, 2)
    offsets = [(2, 1), (2, 0), (1, 1), (3, 1), (1, 0), (3, 0), (0, 1)]
    peers = [lax.rem(ring_y + dy, half) * 2 + lax.rem(ring_z + dz, 2) for dy, dz in offsets]
    barrier = pltpu.get_barrier_semaphore()
    for peer in peers:
        pl.semaphore_signal(barrier, inc=1, device_id=(tile, peer), device_id_type=MESH_ID)

    @pl.when(has_left)
    def _():
        pl.semaphore_signal(barrier, inc=1, device_id=(tile - 1, me), device_id_type=MESH_ID)

    @pl.when(has_right)
    def _():
        pl.semaphore_signal(barrier, inc=1, device_id=(tile + 1, me), device_id_type=MESH_ID)

    uedge[...] = u_ref[:, columns - 1, :]
    wedge[0] = wet_ref[pl.ds(columns - 1, 1), :]
    wedge[1] = wet_ref[pl.ds(0, 1), :]

    def local_sum(k, carry):
        level = members_ref[0, k]
        for m in range(1, members_ref.shape[0]):
            level = level + members_ref[m, k]
        x_ref[k] = level
        return carry

    lax.fori_loop(0, x_ref.shape[0], local_sum, 0)
    pl.semaphore_wait(
        barrier, n - 1 + has_left.astype(jnp.int32) + has_right.astype(jnp.int32)
    )

    def copy_to(src, dst, send, recv_sem, device):
        return pltpu.make_async_remote_copy(
            src_ref=src,
            dst_ref=dst,
            send_sem=send,
            recv_sem=recv_sem,
            device_id=device,
            device_id_type=MESH_ID,
        )

    right_copies = [
        copy_to(uedge, ubuf, se.at[0], re.at[0], (tile + 1, me)),
        copy_to(wedge.at[0], wbuf.at[0], se.at[1], re.at[1], (tile + 1, me)),
    ]
    left_copy = copy_to(wedge.at[1], wbuf.at[1], se.at[2], re.at[2], (tile - 1, me))

    @pl.when(has_right)
    def _():
        for copy in right_copies:
            copy.start()

    @pl.when(has_left)
    def _():
        left_copy.start()

    split = rows // 2
    scale = 1.0 / (n * members_ref.shape[0])
    sems = [(s1, r1, s2, r2), (s1b, r1b, s2b, r2b)]
    firsts = []
    for peer in peers:
        for part, (sa, ra, _, _) in enumerate(sems):
            lo = part * split
            firsts.append(copy_to(
                x_ref.at[pl.ds(peer * rows + lo, split)], recv.at[me, pl.ds(lo, split)],
                sa.at[peer], ra.at[me], (tile, peer),
            ))
    for copy in firsts:
        copy.start()
    seconds = []
    for part, (sa, ra, sb, rb) in enumerate(sems):
        lo = part * split
        for peer in peers:
            copy_to(
                x_ref.at[pl.ds(lo, split)], recv.at[peer, pl.ds(lo, split)],
                sa.at[peer], ra.at[peer], (tile, peer),
            ).wait_recv()
        acc = x_ref[pl.ds(me * rows + lo, split)]
        for peer in peers:
            acc = acc + recv[peer, pl.ds(lo, split)]
        red[pl.ds(lo, split)] = acc
        own = pl.ds(me * rows + lo, split)
        o_ref[own] = c_ref[own] - acc * scale
        batch = [
            copy_to(red.at[pl.ds(lo, split)], gath.at[me, pl.ds(lo, split)], sb.at[peer], rb.at[me], (tile, peer))
            for peer in peers
        ]
        for copy in batch:
            copy.start()
        seconds += batch
    for part, (_, _, sb, rb) in enumerate(sems):
        lo = part * split
        for peer in peers:
            copy_to(
                red.at[pl.ds(lo, split)], gath.at[peer, pl.ds(lo, split)],
                sb.at[peer], rb.at[peer], (tile, peer),
            ).wait_recv()
            rows_here = pl.ds(peer * rows + lo, split)
            o_ref[rows_here] = c_ref[rows_here] - gath[peer, pl.ds(lo, split)] * scale
    for copy in firsts + seconds:
        copy.wait_send()

    @pl.when(has_right)
    def _():
        for copy in right_copies:
            copy.wait_send()

    @pl.when(has_left)
    def _():
        left_copy.wait_send()
        for copy in right_copies:
            copy.wait_recv()
        ulow_ref[...] = ubuf[...]
        wlow_ref[...] = wbuf[0]

    @pl.when(jnp.logical_not(has_left))
    def _():
        ulow_ref[...] = jnp.zeros_like(ulow_ref)
        wlow_ref[...] = jnp.zeros_like(wlow_ref)

    @pl.when(has_right)
    def _():
        left_copy.wait_recv()
        whigh_ref[...] = wbuf[1]

    @pl.when(jnp.logical_not(has_right))
    def _():
        whigh_ref[...] = jnp.zeros_like(whigh_ref)


def member_allreduce(members, u_courant, wet, control):
    total = jax.ShapeDtypeStruct(members.shape[1:], members.dtype)
    n = lax.axis_size("mem")
    rows = total.shape[0] // n
    chunk = (rows,) + total.shape[1:]
    levels, lanes = u_courant.shape[0], u_courant.shape[2]
    vmem = pl.BlockSpec(memory_space=pltpu.VMEM)
    return pl.pallas_call(
        functools.partial(allreduce_kernel, n),
        out_shape=(
            jax.ShapeDtypeStruct(total.shape, total.dtype),
            jax.ShapeDtypeStruct((levels, lanes), u_courant.dtype),
            jax.ShapeDtypeStruct((1, lanes), wet.dtype),
            jax.ShapeDtypeStruct((1, lanes), wet.dtype),
        ),
        in_specs=[vmem] * 4,
        out_specs=(vmem,) * 4,
        scratch_shapes=[
            pltpu.VMEM(total.shape, total.dtype),
            pltpu.VMEM((n,) + chunk, total.dtype),
            pltpu.VMEM(chunk, total.dtype),
            pltpu.VMEM((n,) + chunk, total.dtype),
            pltpu.VMEM((levels, lanes), u_courant.dtype),
            pltpu.VMEM((2, 1, lanes), wet.dtype),
            pltpu.VMEM((levels, lanes), u_courant.dtype),
            pltpu.VMEM((2, 1, lanes), wet.dtype),
            pltpu.SemaphoreType.DMA((n,)),
            pltpu.SemaphoreType.DMA((n,)),
            pltpu.SemaphoreType.DMA((n,)),
            pltpu.SemaphoreType.DMA((n,)),
            pltpu.SemaphoreType.DMA((3,)),
            pltpu.SemaphoreType.DMA((3,)),
            pltpu.SemaphoreType.DMA((n,)),
            pltpu.SemaphoreType.DMA((n,)),
            pltpu.SemaphoreType.DMA((n,)),
            pltpu.SemaphoreType.DMA((n,)),
        ],
        compiler_params=pltpu.CompilerParams(collective_id=0, has_side_effects=True),
    )(members, u_courant, wet, control)


def with_halo(block, sides, width):
    for axis, dim in sides:
        count = lax.axis_size(axis)
        forward = [(i, i + 1) for i in range(count - 1)]
        backward = [(target, source) for source, target in forward]
        low = lax.ppermute(
            lax.slice_in_dim(block, block.shape[dim] - width, None, axis=dim), axis, forward
        )
        high = lax.ppermute(lax.slice_in_dim(block, 0, width, axis=dim), axis, backward)
        block = jnp.concatenate([low, block, high], axis=dim)
    return block


def minmod(first_diff, second_diff):
    return (
        0.5
        * (jnp.sign(first_diff) + jnp.sign(second_diff))
        * jnp.minimum(jnp.abs(first_diff), jnp.abs(second_diff))
    )


def face_flux(courant, far_back, near_back, near_ahead, far_ahead, open_face):
    positive = courant > 0.0
    upwind = jnp.where(positive, near_back, near_ahead)
    side_diff = jnp.where(positive, near_back - far_back, far_ahead - near_ahead)
    limited = minmod(near_ahead - near_back, side_diff)
    magnitude = jnp.abs(courant)
    return (courant * upwind + 0.5 * magnitude * (1.0 - magnitude) * limited) * open_face


def advect(salinity, east_courant, eastern_face_open, north_courant, wet_cells):
    columns = salinity.shape[2]
    east_flux = face_flux(
        east_courant,
        salinity[:, :, 0 : columns - 3],
        salinity[:, :, 1 : columns - 2],
        salinity[:, :, 2 : columns - 1],
        salinity[:, :, 3:columns],
        eastern_face_open,
    )
    interior = salinity[:, :, 2 : columns - 2]
    zero_col = jnp.zeros_like(interior[..., :1])
    lower_cells = jnp.concatenate([zero_col, interior[..., :-1]], -1)
    upper_cells = jnp.concatenate([interior[..., 1:], zero_col], -1)
    upper_two = jnp.concatenate([interior[..., 2:], zero_col, zero_col], -1)
    wet_next = jnp.concatenate([wet_cells[:, 1:], jnp.zeros_like(wet_cells[:, :1])], -1)
    poleward_transport = face_flux(
        north_courant, lower_cells, interior, upper_cells, upper_two, wet_cells * wet_next
    )
    equatorward_transport = jnp.concatenate([zero_col, poleward_transport[..., :-1]], -1)
    return (
        interior
        - (east_flux[:, :, 1:] - east_flux[:, :, :-1])
        - (poleward_transport - equatorward_transport)
    )


def factor(diff_rates):
    levels = diff_rates.shape[1] + 1
    thomas_coefficients = []
    inverse_terms = []
    previous = None
    for level_index in range(levels):
        diagonal = jnp.ones_like(diff_rates[:, 0])
        if level_index > 0:
            diagonal = diagonal + diff_rates[:, level_index - 1]
        if level_index < levels - 1:
            diagonal = diagonal + diff_rates[:, level_index]
        if level_index > 0:
            diagonal = diagonal + diff_rates[:, level_index - 1] * previous
        inverse_den = 1.0 / diagonal
        inverse_terms.append(inverse_den)
        if level_index < levels - 1:
            previous = -diff_rates[:, level_index] * inverse_den
            thomas_coefficients.append(previous)
    return (diff_rates, thomas_coefficients, inverse_terms)


def solve_columns(values, tridiag_terms):
    diff_rates, thomas_coefficients, inverse_terms = tridiag_terms
    levels = values.shape[1]
    forward = [values[:, 0] * inverse_terms[0]]
    for level_index in range(1, levels):
        forward.append(
            (values[:, level_index] + diff_rates[:, level_index - 1] * forward[-1])
            * inverse_terms[level_index]
        )
    solution = [None] * levels
    solution[levels - 1] = forward[levels - 1]
    for level_index in range(levels - 2, -1, -1):
        solution[level_index] = (
            forward[level_index] - thomas_coefficients[level_index] * solution[level_index + 1]
        )
    return jnp.stack(solution, 1)


def per_device(members, control, u_courant, v_courant, diffusion, group_scale, group_of, wet):
    levels = members.shape[1]
    columns = members.shape[2]
    realisation_total = members.shape[0] * lax.axis_size("mem")
    group_ids = jnp.arange(group_scale.shape[0], dtype=jnp.int32)
    spread_multiplier = jnp.sum(
        jnp.where(group_of[:, None] == group_ids[None, :], group_scale[None, :], 0.0), 1
    )
    wet_float = wet.astype(jnp.float32)
    recentre_shift, u_low, wet_low, wet_high = member_allreduce(members, u_courant, wet, control)
    salinity = members + recentre_shift[None]
    east_courant = jnp.concatenate([u_low[:, None], u_courant], 1)
    wet_ext = jnp.concatenate([wet_low, wet, wet_high], 0).astype(jnp.float32)
    eastern_face_open = wet_ext[0 : columns + 1] * wet_ext[1 : columns + 2]
    tridiag_terms = factor(spread_multiplier[:, None, None, None] * diffusion[None])
    for time_step_index in range(2):
        padded = with_halo(salinity, (("tile", 2),), 2)
        salinity = solve_columns(
            advect(padded, east_courant, eastern_face_open, v_courant, wet_float), tridiag_terms
        )
    return salinity


def solution(mesh):
    placed = (
        P("mem", None, "tile", None),
        P(None, "tile", None),
        P(None, "tile", None),
        P(None, "tile", None),
        P(None, "tile", None),
        P(),
        P("mem"),
        P("tile", None),
    )
    return jax.shard_map(
        per_device,
        mesh=mesh,
        in_specs=placed,
        out_specs=P("mem", None, "tile", None),
        check_vma=False,
    )
```

```python
import functools

import jax
import jax.numpy as jnp
from jax import lax
from jax.experimental import pallas as pl
from jax.experimental.pallas import tpu as pltpu
from jax.sharding import PartitionSpec as P

MESH_ID = pl.DeviceIdType.MESH


def allreduce_kernel(
    n, members_ref, u_ref, wet_ref, c_ref, o_ref, ulow_ref, wlow_ref, whigh_ref,
    x_ref, recv, red, gath, uedge, wedge, ubuf, wbuf, s1, r1, s2, r2, se, re, s1b, r1b, s2b, r2b,
):
    me = lax.axis_index("mem")
    tile = lax.axis_index("tile")
    tiles = lax.axis_size("tile")
    has_left = tile > 0
    has_right = tile < tiles - 1
    rows = x_ref.shape[0] // n
    columns = u_ref.shape[1]
    half = n // 2
    ring_y, ring_z = me // 2, lax.rem(me, 2)
    offsets = [(2, 1), (2, 0), (1, 1), (3, 1), (1, 0), (3, 0), (0, 1)]
    peers = [lax.rem(ring_y + dy, half) * 2 + lax.rem(ring_z + dz, 2) for dy, dz in offsets]
    barrier = pltpu.get_barrier_semaphore()
    for peer in peers:
        pl.semaphore_signal(barrier, inc=1, device_id=(tile, peer), device_id_type=MESH_ID)

    @pl.when(has_left)
    def _():
        pl.semaphore_signal(barrier, inc=1, device_id=(tile - 1, me), device_id_type=MESH_ID)

    @pl.when(has_right)
    def _():
        pl.semaphore_signal(barrier, inc=1, device_id=(tile + 1, me), device_id_type=MESH_ID)

    uedge[...] = u_ref[:, columns - 1, :]
    wedge[0] = wet_ref[pl.ds(columns - 1, 1), :]
    wedge[1] = wet_ref[pl.ds(0, 1), :]

    def local_sum(k, carry):
        level = members_ref[0, k]
        for m in range(1, members_ref.shape[0]):
            level = level + members_ref[m, k]
        x_ref[k] = level
        return carry

    lax.fori_loop(0, x_ref.shape[0], local_sum, 0)
    pl.semaphore_wait(
        barrier, n - 1 + has_left.astype(jnp.int32) + has_right.astype(jnp.int32)
    )

    def copy_to(src, dst, send, recv_sem, device):
        return pltpu.make_async_remote_copy(
            src_ref=src,
            dst_ref=dst,
            send_sem=send,
            recv_sem=recv_sem,
            device_id=device,
            device_id_type=MESH_ID,
        )

    right_copies = [
        copy_to(uedge, ubuf, se.at[0], re.at[0], (tile + 1, me)),
        copy_to(wedge.at[0], wbuf.at[0], se.at[1], re.at[1], (tile + 1, me)),
    ]
    left_copy = copy_to(wedge.at[1], wbuf.at[1], se.at[2], re.at[2], (tile - 1, me))

    @pl.when(has_right)
    def _():
        for copy in right_copies:
            copy.start()

    @pl.when(has_left)
    def _():
        left_copy.start()

    split = rows // 2
    scale = 1.0 / (n * members_ref.shape[0])
    sems = [(s1, r1, s2, r2), (s1b, r1b, s2b, r2b)]
    firsts = []
    for part, (sa, ra, _, _) in enumerate(sems):
        lo = part * split
        for peer in peers:
            firsts.append(copy_to(
                x_ref.at[pl.ds(peer * rows + lo, split)], recv.at[me, pl.ds(lo, split)],
                sa.at[peer], ra.at[me], (tile, peer),
            ))
    for copy in firsts:
        copy.start()
    seconds = []
    for part, (sa, ra, sb, rb) in enumerate(sems):
        lo = part * split
        for peer in peers:
            copy_to(
                x_ref.at[pl.ds(lo, split)], recv.at[peer, pl.ds(lo, split)],
                sa.at[peer], ra.at[peer], (tile, peer),
            ).wait_recv()
        acc = x_ref[pl.ds(me * rows + lo, split)]
        for peer in peers:
            acc = acc + recv[peer, pl.ds(lo, split)]
        red[pl.ds(lo, split)] = acc
        batch = [
            copy_to(red.at[pl.ds(lo, split)], gath.at[me, pl.ds(lo, split)], sb.at[peer], rb.at[me], (tile, peer))
            for peer in peers
        ]
        for copy in batch:
            copy.start()
        own = pl.ds(me * rows + lo, split)
        o_ref[own] = c_ref[own] - acc * scale
        seconds += batch
    for part, (_, _, sb, rb) in enumerate(sems):
        lo = part * split
        for peer in peers[::-1]:
            copy_to(
                red.at[pl.ds(lo, split)], gath.at[peer, pl.ds(lo, split)],
                sb.at[peer], rb.at[peer], (tile, peer),
            ).wait_recv()
            rows_here = pl.ds(peer * rows + lo, split)
            o_ref[rows_here] = c_ref[rows_here] - gath[peer, pl.ds(lo, split)] * scale
    for copy in firsts + seconds:
        copy.wait_send()

    @pl.when(has_right)
    def _():
        for copy in right_copies:
            copy.wait_send()

    @pl.when(has_left)
    def _():
        left_copy.wait_send()
        for copy in right_copies:
            copy.wait_recv()
        ulow_ref[...] = ubuf[...]
        wlow_ref[...] = wbuf[0]

    @pl.when(jnp.logical_not(has_left))
    def _():
        ulow_ref[...] = jnp.zeros_like(ulow_ref)
        wlow_ref[...] = jnp.zeros_like(wlow_ref)

    @pl.when(has_right)
    def _():
        left_copy.wait_recv()
        whigh_ref[...] = wbuf[1]

    @pl.when(jnp.logical_not(has_right))
    def _():
        whigh_ref[...] = jnp.zeros_like(whigh_ref)


def member_allreduce(members, u_courant, wet, control):
    total = jax.ShapeDtypeStruct(members.shape[1:], members.dtype)
    n = lax.axis_size("mem")
    rows = total.shape[0] // n
    chunk = (rows,) + total.shape[1:]
    levels, lanes = u_courant.shape[0], u_courant.shape[2]
    vmem = pl.BlockSpec(memory_space=pltpu.VMEM)
    return pl.pallas_call(
        functools.partial(allreduce_kernel, n),
        out_shape=(
            jax.ShapeDtypeStruct(total.shape, total.dtype),
            jax.ShapeDtypeStruct((levels, lanes), u_courant.dtype),
            jax.ShapeDtypeStruct((1, lanes), wet.dtype),
            jax.ShapeDtypeStruct((1, lanes), wet.dtype),
        ),
        in_specs=[vmem] * 4,
        out_specs=(vmem,) * 4,
        scratch_shapes=[
            pltpu.VMEM(total.shape, total.dtype),
            pltpu.VMEM((n,) + chunk, total.dtype),
            pltpu.VMEM(chunk, total.dtype),
            pltpu.VMEM((n,) + chunk, total.dtype),
            pltpu.VMEM((levels, lanes), u_courant.dtype),
            pltpu.VMEM((2, 1, lanes), wet.dtype),
            pltpu.VMEM((levels, lanes), u_courant.dtype),
            pltpu.VMEM((2, 1, lanes), wet.dtype),
            pltpu.SemaphoreType.DMA((n,)),
            pltpu.SemaphoreType.DMA((n,)),
            pltpu.SemaphoreType.DMA((n,)),
            pltpu.SemaphoreType.DMA((n,)),
            pltpu.SemaphoreType.DMA((3,)),
            pltpu.SemaphoreType.DMA((3,)),
            pltpu.SemaphoreType.DMA((n,)),
            pltpu.SemaphoreType.DMA((n,)),
            pltpu.SemaphoreType.DMA((n,)),
            pltpu.SemaphoreType.DMA((n,)),
        ],
        compiler_params=pltpu.CompilerParams(collective_id=0, has_side_effects=True),
    )(members, u_courant, wet, control)


def with_halo(block, sides, width):
    for axis, dim in sides:
        count = lax.axis_size(axis)
        forward = [(i, i + 1) for i in range(count - 1)]
        backward = [(target, source) for source, target in forward]
        low = lax.ppermute(
            lax.slice_in_dim(block, block.shape[dim] - width, None, axis=dim), axis, forward
        )
        high = lax.ppermute(lax.slice_in_dim(block, 0, width, axis=dim), axis, backward)
        block = jnp.concatenate([low, block, high], axis=dim)
    return block


def minmod(first_diff, second_diff):
    return (
        0.5
        * (jnp.sign(first_diff) + jnp.sign(second_diff))
        * jnp.minimum(jnp.abs(first_diff), jnp.abs(second_diff))
    )


def face_flux(courant, far_back, near_back, near_ahead, far_ahead, open_face):
    positive = courant > 0.0
    upwind = jnp.where(positive, near_back, near_ahead)
    side_diff = jnp.where(positive, near_back - far_back, far_ahead - near_ahead)
    limited = minmod(near_ahead - near_back, side_diff)
    magnitude = jnp.abs(courant)
    return (courant * upwind + 0.5 * magnitude * (1.0 - magnitude) * limited) * open_face


def advect(salinity, east_courant, eastern_face_open, north_courant, wet_cells):
    columns = salinity.shape[2]
    east_flux = face_flux(
        east_courant,
        salinity[:, :, 0 : columns - 3],
        salinity[:, :, 1 : columns - 2],
        salinity[:, :, 2 : columns - 1],
        salinity[:, :, 3:columns],
        eastern_face_open,
    )
    interior = salinity[:, :, 2 : columns - 2]
    zero_col = jnp.zeros_like(interior[..., :1])
    lower_cells = jnp.concatenate([zero_col, interior[..., :-1]], -1)
    upper_cells = jnp.concatenate([interior[..., 1:], zero_col], -1)
    upper_two = jnp.concatenate([interior[..., 2:], zero_col, zero_col], -1)
    wet_next = jnp.concatenate([wet_cells[:, 1:], jnp.zeros_like(wet_cells[:, :1])], -1)
    poleward_transport = face_flux(
        north_courant, lower_cells, interior, upper_cells, upper_two, wet_cells * wet_next
    )
    equatorward_transport = jnp.concatenate([zero_col, poleward_transport[..., :-1]], -1)
    return (
        interior
        - (east_flux[:, :, 1:] - east_flux[:, :, :-1])
        - (poleward_transport - equatorward_transport)
    )


def factor(diff_rates):
    levels = diff_rates.shape[1] + 1
    thomas_coefficients = []
    inverse_terms = []
    previous = None
    for level_index in range(levels):
        diagonal = jnp.ones_like(diff_rates[:, 0])
        if level_index > 0:
            diagonal = diagonal + diff_rates[:, level_index - 1]
        if level_index < levels - 1:
            diagonal = diagonal + diff_rates[:, level_index]
        if level_index > 0:
            diagonal = diagonal + diff_rates[:, level_index - 1] * previous
        inverse_den = 1.0 / diagonal
        inverse_terms.append(inverse_den)
        if level_index < levels - 1:
            previous = -diff_rates[:, level_index] * inverse_den
            thomas_coefficients.append(previous)
    return (diff_rates, thomas_coefficients, inverse_terms)


def solve_columns(values, tridiag_terms):
    diff_rates, thomas_coefficients, inverse_terms = tridiag_terms
    levels = values.shape[1]
    forward = [values[:, 0] * inverse_terms[0]]
    for level_index in range(1, levels):
        forward.append(
            (values[:, level_index] + diff_rates[:, level_index - 1] * forward[-1])
            * inverse_terms[level_index]
        )
    solution = [None] * levels
    solution[levels - 1] = forward[levels - 1]
    for level_index in range(levels - 2, -1, -1):
        solution[level_index] = (
            forward[level_index] - thomas_coefficients[level_index] * solution[level_index + 1]
        )
    return jnp.stack(solution, 1)


def per_device(members, control, u_courant, v_courant, diffusion, group_scale, group_of, wet):
    levels = members.shape[1]
    columns = members.shape[2]
    realisation_total = members.shape[0] * lax.axis_size("mem")
    group_ids = jnp.arange(group_scale.shape[0], dtype=jnp.int32)
    spread_multiplier = jnp.sum(
        jnp.where(group_of[:, None] == group_ids[None, :], group_scale[None, :], 0.0), 1
    )
    wet_float = wet.astype(jnp.float32)
    recentre_shift, u_low, wet_low, wet_high = member_allreduce(members, u_courant, wet, control)
    salinity = members + recentre_shift[None]
    east_courant = jnp.concatenate([u_low[:, None], u_courant], 1)
    wet_ext = jnp.concatenate([wet_low, wet, wet_high], 0).astype(jnp.float32)
    eastern_face_open = wet_ext[0 : columns + 1] * wet_ext[1 : columns + 2]
    tridiag_terms = factor(spread_multiplier[:, None, None, None] * diffusion[None])
    for time_step_index in range(2):
        padded = with_halo(salinity, (("tile", 2),), 2)
        salinity = solve_columns(
            advect(padded, east_courant, eastern_face_open, v_courant, wet_float), tridiag_terms
        )
    return salinity


def solution(mesh):
    placed = (
        P("mem", None, "tile", None),
        P(None, "tile", None),
        P(None, "tile", None),
        P(None, "tile", None),
        P(None, "tile", None),
        P(),
        P("mem"),
        P("tile", None),
    )
    return jax.shard_map(
        per_device,
        mesh=mesh,
        in_specs=placed,
        out_specs=P("mem", None, "tile", None),
        check_vma=False,
    )
```

```python
import functools

import jax
import jax.numpy as jnp
from jax import lax
from jax.experimental import pallas as pl
from jax.experimental.pallas import tpu as pltpu
from jax.sharding import PartitionSpec as P

MESH_ID = pl.DeviceIdType.MESH


def allreduce_kernel(
    n, members_ref, u_ref, wet_ref, c_ref, o_ref, ulow_ref, wlow_ref, whigh_ref,
    x_ref, recv, red, gath, uedge, wedge, ubuf, wbuf, s1, r1, s2, r2, se, re, s1b, r1b, s2b, r2b,
):
    me = lax.axis_index("mem")
    tile = lax.axis_index("tile")
    tiles = lax.axis_size("tile")
    has_left = tile > 0
    has_right = tile < tiles - 1
    rows = x_ref.shape[0] // n
    columns = u_ref.shape[1]
    half = n // 2
    ring_y, ring_z = me // 2, lax.rem(me, 2)
    offsets = [(2, 1), (2, 0), (1, 1), (3, 1), (1, 0), (3, 0), (0, 1)]
    peers = [lax.rem(ring_y + dy, half) * 2 + lax.rem(ring_z + dz, 2) for dy, dz in offsets]
    barrier = pltpu.get_barrier_semaphore()
    for peer in peers:
        pl.semaphore_signal(barrier, inc=1, device_id=(tile, peer), device_id_type=MESH_ID)

    @pl.when(has_left)
    def _():
        pl.semaphore_signal(barrier, inc=1, device_id=(tile - 1, me), device_id_type=MESH_ID)

    @pl.when(has_right)
    def _():
        pl.semaphore_signal(barrier, inc=1, device_id=(tile + 1, me), device_id_type=MESH_ID)

    uedge[...] = u_ref[:, columns - 1, :]
    wedge[0] = wet_ref[pl.ds(columns - 1, 1), :]
    wedge[1] = wet_ref[pl.ds(0, 1), :]

    def local_sum(k, carry):
        level = members_ref[0, k]
        for m in range(1, members_ref.shape[0]):
            level = level + members_ref[m, k]
        x_ref[k] = level
        return carry

    lax.fori_loop(0, x_ref.shape[0], local_sum, 0, unroll=4)
    pl.semaphore_wait(
        barrier, n - 1 + has_left.astype(jnp.int32) + has_right.astype(jnp.int32)
    )

    def copy_to(src, dst, send, recv_sem, device):
        return pltpu.make_async_remote_copy(
            src_ref=src,
            dst_ref=dst,
            send_sem=send,
            recv_sem=recv_sem,
            device_id=device,
            device_id_type=MESH_ID,
        )

    right_copies = [
        copy_to(uedge, ubuf, se.at[0], re.at[0], (tile + 1, me)),
        copy_to(wedge.at[0], wbuf.at[0], se.at[1], re.at[1], (tile + 1, me)),
    ]
    left_copy = copy_to(wedge.at[1], wbuf.at[1], se.at[2], re.at[2], (tile - 1, me))

    @pl.when(has_right)
    def _():
        for copy in right_copies:
            copy.start()

    @pl.when(has_left)
    def _():
        left_copy.start()

    split = rows // 2
    scale = 1.0 / (n * members_ref.shape[0])
    sems = [(s1, r1, s2, r2), (s1b, r1b, s2b, r2b)]
    firsts = []
    for part, (sa, ra, _, _) in enumerate(sems):
        lo = part * split
        for peer in peers:
            firsts.append(copy_to(
                x_ref.at[pl.ds(peer * rows + lo, split)], recv.at[me, pl.ds(lo, split)],
                sa.at[peer], ra.at[me], (tile, peer),
            ))
    for copy in firsts:
        copy.start()
    seconds = []
    for part, (sa, ra, sb, rb) in enumerate(sems):
        lo = part * split
        for peer in peers:
            copy_to(
                x_ref.at[pl.ds(lo, split)], recv.at[peer, pl.ds(lo, split)],
                sa.at[peer], ra.at[peer], (tile, peer),
            ).wait_recv()
        acc = x_ref[pl.ds(me * rows + lo, split)]
        for peer in peers:
            acc = acc + recv[peer, pl.ds(lo, split)]
        red[pl.ds(lo, split)] = acc
        own = pl.ds(me * rows + lo, split)
        o_ref[own] = c_ref[own] - acc * scale
        batch = [
            copy_to(red.at[pl.ds(lo, split)], gath.at[me, pl.ds(lo, split)], sb.at[peer], rb.at[me], (tile, peer))
            for peer in peers
        ]
        for copy in batch:
            copy.start()
        seconds += batch
    for part, (_, _, sb, rb) in enumerate(sems):
        lo = part * split
        for peer in peers:
            copy_to(
                red.at[pl.ds(lo, split)], gath.at[peer, pl.ds(lo, split)],
                sb.at[peer], rb.at[peer], (tile, peer),
            ).wait_recv()
            rows_here = pl.ds(peer * rows + lo, split)
            o_ref[rows_here] = c_ref[rows_here] - gath[peer, pl.ds(lo, split)] * scale
    for copy in firsts + seconds:
        copy.wait_send()

    @pl.when(has_right)
    def _():
        for copy in right_copies:
            copy.wait_send()

    @pl.when(has_left)
    def _():
        left_copy.wait_send()
        for copy in right_copies:
            copy.wait_recv()
        ulow_ref[...] = ubuf[...]
        wlow_ref[...] = wbuf[0]

    @pl.when(jnp.logical_not(has_left))
    def _():
        ulow_ref[...] = jnp.zeros_like(ulow_ref)
        wlow_ref[...] = jnp.zeros_like(wlow_ref)

    @pl.when(has_right)
    def _():
        left_copy.wait_recv()
        whigh_ref[...] = wbuf[1]

    @pl.when(jnp.logical_not(has_right))
    def _():
        whigh_ref[...] = jnp.zeros_like(whigh_ref)


def member_allreduce(members, u_courant, wet, control):
    total = jax.ShapeDtypeStruct(members.shape[1:], members.dtype)
    n = lax.axis_size("mem")
    rows = total.shape[0] // n
    chunk = (rows,) + total.shape[1:]
    levels, lanes = u_courant.shape[0], u_courant.shape[2]
    vmem = pl.BlockSpec(memory_space=pltpu.VMEM)
    return pl.pallas_call(
        functools.partial(allreduce_kernel, n),
        out_shape=(
            jax.ShapeDtypeStruct(total.shape, total.dtype),
            jax.ShapeDtypeStruct((levels, lanes), u_courant.dtype),
            jax.ShapeDtypeStruct((1, lanes), wet.dtype),
            jax.ShapeDtypeStruct((1, lanes), wet.dtype),
        ),
        in_specs=[vmem] * 4,
        out_specs=(vmem,) * 4,
        scratch_shapes=[
            pltpu.VMEM(total.shape, total.dtype),
            pltpu.VMEM((n,) + chunk, total.dtype),
            pltpu.VMEM(chunk, total.dtype),
            pltpu.VMEM((n,) + chunk, total.dtype),
            pltpu.VMEM((levels, lanes), u_courant.dtype),
            pltpu.VMEM((2, 1, lanes), wet.dtype),
            pltpu.VMEM((levels, lanes), u_courant.dtype),
            pltpu.VMEM((2, 1, lanes), wet.dtype),
            pltpu.SemaphoreType.DMA((n,)),
            pltpu.SemaphoreType.DMA((n,)),
            pltpu.SemaphoreType.DMA((n,)),
            pltpu.SemaphoreType.DMA((n,)),
            pltpu.SemaphoreType.DMA((3,)),
            pltpu.SemaphoreType.DMA((3,)),
            pltpu.SemaphoreType.DMA((n,)),
            pltpu.SemaphoreType.DMA((n,)),
            pltpu.SemaphoreType.DMA((n,)),
            pltpu.SemaphoreType.DMA((n,)),
        ],
        compiler_params=pltpu.CompilerParams(collective_id=0, has_side_effects=True),
    )(members, u_courant, wet, control)


def with_halo(block, sides, width):
    for axis, dim in sides:
        count = lax.axis_size(axis)
        forward = [(i, i + 1) for i in range(count - 1)]
        backward = [(target, source) for source, target in forward]
        low = lax.ppermute(
            lax.slice_in_dim(block, block.shape[dim] - width, None, axis=dim), axis, forward
        )
        high = lax.ppermute(lax.slice_in_dim(block, 0, width, axis=dim), axis, backward)
        block = jnp.concatenate([low, block, high], axis=dim)
    return block


def minmod(first_diff, second_diff):
    return (
        0.5
        * (jnp.sign(first_diff) + jnp.sign(second_diff))
        * jnp.minimum(jnp.abs(first_diff), jnp.abs(second_diff))
    )


def face_flux(courant, far_back, near_back, near_ahead, far_ahead, open_face):
    positive = courant > 0.0
    upwind = jnp.where(positive, near_back, near_ahead)
    side_diff = jnp.where(positive, near_back - far_back, far_ahead - near_ahead)
    limited = minmod(near_ahead - near_back, side_diff)
    magnitude = jnp.abs(courant)
    return (courant * upwind + 0.5 * magnitude * (1.0 - magnitude) * limited) * open_face


def advect(salinity, east_courant, eastern_face_open, north_courant, wet_cells):
    columns = salinity.shape[2]
    east_flux = face_flux(
        east_courant,
        salinity[:, :, 0 : columns - 3],
        salinity[:, :, 1 : columns - 2],
        salinity[:, :, 2 : columns - 1],
        salinity[:, :, 3:columns],
        eastern_face_open,
    )
    interior = salinity[:, :, 2 : columns - 2]
    zero_col = jnp.zeros_like(interior[..., :1])
    lower_cells = jnp.concatenate([zero_col, interior[..., :-1]], -1)
    upper_cells = jnp.concatenate([interior[..., 1:], zero_col], -1)
    upper_two = jnp.concatenate([interior[..., 2:], zero_col, zero_col], -1)
    wet_next = jnp.concatenate([wet_cells[:, 1:], jnp.zeros_like(wet_cells[:, :1])], -1)
    poleward_transport = face_flux(
        north_courant, lower_cells, interior, upper_cells, upper_two, wet_cells * wet_next
    )
    equatorward_transport = jnp.concatenate([zero_col, poleward_transport[..., :-1]], -1)
    return (
        interior
        - (east_flux[:, :, 1:] - east_flux[:, :, :-1])
        - (poleward_transport - equatorward_transport)
    )


def factor(diff_rates):
    levels = diff_rates.shape[1] + 1
    thomas_coefficients = []
    inverse_terms = []
    previous = None
    for level_index in range(levels):
        diagonal = jnp.ones_like(diff_rates[:, 0])
        if level_index > 0:
            diagonal = diagonal + diff_rates[:, level_index - 1]
        if level_index < levels - 1:
            diagonal = diagonal + diff_rates[:, level_index]
        if level_index > 0:
            diagonal = diagonal + diff_rates[:, level_index - 1] * previous
        inverse_den = 1.0 / diagonal
        inverse_terms.append(inverse_den)
        if level_index < levels - 1:
            previous = -diff_rates[:, level_index] * inverse_den
            thomas_coefficients.append(previous)
    return (diff_rates, thomas_coefficients, inverse_terms)


def solve_columns(values, tridiag_terms):
    diff_rates, thomas_coefficients, inverse_terms = tridiag_terms
    levels = values.shape[1]
    forward = [values[:, 0] * inverse_terms[0]]
    for level_index in range(1, levels):
        forward.append(
            (values[:, level_index] + diff_rates[:, level_index - 1] * forward[-1])
            * inverse_terms[level_index]
        )
    solution = [None] * levels
    solution[levels - 1] = forward[levels - 1]
    for level_index in range(levels - 2, -1, -1):
        solution[level_index] = (
            forward[level_index] - thomas_coefficients[level_index] * solution[level_index + 1]
        )
    return jnp.stack(solution, 1)


def per_device(members, control, u_courant, v_courant, diffusion, group_scale, group_of, wet):
    levels = members.shape[1]
    columns = members.shape[2]
    realisation_total = members.shape[0] * lax.axis_size("mem")
    group_ids = jnp.arange(group_scale.shape[0], dtype=jnp.int32)
    spread_multiplier = jnp.sum(
        jnp.where(group_of[:, None] == group_ids[None, :], group_scale[None, :], 0.0), 1
    )
    wet_float = wet.astype(jnp.float32)
    recentre_shift, u_low, wet_low, wet_high = member_allreduce(members, u_courant, wet, control)
    salinity = members + recentre_shift[None]
    east_courant = jnp.concatenate([u_low[:, None], u_courant], 1)
    wet_ext = jnp.concatenate([wet_low, wet, wet_high], 0).astype(jnp.float32)
    eastern_face_open = wet_ext[0 : columns + 1] * wet_ext[1 : columns + 2]
    tridiag_terms = factor(spread_multiplier[:, None, None, None] * diffusion[None])
    for time_step_index in range(2):
        padded = with_halo(salinity, (("tile", 2),), 2)
        salinity = solve_columns(
            advect(padded, east_courant, eastern_face_open, v_courant, wet_float), tridiag_terms
        )
    return salinity


def solution(mesh):
    placed = (
        P("mem", None, "tile", None),
        P(None, "tile", None),
        P(None, "tile", None),
        P(None, "tile", None),
        P(None, "tile", None),
        P(),
        P("mem"),
        P("tile", None),
    )
    return jax.shard_map(
        per_device,
        mesh=mesh,
        in_specs=placed,
        out_specs=P("mem", None, "tile", None),
        check_vma=False,
    )
```

```python
import functools

import jax
import jax.numpy as jnp
from jax import lax
from jax.experimental import pallas as pl
from jax.experimental.pallas import tpu as pltpu
from jax.sharding import PartitionSpec as P

MESH_ID = pl.DeviceIdType.MESH


def allreduce_kernel(
    n, members_ref, u_ref, wet_ref, c_ref, o_ref, ulow_ref, wlow_ref, whigh_ref,
    x_ref, recv, red, gath, uedge, wedge, ubuf, wbuf, s1, r1, s2, r2, se, re, s1b, r1b, s2b, r2b,
):
    me = lax.axis_index("mem")
    tile = lax.axis_index("tile")
    tiles = lax.axis_size("tile")
    has_left = tile > 0
    has_right = tile < tiles - 1
    rows = x_ref.shape[0] // n
    columns = u_ref.shape[1]
    half = n // 2
    ring_y, ring_z = me // 2, lax.rem(me, 2)
    offsets = [(2, 1), (2, 0), (1, 1), (3, 1), (1, 0), (3, 0), (0, 1)]
    peers = [lax.rem(ring_y + dy, half) * 2 + lax.rem(ring_z + dz, 2) for dy, dz in offsets]
    barrier = pltpu.get_barrier_semaphore()
    for peer in peers:
        pl.semaphore_signal(barrier, inc=1, device_id=(tile, peer), device_id_type=MESH_ID)

    @pl.when(has_left)
    def _():
        pl.semaphore_signal(barrier, inc=1, device_id=(tile - 1, me), device_id_type=MESH_ID)

    @pl.when(has_right)
    def _():
        pl.semaphore_signal(barrier, inc=1, device_id=(tile + 1, me), device_id_type=MESH_ID)

    uedge[...] = u_ref[:, columns - 1, :]
    wedge[0] = wet_ref[pl.ds(columns - 1, 1), :]
    wedge[1] = wet_ref[pl.ds(0, 1), :]

    def local_sum(k, carry):
        level = members_ref[0, k]
        for m in range(1, members_ref.shape[0]):
            level = level + members_ref[m, k]
        x_ref[k] = level
        return carry

    lax.fori_loop(0, x_ref.shape[0], local_sum, 0)
    pl.semaphore_wait(
        barrier, n - 1 + has_left.astype(jnp.int32) + has_right.astype(jnp.int32)
    )

    def copy_to(src, dst, send, recv_sem, device):
        return pltpu.make_async_remote_copy(
            src_ref=src,
            dst_ref=dst,
            send_sem=send,
            recv_sem=recv_sem,
            device_id=device,
            device_id_type=MESH_ID,
        )

    right_copies = [
        copy_to(uedge, ubuf, se.at[0], re.at[0], (tile + 1, me)),
        copy_to(wedge.at[0], wbuf.at[0], se.at[1], re.at[1], (tile + 1, me)),
    ]
    left_copy = copy_to(wedge.at[1], wbuf.at[1], se.at[2], re.at[2], (tile - 1, me))

    split = rows // 2
    scale = 1.0 / (n * members_ref.shape[0])
    sems = [(s1, r1, s2, r2), (s1b, r1b, s2b, r2b)]
    firsts = []
    for part, (sa, ra, _, _) in enumerate(sems):
        lo = part * split
        for peer in peers:
            firsts.append(copy_to(
                x_ref.at[pl.ds(peer * rows + lo, split)], recv.at[me, pl.ds(lo, split)],
                sa.at[peer], ra.at[me], (tile, peer),
            ))
    for copy in firsts:
        copy.start()

    @pl.when(has_right)
    def _():
        for copy in right_copies:
            copy.start()

    @pl.when(has_left)
    def _():
        left_copy.start()

    seconds = []
    for part, (sa, ra, sb, rb) in enumerate(sems):
        lo = part * split
        for peer in peers:
            copy_to(
                x_ref.at[pl.ds(lo, split)], recv.at[peer, pl.ds(lo, split)],
                sa.at[peer], ra.at[peer], (tile, peer),
            ).wait_recv()
        acc = x_ref[pl.ds(me * rows + lo, split)]
        for peer in peers:
            acc = acc + recv[peer, pl.ds(lo, split)]
        red[pl.ds(lo, split)] = acc
        own = pl.ds(me * rows + lo, split)
        o_ref[own] = c_ref[own] - acc * scale
        batch = [
            copy_to(red.at[pl.ds(lo, split)], gath.at[me, pl.ds(lo, split)], sb.at[peer], rb.at[me], (tile, peer))
            for peer in peers
        ]
        for copy in batch:
            copy.start()
        seconds += batch
    for part, (_, _, sb, rb) in enumerate(sems):
        lo = part * split
        for peer in peers:
            copy_to(
                red.at[pl.ds(lo, split)], gath.at[peer, pl.ds(lo, split)],
                sb.at[peer], rb.at[peer], (tile, peer),
            ).wait_recv()
            rows_here = pl.ds(peer * rows + lo, split)
            o_ref[rows_here] = c_ref[rows_here] - gath[peer, pl.ds(lo, split)] * scale
    for copy in firsts + seconds:
        copy.wait_send()

    @pl.when(has_right)
    def _():
        for copy in right_copies:
            copy.wait_send()

    @pl.when(has_left)
    def _():
        left_copy.wait_send()
        for copy in right_copies:
            copy.wait_recv()
        ulow_ref[...] = ubuf[...]
        wlow_ref[...] = wbuf[0]

    @pl.when(jnp.logical_not(has_left))
    def _():
        ulow_ref[...] = jnp.zeros_like(ulow_ref)
        wlow_ref[...] = jnp.zeros_like(wlow_ref)

    @pl.when(has_right)
    def _():
        left_copy.wait_recv()
        whigh_ref[...] = wbuf[1]

    @pl.when(jnp.logical_not(has_right))
    def _():
        whigh_ref[...] = jnp.zeros_like(whigh_ref)


def member_allreduce(members, u_courant, wet, control):
    total = jax.ShapeDtypeStruct(members.shape[1:], members.dtype)
    n = lax.axis_size("mem")
    rows = total.shape[0] // n
    chunk = (rows,) + total.shape[1:]
    levels, lanes = u_courant.shape[0], u_courant.shape[2]
    vmem = pl.BlockSpec(memory_space=pltpu.VMEM)
    return pl.pallas_call(
        functools.partial(allreduce_kernel, n),
        out_shape=(
            jax.ShapeDtypeStruct(total.shape, total.dtype),
            jax.ShapeDtypeStruct((levels, lanes), u_courant.dtype),
            jax.ShapeDtypeStruct((1, lanes), wet.dtype),
            jax.ShapeDtypeStruct((1, lanes), wet.dtype),
        ),
        in_specs=[vmem] * 4,
        out_specs=(vmem,) * 4,
        scratch_shapes=[
            pltpu.VMEM(total.shape, total.dtype),
            pltpu.VMEM((n,) + chunk, total.dtype),
            pltpu.VMEM(chunk, total.dtype),
            pltpu.VMEM((n,) + chunk, total.dtype),
            pltpu.VMEM((levels, lanes), u_courant.dtype),
            pltpu.VMEM((2, 1, lanes), wet.dtype),
            pltpu.VMEM((levels, lanes), u_courant.dtype),
            pltpu.VMEM((2, 1, lanes), wet.dtype),
            pltpu.SemaphoreType.DMA((n,)),
            pltpu.SemaphoreType.DMA((n,)),
            pltpu.SemaphoreType.DMA((n,)),
            pltpu.SemaphoreType.DMA((n,)),
            pltpu.SemaphoreType.DMA((3,)),
            pltpu.SemaphoreType.DMA((3,)),
            pltpu.SemaphoreType.DMA((n,)),
            pltpu.SemaphoreType.DMA((n,)),
            pltpu.SemaphoreType.DMA((n,)),
            pltpu.SemaphoreType.DMA((n,)),
        ],
        compiler_params=pltpu.CompilerParams(collective_id=0, has_side_effects=True),
    )(members, u_courant, wet, control)


def with_halo(block, sides, width):
    for axis, dim in sides:
        count = lax.axis_size(axis)
        forward = [(i, i + 1) for i in range(count - 1)]
        backward = [(target, source) for source, target in forward]
        low = lax.ppermute(
            lax.slice_in_dim(block, block.shape[dim] - width, None, axis=dim), axis, forward
        )
        high = lax.ppermute(lax.slice_in_dim(block, 0, width, axis=dim), axis, backward)
        block = jnp.concatenate([low, block, high], axis=dim)
    return block


def minmod(first_diff, second_diff):
    return (
        0.5
        * (jnp.sign(first_diff) + jnp.sign(second_diff))
        * jnp.minimum(jnp.abs(first_diff), jnp.abs(second_diff))
    )


def face_flux(courant, far_back, near_back, near_ahead, far_ahead, open_face):
    positive = courant > 0.0
    upwind = jnp.where(positive, near_back, near_ahead)
    side_diff = jnp.where(positive, near_back - far_back, far_ahead - near_ahead)
    limited = minmod(near_ahead - near_back, side_diff)
    magnitude = jnp.abs(courant)
    return (courant * upwind + 0.5 * magnitude * (1.0 - magnitude) * limited) * open_face


def advect(salinity, east_courant, eastern_face_open, north_courant, wet_cells):
    columns = salinity.shape[2]
    east_flux = face_flux(
        east_courant,
        salinity[:, :, 0 : columns - 3],
        salinity[:, :, 1 : columns - 2],
        salinity[:, :, 2 : columns - 1],
        salinity[:, :, 3:columns],
        eastern_face_open,
    )
    interior = salinity[:, :, 2 : columns - 2]
    zero_col = jnp.zeros_like(interior[..., :1])
    lower_cells = jnp.concatenate([zero_col, interior[..., :-1]], -1)
    upper_cells = jnp.concatenate([interior[..., 1:], zero_col], -1)
    upper_two = jnp.concatenate([interior[..., 2:], zero_col, zero_col], -1)
    wet_next = jnp.concatenate([wet_cells[:, 1:], jnp.zeros_like(wet_cells[:, :1])], -1)
    poleward_transport = face_flux(
        north_courant, lower_cells, interior, upper_cells, upper_two, wet_cells * wet_next
    )
    equatorward_transport = jnp.concatenate([zero_col, poleward_transport[..., :-1]], -1)
    return (
        interior
        - (east_flux[:, :, 1:] - east_flux[:, :, :-1])
        - (poleward_transport - equatorward_transport)
    )


def factor(diff_rates):
    levels = diff_rates.shape[1] + 1
    thomas_coefficients = []
    inverse_terms = []
    previous = None
    for level_index in range(levels):
        diagonal = jnp.ones_like(diff_rates[:, 0])
        if level_index > 0:
            diagonal = diagonal + diff_rates[:, level_index - 1]
        if level_index < levels - 1:
            diagonal = diagonal + diff_rates[:, level_index]
        if level_index > 0:
            diagonal = diagonal + diff_rates[:, level_index - 1] * previous
        inverse_den = 1.0 / diagonal
        inverse_terms.append(inverse_den)
        if level_index < levels - 1:
            previous = -diff_rates[:, level_index] * inverse_den
            thomas_coefficients.append(previous)
    return (diff_rates, thomas_coefficients, inverse_terms)


def solve_columns(values, tridiag_terms):
    diff_rates, thomas_coefficients, inverse_terms = tridiag_terms
    levels = values.shape[1]
    forward = [values[:, 0] * inverse_terms[0]]
    for level_index in range(1, levels):
        forward.append(
            (values[:, level_index] + diff_rates[:, level_index - 1] * forward[-1])
            * inverse_terms[level_index]
        )
    solution = [None] * levels
    solution[levels - 1] = forward[levels - 1]
    for level_index in range(levels - 2, -1, -1):
        solution[level_index] = (
            forward[level_index] - thomas_coefficients[level_index] * solution[level_index + 1]
        )
    return jnp.stack(solution, 1)


def per_device(members, control, u_courant, v_courant, diffusion, group_scale, group_of, wet):
    levels = members.shape[1]
    columns = members.shape[2]
    realisation_total = members.shape[0] * lax.axis_size("mem")
    group_ids = jnp.arange(group_scale.shape[0], dtype=jnp.int32)
    spread_multiplier = jnp.sum(
        jnp.where(group_of[:, None] == group_ids[None, :], group_scale[None, :], 0.0), 1
    )
    wet_float = wet.astype(jnp.float32)
    recentre_shift, u_low, wet_low, wet_high = member_allreduce(members, u_courant, wet, control)
    salinity = members + recentre_shift[None]
    east_courant = jnp.concatenate([u_low[:, None], u_courant], 1)
    wet_ext = jnp.concatenate([wet_low, wet, wet_high], 0).astype(jnp.float32)
    eastern_face_open = wet_ext[0 : columns + 1] * wet_ext[1 : columns + 2]
    tridiag_terms = factor(spread_multiplier[:, None, None, None] * diffusion[None])
    for time_step_index in range(2):
        padded = with_halo(salinity, (("tile", 2),), 2)
        salinity = solve_columns(
            advect(padded, east_courant, eastern_face_open, v_courant, wet_float), tridiag_terms
        )
    return salinity


def solution(mesh):
    placed = (
        P("mem", None, "tile", None),
        P(None, "tile", None),
        P(None, "tile", None),
        P(None, "tile", None),
        P(None, "tile", None),
        P(),
        P("mem"),
        P("tile", None),
    )
    return jax.shard_map(
        per_device,
        mesh=mesh,
        in_specs=placed,
        out_specs=P("mem", None, "tile", None),
        check_vma=False,
    )
```
